256 devices in a mesh: tiles: 64 (over z, y, core), chan: 4 (over x).
Axes of the slice: x: 4, y: 4, z: 8, core: 2. Of those that a mesh axis runs over, the one named last changes fastest.
Arguments:
- x_scan: bfloat16 [1024, 192, 256], P('tiles', 'chan'), may hold values from -40 to 40
- slot_owner: int32 [1024], P('tiles'), may hold values from 0 to 512, as said below
- adjacency: int32 [512, 8], P('tiles'), may hold values from 0 to 512, as said below
- cotangent: bfloat16 [512, 192, 256], P('tiles', 'chan'), may hold values from -6 to 6
- dw_weight: float32 [192, 49], P('chan'), may hold values from -0.875 to 0.875
- ln_gain: bfloat16 [192], P('chan'), may hold values from 0.25 to 1.75
- w_in: bfloat16 [192, 768], P(None, 'chan'), may hold values from -0.4375 to 0.4375
- b_in: bfloat16 [768], P('chan'), may hold values from -3 to 3
- w_out: bfloat16 [768, 192], P('chan'), may hold values from -0.21875 to 0.21875
- layer_scale: float32 [192], P('chan'), may hold values from 0.3 to 1.5
Outputs:
- output: bfloat16 [512, 192, 256], P('tiles', 'chan')
- grad_in: bfloat16 [512, 192, 256], P('tiles', 'chan')
- grad_dw: float32 [192, 49], P('chan')
- grad_w1: float32 [192, 768], P(None, 'chan')
- grad_w2: float32 [768, 192], P('chan')
The draws below stay inside these ranges and needn't reach their ends.
Inputs may be any that keep to these rules, and one draw needn't show every extreme that they name: `slot_owner`: slots run in scan order over a grid of tiles with 16 columns, one grid row for each device along tiles. A tissue slot holds its tile's owner-order index, a background slot holds 512. Tissue tiles are numbered in scan order, and owner-order index q belongs to device q // 8. Grid rows 2k and 2k + 1 hold 4 to 12 tissue tiles each and 16 together, so a device's tissue tiles belong to it or to the device whose index differs in the lowest bit, and at most 4 of them, a number reached in every draw, to the latter. `adjacency`: entry k of a tissue tile is the owner-order index of the grid cell at row and column offsets (-1,-1), (-1,0), (-1,1), (0,-1), (0,1), (1,-1), (1,0), (1,1) from it, 512 where that cell is background or off the grid. Every neighbour of a tile owned by device o is owned by one of the devices o - 3 to o + 3, a distance reached in every draw.
All inputs are finite; a program needn't handle non-finite values.
Results may differ from the reference program's by a relative error of at most 0.015.
Values may be sent and summed in bfloat16 or wider, within the bound.
No kernel may reach another device: no remote copies, remote signals or barrier semaphores. Data moves between devices by JAX's collectives and lax.ppermute only.
A program may use at most 128 MiB of HBM per device.

```python
import math
import jax
import jax.numpy as jnp
from jax import lax

CHANNEL_COUNT = 192
HID = 768
P_SIZE = 16
TILE_DEV = 8
PIX = 256
HID_DEV = 192
TILES = 512
SLOTS = 1024


def tissue_layout(key):
    grid_rows = TILES // TILE_DEV
    grid_cols = 2 * TILE_DEV
    half_dev = TILE_DEV // 2
    pair_count = grid_rows // 2
    offsets = jax.random.randint(jax.random.fold_in(key, 1), (pair_count,), -half_dev, half_dev + 1)
    offsets = offsets.at[0].set(-half_dev).at[1].set(half_dev)
    counts = jnp.stack([TILE_DEV + offsets, TILE_DEV - offsets], axis=1).reshape(grid_rows)
    row_keys = jax.random.split(jax.random.fold_in(key, 2), grid_rows)

    def shuffled(row_key):
        return jax.random.permutation(row_key, grid_cols)
    orders = jax.vmap(shuffled)(row_keys)
    tissue = orders < counts[:, None]
    column_ids = jnp.arange(grid_cols)
    tissue = tissue.at[1].set(column_ids >= half_dev).at[2].set(column_ids < grid_cols - half_dev)
    flags = tissue.reshape(-1).astype(jnp.int32)
    ranks = jnp.cumsum(flags) - flags
    owners = jnp.where(flags > 0, ranks, TILES).astype(jnp.int32)
    owner_grid = jnp.pad(owners.reshape(grid_rows, grid_cols), 1, constant_values=TILES)
    neighbours = []
    for row_step in (-1, 0, 1):
        for col_step in (-1, 0, 1):
            if row_step != 0 or col_step != 0:
                neighbours.append(owner_grid[1 + row_step:1 + row_step + grid_rows, 1 + col_step:1 + col_step + grid_cols].reshape(-1))
    neighbour_table = jnp.stack(neighbours, axis=1).astype(jnp.int32)
    adjacency = jnp.full((TILES, 8), TILES, jnp.int32).at[owners].set(neighbour_table, mode='drop')
    return (owners, adjacency)


def draw_slot_owner(key, part):
    return tissue_layout(jax.random.fold_in(key, 5))[0]


def draw_adjacency(key, part):
    return tissue_layout(jax.random.fold_in(key, 5))[1]


def draw_x_scan(key, part):
    value_key = jax.random.fold_in(key, 11)
    chan_key = jax.random.fold_in(key, 12)
    tile_key = jax.random.fold_in(key, 13)
    chan_scale = jnp.exp(jax.random.uniform(chan_key, (CHANNEL_COUNT,), jnp.float32, math.log(0.3), math.log(3.0)))
    tile_scale = jnp.exp(jax.random.uniform(tile_key, (SLOTS, 1, 1), jnp.float32, math.log(0.5), math.log(2.0)))
    values = jax.random.truncated_normal(value_key, -4.0, 4.0, (SLOTS, CHANNEL_COUNT, PIX), jnp.float32)
    return (values * chan_scale[None, :, None] * tile_scale).astype(jnp.bfloat16)


def block_scale(stream_key, dims, pieces, low, largest):
    def one(position, blocks):
        steps = jax.random.uniform(jax.random.fold_in(jax.random.fold_in(stream_key, 6), position), (blocks,), jnp.float32, low / len(pieces), largest / len(pieces))
        return jnp.repeat(jnp.exp(steps), dims[position] // blocks).reshape((-1,) + (1,) * (len(dims) - position - 1))

    factor_of = one(*pieces[0])
    for cut in pieces[1:]:
        factor_of = factor_of * one(*cut)
    return factor_of


def scatter_about(key, extent, scale, reach, shards=(), kind=jnp.bfloat16):
    drawn = scale * jax.random.normal(key, extent, jnp.float32)
    if shards:
        drawn = drawn * block_scale(key, extent, shards, -0.22, 0.18)
    return jnp.clip(drawn, -reach, reach).astype(kind)


def setup_inputs(seed: int = 0) -> dict:
    seeds = jax.random.split(jax.random.key(seed), 11)
    return {
        "x_scan": draw_x_scan(jax.random.fold_in(seeds[10], 71), 0),
        "slot_owner": draw_slot_owner(jax.random.fold_in(seeds[10], 71), 0),
        "adjacency": draw_adjacency(jax.random.fold_in(seeds[10], 71), 0),
        "cotangent": scatter_about(seeds[3], (TILES, CHANNEL_COUNT, PIX), 1.0, 6.0, ((0, 64), (1, 4))),
        "dw_weight": scatter_about(seeds[4], (CHANNEL_COUNT, 49), 49 ** -0.5, 0.875, ((0, 4),), jnp.float32),
        "ln_gain": jnp.clip(1.0 + 0.15 * jax.random.normal(seeds[5], (CHANNEL_COUNT,), jnp.float32), 0.25, 1.75).astype(jnp.bfloat16),
        "w_in": scatter_about(seeds[6], (CHANNEL_COUNT, HID), CHANNEL_COUNT ** -0.5, 0.4375, ((1, 4),)),
        "b_in": scatter_about(seeds[7], (HID,), 0.5, 3.0, ((0, 4),)),
        "w_out": scatter_about(seeds[8], (HID, CHANNEL_COUNT), HID ** -0.5, 0.21875, ((0, 4),)),
        "layer_scale": jnp.clip(jnp.exp(math.log(1.5) - 1.60943787 * jax.random.uniform(seeds[9], (CHANNEL_COUNT,), jnp.float32) ** block_scale(seeds[9], (CHANNEL_COUNT,), ((0, 4),), -0.2, 0.2)), 0.3, 1.5),
    }


EPSILON = 1e-06
GELU_SCALE = 0.7978845608
GELU_CUBIC = 0.044715

def strips(tile_field):
    side_len = tile_field.shape[-1]
    top_rows = tile_field[:, :, :3, :]
    bottom_rows = tile_field[:, :, side_len - 3:, :]
    left_cols = jnp.swapaxes(tile_field[:, :, :, :3], 2, 3)
    right_cols = jnp.swapaxes(tile_field[:, :, :, side_len - 3:], 2, 3)
    return jnp.stack([top_rows, bottom_rows, left_cols, right_cols], axis=2)

def assemble(tile_field, around):
    side_len = tile_field.shape[-1]
    upper_band = jnp.concatenate([around[:, 0, :, 1, :, side_len - 3:], around[:, 1, :, 1], around[:, 2, :, 1, :, :3]], axis=3)
    middle = jnp.concatenate([jnp.swapaxes(around[:, 3, :, 3], 2, 3), tile_field, jnp.swapaxes(around[:, 4, :, 2], 2, 3)], axis=3)
    lower_band = jnp.concatenate([around[:, 5, :, 0, :, side_len - 3:], around[:, 6, :, 0], around[:, 7, :, 0, :, :3]], axis=3)
    return jnp.concatenate([upper_band, middle, lower_band], axis=2)

def depthwise(padded, kernel):
    tile_count = padded.shape[0]
    channels = padded.shape[1]
    wide_len = padded.shape[3]
    side_len = wide_len - 6
    span_len = side_len * wide_len
    flat_pad = jnp.pad(padded.astype(jnp.float32).reshape(tile_count, channels, wide_len * wide_len), ((0, 0), (0, 0), (0, 8)))
    result = jnp.zeros((tile_count, channels, span_len), jnp.float32)
    for row_tap in range(7):
        for col_tap in range(7):
            offset = row_tap * wide_len + col_tap
            result = result + kernel[:, row_tap * 7 + col_tap][None, :, None] * flat_pad[:, :, offset:offset + span_len]
    return result.reshape(tile_count, channels, side_len, wide_len)[:, :, :, :side_len]

def kernel_grad(grad_tiles, padded):
    tile_count = grad_tiles.shape[0]
    channels = grad_tiles.shape[1]
    side_len = grad_tiles.shape[3]
    wide_len = side_len + 6
    span_len = side_len * wide_len
    flat_pad = jnp.pad(padded.astype(jnp.float32).reshape(tile_count, channels, wide_len * wide_len), ((0, 0), (0, 0), (0, 8)))
    spread = jnp.pad(grad_tiles.astype(jnp.float32), ((0, 0), (0, 0), (0, 0), (0, 6))).reshape(tile_count, channels, span_len)
    columns = []
    for row_tap in range(7):
        for col_tap in range(7):
            offset = row_tap * wide_len + col_tap
            columns.append(lax.optimization_barrier(jnp.sum(spread * flat_pad[:, :, offset:offset + span_len], axis=(0, 2))))
    return jnp.stack(columns, axis=1)

def gelu_parts(preact):
    tanh_arg = GELU_SCALE * (preact + GELU_CUBIC * preact * preact * preact)
    tangent = jnp.tanh(tanh_arg)
    values = 0.5 * preact * (1.0 + tangent)
    slopes = 0.5 * (1.0 + tangent) + 0.5 * preact * (1.0 - tangent * tangent) * GELU_SCALE * (1.0 + 3.0 * GELU_CUBIC * preact * preact)
    return (values, slopes)

def lookup(rim_table, neighbours):
    return jnp.take(rim_table, neighbours, axis=0, mode='fill', fill_value=0)

def reference(x_scan, slot_owner, adjacency, cotangent, dw_weight, ln_gain, w_in, b_in, w_out, layer_scale):
    owned_tiles = jnp.zeros((TILES, CHANNEL_COUNT, PIX), jnp.bfloat16).at[slot_owner].set(x_scan, mode='drop')
    tile_field = owned_tiles.reshape(TILES, CHANNEL_COUNT, P_SIZE, P_SIZE)
    rim_table = strips(tile_field)
    gain_float = ln_gain.astype(jnp.float32)
    bias_f = b_in.astype(jnp.float32)
    w_in_f = w_in.astype(jnp.float32)
    w_out_f = w_out.astype(jnp.float32)
    groups = HID // HID_DEV
    scale_col = layer_scale[None, :, None]
    block_ids = jnp.arange(TILES // TILE_DEV, dtype=jnp.int32)

    def forward_block(carry, block_id):
        start = (block_id * TILE_DEV).astype(jnp.int32)
        field_block = lax.dynamic_slice_in_dim(tile_field, start, TILE_DEV, 0)
        adj_block = lax.dynamic_slice_in_dim(adjacency, start, TILE_DEV, 0)
        cot_block = lax.dynamic_slice_in_dim(cotangent, start, TILE_DEV, 0)
        padded = assemble(field_block, lookup(rim_table, adj_block))
        mixed_tiles = depthwise(padded, dw_weight).astype(jnp.bfloat16).reshape(TILE_DEV, CHANNEL_COUNT, PIX)
        mixed_f = mixed_tiles.astype(jnp.float32)
        row_mean = lax.optimization_barrier(jnp.sum(mixed_f, axis=1)) / CHANNEL_COUNT
        inverse_deviation = lax.rsqrt(lax.optimization_barrier(jnp.sum(mixed_f * mixed_f, axis=1)) / CHANNEL_COUNT - row_mean * row_mean + EPSILON)
        centered_input = (mixed_f - row_mean[:, None, :]) * inverse_deviation[:, None, :]
        normed = (centered_input * gain_float[None, :, None]).astype(jnp.bfloat16)
        preact = jnp.einsum('tcp,ch->thp', normed.astype(jnp.float32), w_in_f) + bias_f[None, :, None]
        values, slopes = gelu_parts(preact)
        activated = values.astype(jnp.bfloat16)
        branch_parts = jnp.einsum('tqhp,qhc->tqcp', activated.astype(jnp.float32).reshape(TILE_DEV, groups, HID_DEV, PIX), w_out_f.reshape(groups, HID_DEV, CHANNEL_COUNT))
        branch = lax.optimization_barrier(jnp.sum(lax.optimization_barrier(branch_parts.astype(jnp.bfloat16)).astype(jnp.float32), axis=1)).astype(jnp.bfloat16)
        field_flat = field_block.reshape(TILE_DEV, CHANNEL_COUNT, PIX)
        output = (field_flat.astype(jnp.float32) + scale_col * branch.astype(jnp.float32)).astype(jnp.bfloat16)
        dbranch = (cot_block.astype(jnp.float32) * scale_col).astype(jnp.bfloat16)
        act_grad = jnp.einsum('tcp,hc->thp', dbranch.astype(jnp.float32), w_out_f)
        pre_grad = (act_grad * slopes).astype(jnp.bfloat16)
        part_w2 = jnp.einsum('thp,tcp->hc', activated.astype(jnp.float32), dbranch.astype(jnp.float32))
        part_w1 = jnp.einsum('tcp,thp->ch', normed.astype(jnp.float32), pre_grad.astype(jnp.float32))
        input_parts = jnp.einsum('tqhp,cqh->tqcp', pre_grad.astype(jnp.float32).reshape(TILE_DEV, groups, HID_DEV, PIX), w_in_f.reshape(CHANNEL_COUNT, groups, HID_DEV))
        normed_gradient = lax.optimization_barrier(jnp.sum(lax.optimization_barrier(input_parts.astype(jnp.bfloat16)).astype(jnp.float32), axis=1))
        centered_input_gradient = normed_gradient * gain_float[None, :, None]
        mean_first_moment = lax.optimization_barrier(jnp.sum(centered_input_gradient, axis=1)) / CHANNEL_COUNT
        mean_second_moment = lax.optimization_barrier(jnp.sum(centered_input_gradient * centered_input, axis=1)) / CHANNEL_COUNT
        mixed_gradient = (inverse_deviation[:, None, :] * (centered_input_gradient - mean_first_moment[:, None, :] - centered_input * mean_second_moment[:, None, :])).astype(jnp.bfloat16)
        return ((carry[0] + part_w1, carry[1] + part_w2), (output, mixed_gradient))
    start_sums = (jnp.zeros((CHANNEL_COUNT, HID), jnp.float32), jnp.zeros((HID, CHANNEL_COUNT), jnp.float32))
    raw_sums, stacked = lax.scan(forward_block, start_sums, block_ids)
    output = stacked[0].reshape(TILES, CHANNEL_COUNT, PIX)
    grad_field = stacked[1].reshape(TILES, CHANNEL_COUNT, P_SIZE, P_SIZE)
    grad_rims = strips(grad_field)

    def backward_block(carry, block_id):
        start = (block_id * TILE_DEV).astype(jnp.int32)
        field_block = lax.dynamic_slice_in_dim(tile_field, start, TILE_DEV, 0)
        grad_block = lax.dynamic_slice_in_dim(grad_field, start, TILE_DEV, 0)
        adj_block = lax.dynamic_slice_in_dim(adjacency, start, TILE_DEV, 0)
        cot_block = lax.dynamic_slice_in_dim(cotangent, start, TILE_DEV, 0)
        padded = assemble(field_block, lookup(rim_table, adj_block))
        dpadded = assemble(grad_block, lookup(grad_rims, adj_block))
        backflow = depthwise(dpadded, dw_weight[:, ::-1]).reshape(TILE_DEV, CHANNEL_COUNT, PIX)
        grad_in = (cot_block.astype(jnp.float32) + backflow).astype(jnp.bfloat16)
        return (carry + kernel_grad(grad_block, padded), grad_in)
    raw_dw, grad_blocks = lax.scan(backward_block, jnp.zeros((CHANNEL_COUNT, 49), jnp.float32), block_ids)
    factor = 1.0 / math.sqrt(TILES * PIX)
    return (output, grad_blocks.reshape(TILES, CHANNEL_COUNT, PIX), raw_dw * factor, raw_sums[0] * factor, raw_sums[1] * factor)
```

```python
import functools
import math

import jax
import jax.numpy as jnp
import numpy as np
from jax import lax
from jax.experimental import pallas as pl
from jax.experimental.pallas import tpu as pltpu
from jax.sharding import PartitionSpec as P

CHANNELS = 192
SIDE = 16
PIX = 256
WIDE = 24
EPSILON = 1e-06
GELU_SCALE = 0.7978845608
GELU_CUBIC = 0.044715

F32 = jnp.float32
BF16 = jnp.bfloat16
NT = (((1,), (1,)), ((), ()))
NN = (((1,), (0,)), ((), ()))


def dot(a, b, dims):
    return lax.dot_general(a, b, dims, preferred_element_type=F32)


def placement_tables():
    up = np.zeros((72, 384), np.float32)
    mid = np.zeros((384, 768), np.float32)
    down = np.zeros((72, 384), np.float32)
    for j in range(22):
        if j < 3:
            side, col = 0, 13 + j
        elif j < 19:
            side, col = 1, j - 3
        else:
            side, col = 2, j - 19
        for i in range(3):
            up[i * WIDE + j, 128 * side + 16 * (13 + i) + col - 128] = 1
            down[i * WIDE + j, 128 * side + 16 * i + col] = 1
        for i in range(16):
            block = (1, 0, 2)[side]
            mid[i * WIDE + j, 256 * block + 16 * i + col] = 1
    return up.astype(jnp.bfloat16), mid.astype(jnp.bfloat16), down.astype(jnp.bfloat16)


def column(row):
    n = row.shape[1]
    same = lax.broadcasted_iota(jnp.int32, (n, n), 0) == lax.broadcasted_iota(jnp.int32, (n, n), 1)
    return jnp.sum(jnp.where(same, jnp.broadcast_to(row, (n, n)), 0.0), axis=1, keepdims=True)


def eye(n):
    same = lax.broadcasted_iota(jnp.int32, (n, n), 0) == lax.broadcasted_iota(jnp.int32, (n, n), 1)
    return same.astype(F32).astype(BF16)


def swap_halves(value):
    return pltpu.roll(value.astype(F32), 64, 1)


def low_lanes(shape):
    return lax.broadcasted_iota(jnp.int32, shape, 1) < 64


def pack_pair(natural, other, natural_low):
    shape = natural.shape
    keep = low_lanes(shape) if natural_low else jnp.logical_not(low_lanes(shape))
    return jnp.where(keep, natural.astype(F32), swap_halves(other)).astype(BF16)


def prepare_kernel(x_ref, cot_ref, scale_ref, strips_ref, d0, d1, d2, d3):
    odd = lax.axis_index("tiles") & 1
    mine = lax.axis_index("chan")

    @pl.when(odd == 1)
    def _():
        for s in range(8):
            strips_ref[s] = pack_pair(x_ref[s, :, 128:256], x_ref[s + 8, :, 128:256], False)

    @pl.when(odd == 0)
    def _():
        for s in range(8):
            strips_ref[s] = pack_pair(x_ref[s, :, 0:128], x_ref[s + 8, :, 0:128], True)

    scale = column(scale_ref[...])
    for j, out in enumerate((d0, d1, d2, d3)):
        first = 2 * ((mine + j) & 3)
        for i in range(2):
            out[i] = (cot_ref[first + i].astype(F32) * scale).astype(BF16)


def gather_tile(table, up_g, mid_g, down_g, t, center, entries):
    rows = pl.ds(48 * t, 48)
    mid_g[rows, 0:256] = table[center]
    mid_g[rows, 256:512] = table[entries[3]]
    mid_g[rows, 512:768] = table[entries[4]]
    for k in range(3):
        up_g[rows, 128 * k : 128 * k + 128] = table[entries[k], :, 128:256]
        down_g[rows, 128 * k : 128 * k + 128] = table[entries[5 + k], :, 0:128]


def build_padded(pad, up_g, mid_g, down_g, up_p, mid_p, down_p):
    pad[0:3] = dot(up_p[...], up_g[...], NT).reshape(3, WIDE, 384)
    pad[3:19] = dot(mid_p[...], mid_g[...], NT).reshape(16, WIDE, 384)
    pad[19:22] = dot(down_p[...], down_g[...], NT).reshape(3, WIDE, 384)


def convolve(pad, taps, result, flip):
    def lane_block(block, carry):
        lanes = pl.ds(pl.multiple_of(block * 128, 128), 128)
        acc = [jnp.zeros((16, 128), F32) for _ in range(16)]
        for b in range(7):
            weights = []
            for a in range(7):
                tap = 7 * a + b
                weights.append(taps[pl.ds(48 - tap if flip else tap, 1), lanes])
            for r in range(22):
                line = pad[r, pl.ds(b, 16), lanes]
                for a in range(7):
                    i = r - a
                    if 0 <= i < 16:
                        acc[i] = acc[i] + line * weights[a]
        for i in range(16):
            result[pl.ds(16 * i, 16), lanes] = acc[i]
        return carry

    lax.fori_loop(0, 3, lane_block, 0)


OFFSETS = (-17, -16, -15, -1, 1, 15, 16, 17)


def mix_kernel(
    own_slots, par_slots, adj, x_ref, par_ref, sa_ref, sb_ref, taps, up_p, mid_p, down_p,
    owned_ref, pad_out, m0, m1, m2, m3,
    place, table, up_g, mid_g, down_g, pad, result, flat,
):
    me = lax.axis_index("tiles")
    odd = me & 1
    mine = lax.axis_index("chan")
    base = 8 * me
    for t in range(8):
        place[t] = 0
    for s in range(16):
        for slots, row in ((own_slots, odd), (par_slots, 1 - odd)):
            t = slots[s] - base

            @pl.when((t >= 0) & (t < 8))
            def _():
                place[t] = 16 + 16 * row + s

    table[pl.ds(16 + 16 * odd, 16)] = x_ref[...]
    table[pl.ds(32 - 16 * odd, 16)] = par_ref[...]
    table[64] = jnp.zeros((48, 256), BF16)

    def halo_rows(above, below):
        for s in range(8):
            up = above[s]
            table[s, :, 128:256] = up
            table[s + 8, :, 128:256] = swap_halves(up).astype(BF16)
            down = below[s]
            table[48 + s, :, 0:128] = down
            table[56 + s, :, 0:128] = swap_halves(down).astype(BF16)

    @pl.when(odd == 0)
    def _():
        halo_rows(sa_ref, sb_ref)

    @pl.when(odd == 1)
    def _():
        halo_rows(sb_ref, sa_ref)

    for t in range(8):
        center = place[t]
        entries = [jnp.where(adj[t, k] < 512, center + OFFSETS[k], 64) for k in range(8)]
        gather_tile(table, up_g, mid_g, down_g, t, center, entries)
    owned_ref[...] = mid_g[:, 0:256].reshape(8, 48, 256)
    build_padded(pad, up_g, mid_g, down_g, up_p, mid_p, down_p)
    pad_out[...] = pad[...].astype(BF16)
    convolve(pad, taps, result, False)
    flat[...] = result[...].T.astype(BF16).reshape(8, 48, 256)
    for j, out in enumerate((m0, m1, m2, m3)):
        first = 2 * ((mine + j) & 3)
        out[0] = flat[first]
        out[1] = flat[first + 1]


def weights_kernel(w0, w1, w2, w3, in_t, out_t, bias, gain):
    mine = lax.axis_index("chan")
    unit = eye(192)
    for j, ref in enumerate((w0, w1, w2, w3)):
        in_t[j] = dot(unit, ref[0:192], NT).astype(BF16)
        out_t[j] = dot(unit, ref[192:384], NT).astype(BF16)
        cols = dot(unit, ref[384:400], NT)
        bias[j] = jnp.broadcast_to(cols[:, 0:1], (192, 128))
        gain[(mine + 4 - j) & 3] = jnp.broadcast_to(cols[0:48, 1:2], (48, 128))


def across(col_block):
    return jnp.concatenate([col_block] * 4, axis=1)


def mlp_kernel(
    m0, m1, m2, m3, b0, b1, b2, b3, w0, w1, w2, w3, in_t, out_t, bias, gain,
    g0, g1, g2, g3, r0, r1, r2, r3, v0, v1, v2, v3,
    mixed_s, dbranch_s, back_s, branch_s,
):
    mine = lax.axis_index("chan")
    for j, (m_ref, b_ref) in enumerate(((m0, b0), (m1, b1), (m2, b2), (m3, b3))):
        a = (mine + 4 - j) & 3
        for i in range(2):
            mixed_s[a, :, 256 * i : 256 * i + 256] = m_ref[i]
            dbranch_s[a, :, 256 * i : 256 * i + 256] = b_ref[i]
    mixed = mixed_s[...].reshape(192, 512).astype(F32)
    dbranch = dbranch_s[...].reshape(192, 512)
    mean = jnp.sum(mixed, axis=0, keepdims=True) / CHANNELS
    inv = lax.rsqrt(
        jnp.sum(mixed * mixed, axis=0, keepdims=True) / CHANNELS - mean * mean + EPSILON
    )
    x_hat = (mixed - mean) * inv
    gain_full = across(gain[...].reshape(192, 128))
    normed = (x_hat * gain_full).astype(BF16)
    branch = jnp.zeros((192, 512), F32)
    dnormed = jnp.zeros((192, 512), F32)
    for j, (w_ref, v_ref) in enumerate(((w0, v0), (w1, v1), (w2, v2), (w3, v3))):
        preact = dot(in_t[j], normed, NN) + across(bias[j])
        square = preact * preact
        tangent = jnp.tanh(GELU_SCALE * (preact + GELU_CUBIC * square * preact))
        half = 0.5 * (1.0 + tangent)
        act = (preact * half).astype(BF16)
        slope = half + 0.5 * preact * (1.0 - tangent * tangent) * (
            GELU_SCALE * (1.0 + 3.0 * GELU_CUBIC * square)
        )
        branch = branch + dot(out_t[j], act, NN)
        pre_grad = (dot(w_ref[192:384], dbranch, NN) * slope).astype(BF16)
        dnormed = dnormed + dot(w_ref[0:192], pre_grad, NN)
        v_ref[0:192] = dot(normed, pre_grad, NT).astype(BF16)
        v_ref[192:384] = dot(act, dbranch, NT).astype(BF16)
    xhat_grad = dnormed * gain_full
    first = jnp.sum(xhat_grad, axis=0, keepdims=True) / CHANNELS
    second = jnp.sum(xhat_grad * x_hat, axis=0, keepdims=True) / CHANNELS
    dmixed = (inv * (xhat_grad - first - x_hat * second)).astype(BF16)
    back_s[...] = dmixed.reshape(4, 48, 512)
    branch_s[...] = branch.astype(BF16).reshape(4, 48, 512)
    for j, (g_ref, r_ref) in enumerate(((g0, r0), (g1, r1), (g2, r2), (g3, r3))):
        a = (mine + j) & 3
        for i in range(2):
            g_ref[i] = back_s[a, :, 256 * i : 256 * i + 256]
            r_ref[i] = branch_s[a, :, 256 * i : 256 * i + 256]


def collect_kernel(g0, g1, g2, g3, grad_ref, top_ref, bottom_ref):
    mine = lax.axis_index("chan")
    for j, ref in enumerate((g0, g1, g2, g3)):
        grad_ref[pl.ds(2 * ((mine + 4 - j) & 3), 2)] = ref[...]
    for t in range(4):
        top_ref[t] = pack_pair(grad_ref[t, :, 0:128], grad_ref[t + 4, :, 0:128], True)
        bottom_ref[t] = pack_pair(grad_ref[t, :, 128:256], grad_ref[t + 4, :, 128:256], False)


def taps_kernel(grad_ref, pad_ref, fold, v0, v1, v2, v3, out_ref, pad, grad_t, sums):
    pad[...] = pad_ref[...].astype(F32)
    grad_t[...] = grad_ref[...].reshape(384, 256).astype(F32).T
    sums[...] = jnp.zeros((64, 384), F32)

    def lane_block(block, carry):
        lanes = pl.ds(pl.multiple_of(block * 128, 128), 128)
        lines = [grad_t[pl.ds(16 * i, 16), lanes] for i in range(16)]
        for b in range(7):
            acc = [jnp.zeros((16, 128), F32) for _ in range(7)]
            for r in range(22):
                line = pad[r, pl.ds(b, 16), lanes]
                for a in range(7):
                    i = r - a
                    if 0 <= i < 16:
                        acc[a] = acc[a] + line * lines[i]
            for a in range(7):
                sums[pl.ds(7 * a + b, 1), lanes] = jnp.sum(acc[a], axis=0, keepdims=True)
        return carry

    lax.fori_loop(0, 3, lane_block, 0)
    total = jnp.zeros((384, 192), F32)
    for ref in (v0, v1, v2, v3):
        total = total + ref[...].astype(F32)
    for q in range(6):
        out_ref[:, 128 * q : 128 * q + 128] = total[64 * q : 64 * q + 64, 0:128].astype(BF16)
    for q in range(3):
        both = jnp.concatenate(
            [total[128 * q : 128 * q + 64, 128:192], total[128 * q + 64 : 128 * q + 128, 128:192]],
            axis=1,
        )
        out_ref[:, 768 + 128 * q : 896 + 128 * q] = both.astype(BF16)
    folded = lax.dot_general(
        sums[...], fold[...], NN, precision=lax.Precision.HIGHEST, preferred_element_type=F32
    )
    out_ref[:, 1152:1280] = folded.astype(BF16)


def total_kernel(factor, in_ref, out_ref):
    total = jnp.sum(in_ref[...].astype(F32), axis=0, keepdims=True) * factor
    out_ref[...] = jnp.broadcast_to(total, in_ref.shape).astype(out_ref.dtype)


def finish_kernel(in_ref, dw_ref, w1_ref, w2_ref):
    for q in range(6):
        out, row = (w1_ref, 64 * q) if q < 3 else (w2_ref, 64 * q - 192)
        out[row : row + 64, 0:128] = in_ref[:, 128 * q : 128 * q + 128].astype(F32)
        lo = 768 + 128 * (q // 2) + 64 * (q % 2)
        out[row : row + 64, 128:192] = in_ref[:, lo : lo + 64].astype(F32)
    dw_ref[...] = in_ref[:, 1152:1280].astype(F32).T[0:48, 0:49]


def unmix_kernel(
    adj, grad_ref, par_ref, us, uc, ds_, dc, cot_ref, taps, up_p, mid_p, down_p,
    owned_ref, scale_ref, r0, r1, r2, r3,
    out_ref, gin_ref,
    table, up_g, mid_g, down_g, pad, result,
):
    me = lax.axis_index("tiles")
    odd = me & 1
    mine = lax.axis_index("chan")
    start = 16 * (me // 2) - 16
    table[pl.ds(16 + 8 * odd, 8)] = grad_ref[...]
    table[pl.ds(24 - 8 * odd, 8)] = par_ref[...]
    table[48] = jnp.zeros((48, 256), BF16)
    for t in range(4):
        for ref, side in ((us, odd), (uc, 1 - odd)):
            up = ref[t]
            table[8 * side + t, :, 128:256] = up
            table[8 * side + t + 4, :, 128:256] = swap_halves(up).astype(BF16)
        for ref, side in ((ds_, odd), (dc, 1 - odd)):
            down = ref[t]
            table[32 + 8 * side + t, :, 0:128] = down
            table[32 + 8 * side + t + 4, :, 0:128] = swap_halves(down).astype(BF16)
    for t in range(8):
        center = 16 + 8 * odd + t
        entries = [jnp.where(adj[t, k] < 512, adj[t, k] - start, 48) for k in range(8)]
        gather_tile(table, up_g, mid_g, down_g, t, center, entries)
    build_padded(pad, up_g, mid_g, down_g, up_p, mid_p, down_p)
    convolve(pad, taps, result, True)
    back = result[...].T.reshape(8, 48, 256)
    gin_ref[...] = (cot_ref[...].astype(F32) + back).astype(BF16)
    scale = column(scale_ref[...])
    for j, ref in enumerate((r0, r1, r2, r3)):
        first = 2 * ((mine + 4 - j) & 3)
        for i in range(2):
            out_ref[first + i] = (
                owned_ref[first + i].astype(F32) + scale * ref[i].astype(F32)
            ).astype(BF16)


def call(kernel, shapes, scratch=(), smem=0, n_in=0, name=None):
    vmem = pl.BlockSpec(memory_space=pltpu.VMEM)
    scalar = pl.BlockSpec(memory_space=pltpu.SMEM)
    many = isinstance(shapes, (list, tuple))
    return pl.pallas_call(
        kernel,
        out_shape=shapes,
        in_specs=[scalar] * smem + [vmem] * (n_in - smem),
        out_specs=[vmem] * len(shapes) if many else vmem,
        scratch_shapes=list(scratch),
        name=name,
    )


def shape(*dims, dtype=BF16):
    return jax.ShapeDtypeStruct(dims, dtype)


def along_chan(values):
    got = [values[0]]
    for j in range(1, 4):
        got.append(lax.ppermute(values[j], "chan", [(i, (i + j) % 4) for i in range(4)]))
    return got


def body(
    x_scan, slot_owner, adjacency, cotangent, dw_weight, ln_gain, w_in, b_in, w_out, layer_scale
):
    devices = lax.axis_size("tiles")
    up_p, mid_p, down_p = (jnp.asarray(v) for v in placement_tables())
    fold = jnp.asarray((np.arange(384)[:, None] % 48 == np.arange(128)[None, :]).astype(np.float32))
    scale_row = layer_scale.reshape(1, 48)

    def hop(value, target):
        pairs = [(i, target(i)) for i in range(devices)]
        return lax.ppermute(value, "tiles", [p for p in pairs if 0 <= p[1] < devices])

    tile_chunk = shape(2, 48, 256)
    prep = call(prepare_kernel, [shape(8, 48, 128)] + [tile_chunk] * 4, n_in=3, name="prepare")
    strips, *dbranch = prep(x_scan, cotangent, scale_row)
    par_x = hop(x_scan, lambda i: i ^ 1)
    par_slots = hop(slot_owner, lambda i: i ^ 1)
    near = hop(strips, lambda i: i + 1 if i & 1 else i - 1)
    far = hop(strips, lambda i: i + 2 if i & 1 else i - 2)
    taps = jnp.tile(dw_weight.T, (1, 8))

    small = jnp.zeros((16, 192), BF16).at[0].set(b_in).at[1, 0:48].set(ln_gain)
    packed = jnp.concatenate([w_in, w_out, small], axis=0)
    all_dbranch = along_chan(dbranch)
    all_weights = along_chan([packed] * 4)

    grid_scratch = lambda entries: [
        pltpu.VMEM((entries, 48, 256), BF16),
        pltpu.VMEM((384, 384), BF16),
        pltpu.VMEM((384, 768), BF16),
        pltpu.VMEM((384, 384), BF16),
        pltpu.VMEM((22, WIDE, 384), F32),
        pltpu.VMEM((256, 384), F32),
    ]
    mix = call(
        mix_kernel,
        [shape(8, 48, 256), shape(22, WIDE, 384)] + [tile_chunk] * 4,
        scratch=[pltpu.SMEM((8,), jnp.int32)] + grid_scratch(65) + [pltpu.VMEM((8, 48, 256), BF16)],
        smem=3,
        n_in=11,
        name="mix",
    )
    owned, padded, *mixed = mix(
        slot_owner, par_slots, adjacency, x_scan, par_x, near, far, taps, up_p, mid_p, down_p
    )
    all_mixed = along_chan(mixed)

    turn = call(
        weights_kernel,
        [
            shape(4, 192, 192),
            shape(4, 192, 192),
            shape(4, 192, 128, dtype=F32),
            shape(4, 48, 128, dtype=F32),
        ],
        n_in=4,
        name="turn",
    )
    turned = turn(*all_weights)

    mlp = call(
        mlp_kernel,
        [tile_chunk] * 8 + [shape(384, 192)] * 4,
        scratch=[pltpu.VMEM((4, 48, 512), BF16)] * 4,
        n_in=16,
        name="mlp",
    )
    results = mlp(*all_mixed, *all_dbranch, *all_weights, *turned)
    all_back = along_chan(results[0:4])
    collect = call(
        collect_kernel,
        [shape(8, 48, 256), shape(4, 48, 128), shape(4, 48, 128)],
        n_in=4,
        name="collect",
    )
    grads, top, bottom = collect(*all_back)
    par_grads = hop(grads, lambda i: i ^ 1)
    from_up = hop(bottom, lambda i: i + 2)
    from_up_cross = hop(bottom, lambda i: (i ^ 1) + 2)
    from_down = hop(top, lambda i: i - 2)
    from_down_cross = hop(top, lambda i: (i ^ 1) - 2)

    partials = results[8:12]
    all_partials = [partials[0]]
    for j in range(1, 4):
        all_partials.append(
            lax.ppermute(partials[j], "chan", [(i, (i - j) % 4) for i in range(4)])
        )
    all_branch = along_chan(results[4:8])

    tap_sums = call(
        taps_kernel,
        shape(64, 1280),
        scratch=[
            pltpu.VMEM((22, WIDE, 384), F32),
            pltpu.VMEM((256, 384), F32),
            pltpu.VMEM((64, 384), F32),
        ],
        n_in=7,
        name="tap_sums",
    )
    pieces = tap_sums(grads, padded, fold, *all_partials)
    arrived = lax.all_to_all(pieces, "tiles", 0, 0, tiled=True)
    factor = 1.0 / math.sqrt(adjacency.shape[0] * devices * PIX)
    totals = call(
        functools.partial(total_kernel, factor), shape(64, 1280), n_in=1, name="totals"
    )(arrived)
    spread = lax.all_to_all(totals, "tiles", 0, 0, tiled=True)

    unmix = call(
        unmix_kernel,
        [shape(8, 48, 256), shape(8, 48, 256)],
        scratch=grid_scratch(49),
        smem=1,
        n_in=18,
        name="unmix",
    )
    output, grad_in = unmix(
        adjacency, grads, par_grads, from_up, from_up_cross, from_down, from_down_cross,
        cotangent, taps, up_p, mid_p, down_p, owned, scale_row, *all_branch
    )
    grad_dw, grad_w1, grad_w2 = call(
        finish_kernel,
        [shape(48, 49, dtype=F32), shape(192, 192, dtype=F32), shape(192, 192, dtype=F32)],
        n_in=1,
        name="finish",
    )(spread)
    return (output, grad_in, grad_dw, grad_w1, grad_w2)


def solution(mesh):
    in_specs = (
        P("tiles", "chan", None),
        P("tiles"),
        P("tiles", None),
        P("tiles", "chan", None),
        P("chan", None),
        P("chan"),
        P(None, "chan"),
        P("chan"),
        P("chan", None),
        P("chan"),
    )
    out_specs = (
        P("tiles", "chan", None),
        P("tiles", "chan", None),
        P("chan", None),
        P(None, "chan"),
        P("chan", None),
    )
    return jax.shard_map(body, mesh=mesh, in_specs=in_specs, out_specs=out_specs, check_vma=False)
```

```python
import functools
import math

import jax
import jax.numpy as jnp
import numpy as np
from jax import lax
from jax.experimental import pallas as pl
from jax.experimental.pallas import tpu as pltpu
from jax.sharding import PartitionSpec as P

CHANNELS = 192
SIDE = 16
PIX = 256
WIDE = 24
EPSILON = 1e-06
GELU_SCALE = 0.7978845608
GELU_CUBIC = 0.044715

F32 = jnp.float32
BF16 = jnp.bfloat16
NT = (((1,), (1,)), ((), ()))
NN = (((1,), (0,)), ((), ()))


def dot(a, b, dims):
    return lax.dot_general(a, b, dims, preferred_element_type=F32)


def placement_tables():
    up = np.zeros((72, 384), np.float32)
    mid = np.zeros((384, 768), np.float32)
    down = np.zeros((72, 384), np.float32)
    for j in range(22):
        if j < 3:
            side, col = 0, 13 + j
        elif j < 19:
            side, col = 1, j - 3
        else:
            side, col = 2, j - 19
        for i in range(3):
            up[i * WIDE + j, 128 * side + 16 * (13 + i) + col - 128] = 1
            down[i * WIDE + j, 128 * side + 16 * i + col] = 1
        for i in range(16):
            block = (1, 0, 2)[side]
            mid[i * WIDE + j, 256 * block + 16 * i + col] = 1
    return up.astype(jnp.bfloat16), mid.astype(jnp.bfloat16), down.astype(jnp.bfloat16)


def column(row):
    n = row.shape[1]
    same = lax.broadcasted_iota(jnp.int32, (n, n), 0) == lax.broadcasted_iota(jnp.int32, (n, n), 1)
    return jnp.sum(jnp.where(same, jnp.broadcast_to(row, (n, n)), 0.0), axis=1, keepdims=True)


def eye(n):
    same = lax.broadcasted_iota(jnp.int32, (n, n), 0) == lax.broadcasted_iota(jnp.int32, (n, n), 1)
    return same.astype(F32).astype(BF16)


def swap_halves(value):
    return pltpu.roll(value.astype(F32), 64, 1)


def low_lanes(shape):
    return lax.broadcasted_iota(jnp.int32, shape, 1) < 64


def pack_pair(natural, other, natural_low):
    shape = natural.shape
    keep = low_lanes(shape) if natural_low else jnp.logical_not(low_lanes(shape))
    return jnp.where(keep, natural.astype(F32), swap_halves(other)).astype(BF16)


def strips_kernel(x_ref, strips_ref):
    odd = lax.axis_index("tiles") & 1

    @pl.when(odd == 1)
    def _():
        for s in range(8):
            strips_ref[s] = pack_pair(x_ref[s, :, 128:256], x_ref[s + 8, :, 128:256], False)

    @pl.when(odd == 0)
    def _():
        for s in range(8):
            strips_ref[s] = pack_pair(x_ref[s, :, 0:128], x_ref[s + 8, :, 0:128], True)


def sends_kernel(cot_ref, scale_ref, in_ref, w_out_ref, b_ref, gain_ref, *rest):
    outs, small = rest[0:4], rest[4]
    mine = lax.axis_index("chan")
    scale = column(scale_ref[...])
    small[...] = jnp.zeros((16, 256), F32)
    small[0:1, 0:192] = b_ref[...].astype(F32)
    small[1:2, 0:48] = gain_ref[...].astype(F32)
    tails = []
    for ref in (in_ref, w_out_ref):
        tail = ref[:, 128:192].astype(F32)
        tails.append(jnp.concatenate([tail[0:96], tail[96:192]], axis=1).astype(BF16))
    for j, out in enumerate(outs):
        first = 2 * ((mine + j) & 3)
        for i in range(2):
            out[48 * i : 48 * i + 48] = (cot_ref[first + i].astype(F32) * scale).astype(BF16)
        out[96:288, 0:128] = in_ref[:, 0:128]
        out[96:288, 128:256] = w_out_ref[:, 0:128]
        out[288:384, 0:128] = tails[0]
        out[288:384, 128:256] = tails[1]
        out[384:400] = small[...].astype(BF16)


def gather_tile(table, up_g, mid_g, down_g, t, center, entries):
    rows = pl.ds(48 * t, 48)
    mid_g[rows, 0:256] = table[center]
    mid_g[rows, 256:512] = table[entries[3]]
    mid_g[rows, 512:768] = table[entries[4]]
    for k in range(3):
        up_g[rows, 128 * k : 128 * k + 128] = table[entries[k], :, 128:256]
        down_g[rows, 128 * k : 128 * k + 128] = table[entries[5 + k], :, 0:128]


def build_padded(pad, up_g, mid_g, down_g, up_p, mid_p, down_p):
    pad[0:3] = dot(up_p[...], up_g[...], NT).reshape(3, WIDE, 384)
    pad[3:19] = dot(mid_p[...], mid_g[...], NT).reshape(16, WIDE, 384)
    pad[19:22] = dot(down_p[...], down_g[...], NT).reshape(3, WIDE, 384)


def convolve(pad, taps, result, flip):
    def lane_block(block, carry):
        lanes = pl.ds(pl.multiple_of(block * 128, 128), 128)
        acc = [jnp.zeros((16, 128), F32) for _ in range(16)]
        for b in range(7):
            weights = []
            for a in range(7):
                tap = 7 * a + b
                weights.append(taps[pl.ds(48 - tap if flip else tap, 1), lanes])
            for r in range(22):
                line = pad[r, pl.ds(b, 16), lanes]
                for a in range(7):
                    i = r - a
                    if 0 <= i < 16:
                        acc[i] = acc[i] + line * weights[a]
        for i in range(16):
            result[pl.ds(16 * i, 16), lanes] = acc[i]
        return carry

    lax.fori_loop(0, 3, lane_block, 0)


OFFSETS = (-17, -16, -15, -1, 1, 15, 16, 17)


def mix_kernel(
    own_slots, par_slots, adj, x_ref, par_ref, sa_ref, sb_ref, taps, up_p, mid_p, down_p,
    owned_ref, pad_out, m0, m1, m2, m3,
    place, table, up_g, mid_g, down_g, pad, result, flat,
):
    me = lax.axis_index("tiles")
    odd = me & 1
    mine = lax.axis_index("chan")
    base = 8 * me
    for t in range(8):
        place[t] = 0
    for s in range(16):
        for slots, row in ((own_slots, odd), (par_slots, 1 - odd)):
            t = slots[s] - base

            @pl.when((t >= 0) & (t < 8))
            def _():
                place[t] = 16 + 16 * row + s

    table[pl.ds(16 + 16 * odd, 16)] = x_ref[...]
    table[pl.ds(32 - 16 * odd, 16)] = par_ref[...]
    table[64] = jnp.zeros((48, 256), BF16)

    def halo_rows(above, below):
        for s in range(8):
            up = above[s]
            table[s, :, 128:256] = up
            table[s + 8, :, 128:256] = swap_halves(up).astype(BF16)
            down = below[s]
            table[48 + s, :, 0:128] = down
            table[56 + s, :, 0:128] = swap_halves(down).astype(BF16)

    @pl.when(odd == 0)
    def _():
        halo_rows(sa_ref, sb_ref)

    @pl.when(odd == 1)
    def _():
        halo_rows(sb_ref, sa_ref)

    for t in range(8):
        center = place[t]
        entries = [jnp.where(adj[t, k] < 512, center + OFFSETS[k], 64) for k in range(8)]
        gather_tile(table, up_g, mid_g, down_g, t, center, entries)
    owned_ref[...] = mid_g[:, 0:256].reshape(8, 48, 256)
    build_padded(pad, up_g, mid_g, down_g, up_p, mid_p, down_p)
    pad_out[...] = pad[...].astype(BF16)
    convolve(pad, taps, result, False)
    flat[...] = result[...].T.astype(BF16).reshape(8, 48, 256)
    for j, out in enumerate((m0, m1, m2, m3)):
        first = 2 * ((mine + j) & 3)
        out[0] = flat[first]
        out[1] = flat[first + 1]


def turn_kernel(p0, p1, p2, p3, w_in, w_out, in_t, out_t, bias, gain, dbranch):
    mine = lax.axis_index("chan")
    unit = eye(192)
    for j, ref in enumerate((p0, p1, p2, p3)):
        a = (mine + 4 - j) & 3
        for i in range(2):
            dbranch[a, :, 256 * i : 256 * i + 256] = ref[48 * i : 48 * i + 48]
        for full, turned, lanes in ((w_in, in_t, 0), (w_out, out_t, 128)):
            tail = ref[288:384, lanes : lanes + 128].astype(F32)
            whole = jnp.concatenate(
                [
                    ref[96:288, lanes : lanes + 128].astype(F32),
                    jnp.concatenate([tail[:, 0:64], tail[:, 64:128]], axis=0),
                ],
                axis=1,
            ).astype(BF16)
            full[j] = whole
            turned[j] = dot(unit, whole, NT).astype(BF16)
        cols = dot(unit, ref[384:400, 0:192], NT)
        bias[j] = jnp.broadcast_to(cols[:, 0:1], (192, 128))
        gain[a] = jnp.broadcast_to(cols[0:48, 1:2], (48, 128))


def across(col_block):
    return jnp.concatenate([col_block] * 4, axis=1)


def mlp_kernel(
    m0, m1, m2, m3, w_in, w_out, in_t, out_t, bias, gain, db_ref,
    g0, g1, g2, g3, r0, r1, r2, r3, act_ref, pre_ref, normed_ref,
    mixed_s, back_s, branch_s,
):
    mine = lax.axis_index("chan")
    for j, m_ref in enumerate((m0, m1, m2, m3)):
        a = (mine + 4 - j) & 3
        for i in range(2):
            mixed_s[a, :, 256 * i : 256 * i + 256] = m_ref[i]
    mixed = mixed_s[...].reshape(192, 512).astype(F32)
    dbranch = db_ref[...].reshape(192, 512)
    mean = jnp.sum(mixed, axis=0, keepdims=True) / CHANNELS
    inv = lax.rsqrt(
        jnp.sum(mixed * mixed, axis=0, keepdims=True) / CHANNELS - mean * mean + EPSILON
    )
    x_hat = (mixed - mean) * inv
    gain_full = across(gain[...].reshape(192, 128))
    normed = (x_hat * gain_full).astype(BF16)
    normed_ref[...] = normed
    branch = jnp.zeros((192, 512), F32)
    dnormed = jnp.zeros((192, 512), F32)
    for j in range(4):
        preact = dot(in_t[j], normed, NN) + across(bias[j])
        square = preact * preact
        tangent = jnp.tanh(GELU_SCALE * (preact + GELU_CUBIC * square * preact))
        half = 0.5 * (1.0 + tangent)
        act = (preact * half).astype(BF16)
        slope = half + 0.5 * preact * (1.0 - tangent * tangent) * (
            GELU_SCALE * (1.0 + 3.0 * GELU_CUBIC * square)
        )
        branch = branch + dot(out_t[j], act, NN)
        pre_grad = (dot(w_out[j], dbranch, NN) * slope).astype(BF16)
        dnormed = dnormed + dot(w_in[j], pre_grad, NN)
        act_ref[j] = act
        pre_ref[j] = pre_grad
    xhat_grad = dnormed * gain_full
    first = jnp.sum(xhat_grad, axis=0, keepdims=True) / CHANNELS
    second = jnp.sum(xhat_grad * x_hat, axis=0, keepdims=True) / CHANNELS
    dmixed = (inv * (xhat_grad - first - x_hat * second)).astype(BF16)
    back_s[...] = dmixed.reshape(4, 48, 512)
    branch_s[...] = branch.astype(BF16).reshape(4, 48, 512)
    for j, (g_ref, r_ref) in enumerate(((g0, r0), (g1, r1), (g2, r2), (g3, r3))):
        a = (mine + j) & 3
        for i in range(2):
            g_ref[i] = back_s[a, :, 256 * i : 256 * i + 256]
            r_ref[i] = branch_s[a, :, 256 * i : 256 * i + 256]


def outer_kernel(act_ref, pre_ref, normed_ref, db_ref, v0, v1, v2, v3):
    normed = normed_ref[...]
    dbranch = db_ref[...].reshape(192, 512)
    for j, v_ref in enumerate((v0, v1, v2, v3)):
        v_ref[0:192] = dot(normed, pre_ref[j], NT).astype(BF16)
        v_ref[192:384] = dot(act_ref[j], dbranch, NT).astype(BF16)


def taps_kernel(
    g0, g1, g2, g3, pad_ref, fold, grad_ref, top_ref, bottom_ref, out_ref, pad, grad_t, sums
):
    mine = lax.axis_index("chan")
    for j, ref in enumerate((g0, g1, g2, g3)):
        grad_ref[pl.ds(2 * ((mine + 4 - j) & 3), 2)] = ref[...]
    for t in range(4):
        top_ref[t] = pack_pair(grad_ref[t, :, 0:128], grad_ref[t + 4, :, 0:128], True)
        bottom_ref[t] = pack_pair(grad_ref[t, :, 128:256], grad_ref[t + 4, :, 128:256], False)
    pad[...] = pad_ref[...].astype(F32)
    grad_t[...] = grad_ref[...].reshape(384, 256).astype(F32).T
    sums[...] = jnp.zeros((64, 384), F32)

    def lane_block(block, carry):
        lanes = pl.ds(pl.multiple_of(block * 128, 128), 128)
        lines = [grad_t[pl.ds(16 * i, 16), lanes] for i in range(16)]
        for b in range(7):
            acc = [jnp.zeros((16, 128), F32) for _ in range(7)]
            for r in range(22):
                line = pad[r, pl.ds(b, 16), lanes]
                for a in range(7):
                    i = r - a
                    if 0 <= i < 16:
                        acc[a] = acc[a] + line * lines[i]
            for a in range(7):
                sums[pl.ds(7 * a + b, 1), lanes] = jnp.sum(acc[a], axis=0, keepdims=True)
        return carry

    lax.fori_loop(0, 3, lane_block, 0)
    out_ref[...] = lax.dot_general(
        sums[...], fold[...], NN, precision=lax.Precision.HIGHEST, preferred_element_type=F32
    )


def pieces_kernel(v0, v1, v2, v3, taps_ref, out_ref, total, rows):
    total[...] = (
        v0[...].astype(F32) + v1[...].astype(F32) + v2[...].astype(F32) + v3[...].astype(F32)
    )
    rows[...] = jnp.zeros((64, 16, 128), F32)
    for q in range(6):
        rows[:, q, :] = total[64 * q : 64 * q + 64, 0:128]
    for q in range(3):
        rows[:, 6 + q, :] = jnp.concatenate(
            [total[128 * q : 128 * q + 64, 128:192], total[128 * q + 64 : 128 * q + 128, 128:192]],
            axis=1,
        )
    rows[:, 9, :] = taps_ref[...]
    out_ref[...] = rows[...].astype(BF16)


def total_kernel(factor, in_ref, out_ref):
    total = jnp.sum(in_ref[...].astype(F32), axis=0, keepdims=True) * factor
    out_ref[...] = jnp.broadcast_to(total, in_ref.shape).astype(out_ref.dtype)


def finish_kernel(in_ref, dw_ref, w1_ref, w2_ref, rows):
    rows[...] = in_ref[...].astype(F32)
    for q in range(6):
        out, row = (w1_ref, 64 * q) if q < 3 else (w2_ref, 64 * q - 192)
        out[row : row + 64, 0:128] = rows[:, q, :]
    for q in range(3):
        both = rows[:, 6 + q, :]
        for half in range(2):
            row = 128 * q + 64 * half
            out, row = (w1_ref, row) if row < 192 else (w2_ref, row - 192)
            out[row : row + 64, 128:192] = both[:, 64 * half : 64 * half + 64]
    dw_ref[...] = rows[:, 9, :].T[0:48, 0:49]


def unmix_kernel(
    adj, grad_ref, par_ref, us, uc, ds_, dc, cot_ref, taps, up_p, mid_p, down_p,
    owned_ref, scale_ref, r0, r1, r2, r3,
    out_ref, gin_ref,
    table, up_g, mid_g, down_g, pad, result,
):
    me = lax.axis_index("tiles")
    odd = me & 1
    mine = lax.axis_index("chan")
    start = 16 * (me // 2) - 16
    table[pl.ds(16 + 8 * odd, 8)] = grad_ref[...]
    table[pl.ds(24 - 8 * odd, 8)] = par_ref[...]
    table[48] = jnp.zeros((48, 256), BF16)
    for t in range(4):
        for ref, side in ((us, odd), (uc, 1 - odd)):
            up = ref[t]
            table[8 * side + t, :, 128:256] = up
            table[8 * side + t + 4, :, 128:256] = swap_halves(up).astype(BF16)
        for ref, side in ((ds_, odd), (dc, 1 - odd)):
            down = ref[t]
            table[32 + 8 * side + t, :, 0:128] = down
            table[32 + 8 * side + t + 4, :, 0:128] = swap_halves(down).astype(BF16)
    for t in range(8):
        center = 16 + 8 * odd + t
        entries = [jnp.where(adj[t, k] < 512, adj[t, k] - start, 48) for k in range(8)]
        gather_tile(table, up_g, mid_g, down_g, t, center, entries)
    build_padded(pad, up_g, mid_g, down_g, up_p, mid_p, down_p)
    convolve(pad, taps, result, True)
    back = result[...].T.reshape(8, 48, 256)
    gin_ref[...] = (cot_ref[...].astype(F32) + back).astype(BF16)
    scale = column(scale_ref[...])
    for j, ref in enumerate((r0, r1, r2, r3)):
        first = 2 * ((mine + 4 - j) & 3)
        for i in range(2):
            out_ref[first + i] = (
                owned_ref[first + i].astype(F32) + scale * ref[i].astype(F32)
            ).astype(BF16)


def call(kernel, shapes, scratch=(), smem=0, n_in=0, name=None):
    vmem = pl.BlockSpec(memory_space=pltpu.VMEM)
    scalar = pl.BlockSpec(memory_space=pltpu.SMEM)
    many = isinstance(shapes, (list, tuple))
    return pl.pallas_call(
        kernel,
        out_shape=shapes,
        in_specs=[scalar] * smem + [vmem] * (n_in - smem),
        out_specs=[vmem] * len(shapes) if many else vmem,
        scratch_shapes=list(scratch),
        name=name,
    )


def shape(*dims, dtype=BF16):
    return jax.ShapeDtypeStruct(dims, dtype)


def along_chan(values):
    got = [values[0]]
    for j in range(1, 4):
        got.append(lax.ppermute(values[j], "chan", [(i, (i + j) % 4) for i in range(4)]))
    return got


def body(
    x_scan, slot_owner, adjacency, cotangent, dw_weight, ln_gain, w_in, b_in, w_out, layer_scale
):
    devices = lax.axis_size("tiles")
    up_p, mid_p, down_p = (jnp.asarray(v) for v in placement_tables())
    fold = jnp.asarray((np.arange(384)[:, None] % 48 == np.arange(128)[None, :]).astype(np.float32))
    scale_row = layer_scale.reshape(1, 48)

    def hop(value, target):
        pairs = [(i, target(i)) for i in range(devices)]
        return lax.ppermute(value, "tiles", [p for p in pairs if 0 <= p[1] < devices])

    def after(value, *first):
        return lax.optimization_barrier((value, first))[0]

    tile_chunk = shape(2, 48, 256)
    par_x = hop(x_scan, lambda i: i ^ 1)
    par_slots = hop(slot_owner, lambda i: i ^ 1)
    strips = call(strips_kernel, shape(8, 48, 128), n_in=1, name="strips")(x_scan)
    near = hop(strips, lambda i: i + 1 if i & 1 else i - 1)
    far = hop(strips, lambda i: i + 2 if i & 1 else i - 2)
    taps = jnp.tile(after(dw_weight, strips).T, (1, 8))

    sends = call(
        sends_kernel,
        [shape(400, 256)] * 4,
        scratch=[pltpu.VMEM((16, 256), F32)],
        n_in=6,
        name="sends",
    )(
        cotangent, after(scale_row, strips), w_in, w_out,
        b_in.reshape(1, 192), ln_gain.reshape(1, 48),
    )
    all_sends = along_chan(sends)

    grid_scratch = lambda entries: [
        pltpu.VMEM((entries, 48, 256), BF16),
        pltpu.VMEM((384, 384), BF16),
        pltpu.VMEM((384, 768), BF16),
        pltpu.VMEM((384, 384), BF16),
        pltpu.VMEM((22, WIDE, 384), F32),
        pltpu.VMEM((256, 384), F32),
    ]
    mix = call(
        mix_kernel,
        [shape(8, 48, 256), shape(22, WIDE, 384)] + [tile_chunk] * 4,
        scratch=[pltpu.SMEM((8,), jnp.int32)] + grid_scratch(65) + [pltpu.VMEM((8, 48, 256), BF16)],
        smem=3,
        n_in=11,
        name="mix",
    )
    owned, padded, *mixed = mix(
        slot_owner, par_slots, adjacency, x_scan, par_x, near, far, taps, up_p, mid_p, down_p
    )
    all_mixed = along_chan(mixed)

    square = shape(4, 192, 192)
    turn = call(
        turn_kernel,
        [square] * 4
        + [shape(4, 192, 128, dtype=F32), shape(4, 48, 128, dtype=F32), shape(4, 48, 512)],
        n_in=4,
        name="turn",
    )
    turned = turn(*after(all_sends, mixed[0]))

    hidden = shape(4, 192, 512)
    results = call(
        mlp_kernel,
        [tile_chunk] * 8 + [hidden, hidden, shape(192, 512)],
        scratch=[pltpu.VMEM((4, 48, 512), BF16)] * 3,
        n_in=11,
        name="mlp",
    )(*all_mixed, *turned)
    all_back = along_chan(results[0:4])
    partials = call(outer_kernel, [shape(384, 192)] * 4, n_in=4, name="outer")(
        *results[8:11], turned[6]
    )
    all_partials = [partials[0]]
    for j in range(1, 4):
        all_partials.append(
            lax.ppermute(partials[j], "chan", [(i, (i - j) % 4) for i in range(4)])
        )
    grads, top, bottom, tap_sums = call(
        taps_kernel,
        [shape(8, 48, 256), shape(4, 48, 128), shape(4, 48, 128), shape(64, 128, dtype=F32)],
        scratch=[
            pltpu.VMEM((22, WIDE, 384), F32),
            pltpu.VMEM((256, 384), F32),
            pltpu.VMEM((64, 384), F32),
        ],
        n_in=6,
        name="tap_sums",
    )(*all_back, padded, fold)
    pieces = call(
        pieces_kernel,
        shape(64, 16, 128),
        scratch=[pltpu.VMEM((384, 192), F32), pltpu.VMEM((64, 16, 128), F32)],
        n_in=5,
        name="pieces",
    )(*all_partials, tap_sums)
    arrived = lax.all_to_all(pieces, "tiles", 0, 0, tiled=True)

    grads, top, bottom = after((grads, top, bottom), pieces)
    par_grads = hop(grads, lambda i: i ^ 1)
    from_up = hop(bottom, lambda i: i + 2)
    from_up_cross = hop(bottom, lambda i: (i ^ 1) + 2)
    from_down = hop(top, lambda i: i - 2)
    from_down_cross = hop(top, lambda i: (i ^ 1) - 2)
    all_branch = along_chan(after(results[4:8], pieces))

    factor = 1.0 / math.sqrt(adjacency.shape[0] * devices * PIX)
    totals = call(
        functools.partial(total_kernel, factor), shape(64, 16, 128), n_in=1, name="totals"
    )(arrived)
    spread = lax.all_to_all(totals, "tiles", 0, 0, tiled=True)

    unmix = call(
        unmix_kernel,
        [shape(8, 48, 256), shape(8, 48, 256)],
        scratch=grid_scratch(49),
        smem=1,
        n_in=18,
        name="unmix",
    )
    output, grad_in = unmix(
        adjacency, grads, par_grads, from_up, from_up_cross, from_down, from_down_cross,
        cotangent, taps, up_p, mid_p, down_p, owned, after(scale_row, totals), *all_branch
    )
    grad_dw, grad_w1, grad_w2 = call(
        finish_kernel,
        [shape(48, 49, dtype=F32), shape(192, 192, dtype=F32), shape(192, 192, dtype=F32)],
        scratch=[pltpu.VMEM((64, 16, 128), F32)],
        n_in=1,
        name="finish",
    )(spread)
    return (output, grad_in, grad_dw, grad_w1, grad_w2)


def solution(mesh):
    in_specs = (
        P("tiles", "chan", None),
        P("tiles"),
        P("tiles", None),
        P("tiles", "chan", None),
        P("chan", None),
        P("chan"),
        P(None, "chan"),
        P("chan"),
        P("chan", None),
        P("chan"),
    )
    out_specs = (
        P("tiles", "chan", None),
        P("tiles", "chan", None),
        P("chan", None),
        P(None, "chan"),
        P("chan", None),
    )
    return jax.shard_map(body, mesh=mesh, in_specs=in_specs, out_specs=out_specs, check_vma=False)
```

```python
import functools
import math

import jax
import jax.numpy as jnp
import numpy as np
from jax import lax
from jax.experimental import pallas as pl
from jax.experimental.pallas import tpu as pltpu
from jax.sharding import Mesh
from jax.sharding import PartitionSpec as P

CHANNELS = 192
SIDE = 16
PIX = 256
WIDE = 24
EPSILON = 1e-06
GELU_SCALE = 0.7978845608
GELU_CUBIC = 0.044715

F32 = jnp.float32
BF16 = jnp.bfloat16
NT = (((1,), (1,)), ((), ()))
NN = (((1,), (0,)), ((), ()))


def dot(a, b, dims):
    return lax.dot_general(a, b, dims, preferred_element_type=F32)


def placement_tables():
    up = np.zeros((72, 384), np.float32)
    mid = np.zeros((384, 768), np.float32)
    down = np.zeros((72, 384), np.float32)
    for j in range(22):
        if j < 3:
            side, col = 0, 13 + j
        elif j < 19:
            side, col = 1, j - 3
        else:
            side, col = 2, j - 19
        for i in range(3):
            up[i * WIDE + j, 128 * side + 16 * (13 + i) + col - 128] = 1
            down[i * WIDE + j, 128 * side + 16 * i + col] = 1
        for i in range(16):
            block = (1, 0, 2)[side]
            mid[i * WIDE + j, 256 * block + 16 * i + col] = 1
    return up.astype(jnp.bfloat16), mid.astype(jnp.bfloat16), down.astype(jnp.bfloat16)


def column(row):
    n = row.shape[1]
    same = lax.broadcasted_iota(jnp.int32, (n, n), 0) == lax.broadcasted_iota(jnp.int32, (n, n), 1)
    return jnp.sum(jnp.where(same, jnp.broadcast_to(row, (n, n)), 0.0), axis=1, keepdims=True)


def eye(n):
    same = lax.broadcasted_iota(jnp.int32, (n, n), 0) == lax.broadcasted_iota(jnp.int32, (n, n), 1)
    return same.astype(F32).astype(BF16)


def swap_halves(value):
    return pltpu.roll(value.astype(F32), 64, 1)


def low_lanes(shape):
    return lax.broadcasted_iota(jnp.int32, shape, 1) < 64


def pack_pair(natural, other, natural_low):
    shape = natural.shape
    keep = low_lanes(shape) if natural_low else jnp.logical_not(low_lanes(shape))
    return jnp.where(keep, natural.astype(F32), swap_halves(other)).astype(BF16)


def my_owner():
    return 2 * lax.axis_index("chip") + lax.axis_index("core")


def strips_kernel(x_ref, strips_ref):
    odd = lax.axis_index("core")

    @pl.when(odd == 1)
    def _():
        for s in range(8):
            strips_ref[s] = pack_pair(x_ref[s, :, 128:256], x_ref[s + 8, :, 128:256], False)

    @pl.when(odd == 0)
    def _():
        for s in range(8):
            strips_ref[s] = pack_pair(x_ref[s, :, 0:128], x_ref[s + 8, :, 0:128], True)


def pack_tail(value):
    return jnp.concatenate([value[0:96], value[96:192]], axis=1)


def unpack_tail(value):
    return jnp.concatenate([value[:, 0:64], value[:, 64:128]], axis=0)


def sends_kernel(cot_ref, scale_ref, in_ref, w_out_ref, b_ref, gain_ref, dw_ref, spread, *rest):
    outs, taps_ref, small, turned = rest[0:4], rest[4], rest[5], rest[6]
    turned[...] = jnp.zeros((128, 128), F32)
    turned[0:48, 0:49] = dw_ref[...]
    taps_ref[...] = lax.dot_general(
        turned[...].T[0:56], spread[...], NN,
        precision=lax.Precision.HIGHEST, preferred_element_type=F32,
    )
    mine = lax.axis_index("chan")
    scale = column(scale_ref[...])
    small[...] = jnp.zeros((16, 256), F32)
    small[0:1, 0:192] = b_ref[...].astype(F32)
    small[1:2, 0:48] = gain_ref[...].astype(F32)
    tails = []
    for ref in (in_ref, w_out_ref):
        tails.append(pack_tail(ref[:, 128:192].astype(F32)).astype(BF16))
    for j, out in enumerate(outs):
        first = 2 * ((mine + j) & 3)
        for i in range(2):
            out[48 * i : 48 * i + 48] = (cot_ref[first + i].astype(F32) * scale).astype(BF16)
        out[96:288, 0:128] = in_ref[:, 0:128]
        out[96:288, 128:256] = w_out_ref[:, 0:128]
        out[288:384, 0:128] = tails[0]
        out[288:384, 128:256] = tails[1]
        out[384:400] = small[...].astype(BF16)


def gather_tile(table, up_g, mid_g, down_g, t, center, entries):
    rows = pl.ds(48 * t, 48)
    mid_g[rows, 0:256] = table[center]
    mid_g[rows, 256:512] = table[entries[3]]
    mid_g[rows, 512:768] = table[entries[4]]
    for k in range(3):
        up_g[rows, 128 * k : 128 * k + 128] = table[entries[k], :, 128:256]
        down_g[rows, 128 * k : 128 * k + 128] = table[entries[5 + k], :, 0:128]


def build_padded(pad, up_g, mid_g, down_g, up_p, mid_p, down_p):
    pad[0:3] = dot(up_p[...], up_g[...], NT).reshape(3, WIDE, 384)
    pad[3:19] = dot(mid_p[...], mid_g[...], NT).reshape(16, WIDE, 384)
    pad[19:22] = dot(down_p[...], down_g[...], NT).reshape(3, WIDE, 384)


def convolve(pad, taps, result, flip):
    def lane_block(block, carry):
        lanes = pl.ds(pl.multiple_of(block * 128, 128), 128)
        acc = [jnp.zeros((16, 128), F32) for _ in range(16)]
        for b in range(7):
            weights = []
            for a in range(7):
                tap = 7 * a + b
                weights.append(taps[pl.ds(48 - tap if flip else tap, 1), lanes])
            for r in range(22):
                line = pad[r, pl.ds(b, 16), lanes]
                for a in range(7):
                    i = r - a
                    if 0 <= i < 16:
                        acc[i] = acc[i] + line * weights[a]
        for i in range(16):
            result[pl.ds(16 * i, 16), lanes] = acc[i]
        return carry

    lax.fori_loop(0, 3, lane_block, 0)


def fill_edges(table, near_ref, far_ref, below):
    odd = lax.axis_index("core")

    def fill(upper, lower):
        for s in range(8):
            up = upper[s]
            table[s, :, 128:256] = up
            table[s + 8, :, 128:256] = swap_halves(up).astype(BF16)
            down = lower[s]
            table[below + s, :, 0:128] = down
            table[below + 8 + s, :, 0:128] = swap_halves(down).astype(BF16)

    @pl.when(odd == 0)
    def _():
        fill(near_ref, far_ref)

    @pl.when(odd == 1)
    def _():
        fill(far_ref, near_ref)


OFFSETS = (-17, -16, -15, -1, 1, 15, 16, 17)


def mix_kernel(
    own_slots, par_slots, adj, x_ref, par_ref, near_ref, far_ref, taps, up_p, mid_p, down_p,
    owned_ref, pad_out, m0, m1, m2, m3,
    place, table, up_g, mid_g, down_g, pad, result, flat,
):
    me = my_owner()
    odd = lax.axis_index("core")
    mine = lax.axis_index("chan")
    base = 8 * me
    for t in range(8):
        place[t] = 0
    for s in range(16):
        for slots, row in ((own_slots, odd), (par_slots, 1 - odd)):
            t = slots[s] - base

            @pl.when((t >= 0) & (t < 8))
            def _():
                place[t] = 16 + 16 * row + s

    table[pl.ds(16 + 16 * odd, 16)] = x_ref[...]
    table[pl.ds(32 - 16 * odd, 16)] = par_ref[...]
    table[64] = jnp.zeros((48, 256), BF16)

    fill_edges(table, near_ref, far_ref, 48)
    for t in range(8):
        center = place[t]
        entries = [jnp.where(adj[t, k] < 512, center + OFFSETS[k], 64) for k in range(8)]
        gather_tile(table, up_g, mid_g, down_g, t, center, entries)
    owned_ref[...] = mid_g[:, 0:256].reshape(8, 48, 256)
    build_padded(pad, up_g, mid_g, down_g, up_p, mid_p, down_p)
    pad_out[...] = pad[...].astype(BF16)
    convolve(pad, taps, result, False)
    flat[...] = result[...].T.astype(BF16).reshape(8, 48, 256)
    for j, out in enumerate((m0, m1, m2, m3)):
        first = 2 * ((mine + j) & 3)
        out[0] = flat[first]
        out[1] = flat[first + 1]


def turn_kernel(p0, p1, p2, p3, w_in, w_out, in_t, out_t, bias, gain, dbranch):
    mine = lax.axis_index("chan")
    unit = eye(192)
    for j, ref in enumerate((p0, p1, p2, p3)):
        a = (mine + 4 - j) & 3
        for i in range(2):
            dbranch[a, :, 256 * i : 256 * i + 256] = ref[48 * i : 48 * i + 48]
        for full, turned, lanes in ((w_in, in_t, 0), (w_out, out_t, 128)):
            tail = ref[288:384, lanes : lanes + 128].astype(F32)
            whole = jnp.concatenate(
                [
                    ref[96:288, lanes : lanes + 128].astype(F32),
                    unpack_tail(tail),
                ],
                axis=1,
            ).astype(BF16)
            full[j] = whole
            turned[j] = dot(unit, whole, NT).astype(BF16)
        cols = dot(unit, ref[384:400, 0:192], NT)
        bias[j] = jnp.broadcast_to(cols[:, 0:1], (192, 128))
        gain[a] = jnp.broadcast_to(cols[0:48, 1:2], (48, 128))


def across(col_block):
    return jnp.concatenate([col_block] * 4, axis=1)


def mlp_kernel(
    m0, m1, m2, m3, w_in, w_out, in_t, out_t, bias, gain, db_ref,
    g0, g1, g2, g3, mixed_s, back_s, branch_s,
):
    mine = lax.axis_index("chan")
    for j, m_ref in enumerate((m0, m1, m2, m3)):
        a = (mine + 4 - j) & 3
        for i in range(2):
            mixed_s[a, :, 256 * i : 256 * i + 256] = m_ref[i]
    mixed = mixed_s[...].reshape(192, 512).astype(F32)
    dbranch = db_ref[...].reshape(192, 512)
    mean = jnp.sum(mixed, axis=0, keepdims=True) / CHANNELS
    inv = lax.rsqrt(
        jnp.sum(mixed * mixed, axis=0, keepdims=True) / CHANNELS - mean * mean + EPSILON
    )
    x_hat = (mixed - mean) * inv
    gain_full = across(gain[...].reshape(192, 128))
    normed = (x_hat * gain_full).astype(BF16)
    branch = jnp.zeros((192, 512), F32)
    dnormed = jnp.zeros((192, 512), F32)
    for j in range(4):
        preact = dot(in_t[j], normed, NN) + across(bias[j])
        square = preact * preact
        tangent = jnp.tanh(GELU_SCALE * (preact + GELU_CUBIC * square * preact))
        half = 0.5 * (1.0 + tangent)
        act = (preact * half).astype(BF16)
        slope = half + 0.5 * preact * (1.0 - tangent * tangent) * (
            GELU_SCALE * (1.0 + 3.0 * GELU_CUBIC * square)
        )
        branch = branch + dot(out_t[j], act, NN)
        pre_grad = (dot(w_out[j], dbranch, NN) * slope).astype(BF16)
        dnormed = dnormed + dot(w_in[j], pre_grad, NN)
        packet = (g0, g3, g2, g1)[j]
        for grad, lanes in (
            (dot(normed, pre_grad, NT), slice(0, 128)),
            (dot(act, dbranch, NT), slice(128, 256)),
        ):
            packet[96:288, lanes] = grad[:, 0:128].astype(BF16)
            packet[288:384, lanes] = pack_tail(grad[:, 128:192]).astype(BF16)
    xhat_grad = dnormed * gain_full
    first = jnp.sum(xhat_grad, axis=0, keepdims=True) / CHANNELS
    second = jnp.sum(xhat_grad * x_hat, axis=0, keepdims=True) / CHANNELS
    dmixed = (inv * (xhat_grad - first - x_hat * second)).astype(BF16)
    back_s[...] = dmixed.reshape(4, 48, 512)
    branch_s[...] = branch.astype(BF16).reshape(4, 48, 512)
    for j, g_ref in enumerate((g0, g1, g2, g3)):
        a = (mine + j) & 3
        for i in range(2):
            g_ref[48 * i : 48 * i + 48] = back_s[a, :, 256 * i : 256 * i + 256]
            g_ref[384 + 48 * i : 432 + 48 * i] = branch_s[a, :, 256 * i : 256 * i + 256]


def land_kernel(g0, g1, g2, g3, grad_ref):
    mine = lax.axis_index("chan")
    for j, ref in enumerate((g0, g1, g2, g3)):
        first = 2 * ((mine + 4 - j) & 3)
        for i in range(2):
            grad_ref[first + i] = ref[48 * i : 48 * i + 48]


BLOCKS = tuple(
    (64 * q + 32 * h, 64 * q + 32 * h + 32, q, 32 * h) for q in range(9) for h in range(2)
)


def pieces_kernel(
    g0, g1, g2, g3, grad_ref, pad_ref, fold, out_ref, pad, grad_t, sums, total, rows
):
    pad[...] = pad_ref[...].astype(F32)
    grad_t[...] = grad_ref[...].reshape(384, 256).astype(F32).T
    sums[...] = jnp.zeros((64, 384), F32)

    def lane_block(block, carry):
        lanes = pl.ds(pl.multiple_of(block * 128, 128), 128)
        lines = [grad_t[pl.ds(16 * i, 16), lanes] for i in range(16)]
        for b in range(7):
            acc = [jnp.zeros((16, 128), F32) for _ in range(7)]
            for r in range(22):
                line = pad[r, pl.ds(b, 16), lanes]
                for a in range(7):
                    i = r - a
                    if 0 <= i < 16:
                        acc[a] = acc[a] + line * lines[i]
            for a in range(7):
                sums[pl.ds(7 * a + b, 1), lanes] = jnp.sum(acc[a], axis=0, keepdims=True)
        return carry

    lax.fori_loop(0, 3, lane_block, 0)
    total[...] = sum(ref[96:384].astype(F32) for ref in (g0, g1, g2, g3))
    rows[...] = jnp.zeros((64, 16, 128), F32)
    for lo, hi, q, d in BLOCKS:
        rows[d : d + hi - lo, q, :] = total[lo % 288 : lo % 288 + hi - lo, pl.ds(128 * (lo // 288), 128)]
    rows[:, 9, :] = lax.dot_general(
        sums[...], fold[...], NN, precision=lax.Precision.HIGHEST, preferred_element_type=F32
    )
    out_ref[...] = rows[...].astype(BF16)


def edges_kernel(own_ref, par_ref, edge_ref):
    odd = lax.axis_index("core")

    @pl.when(odd == 1)
    def _():
        for t in range(8):
            edge_ref[t] = pack_pair(par_ref[t, :, 128:256], own_ref[t, :, 128:256], False)

    @pl.when(odd == 0)
    def _():
        for t in range(8):
            edge_ref[t] = pack_pair(own_ref[t, :, 0:128], par_ref[t, :, 0:128], True)


def total_kernel(factor, in_ref, out_ref):
    total = jnp.sum(in_ref[...].astype(F32), axis=0, keepdims=True) * factor
    out_ref[...] = jnp.broadcast_to(total, in_ref.shape).astype(out_ref.dtype)


def finish_kernel(in_ref, dw_ref, w1_ref, w2_ref, rows, flat):
    rows[...] = in_ref[...].astype(F32)
    for q in range(9):
        flat[64 * q : 64 * q + 64] = rows[:, q, :]
    for out, row in ((w1_ref, 0), (w2_ref, 288)):
        out[:, 0:128] = flat[row : row + 192]
        out[:, 128:192] = unpack_tail(flat[row + 192 : row + 288])
    dw_ref[...] = rows[:, 9, :].T[0:48, 0:49]


def unmix_kernel(
    adj, grad_ref, par_ref, near_ref, far_ref, cot_ref, taps, up_p, mid_p, down_p,
    owned_ref, scale_ref, r0, r1, r2, r3,
    out_ref, gin_ref,
    table, up_g, mid_g, down_g, pad, result,
):
    me = my_owner()
    odd = lax.axis_index("core")
    mine = lax.axis_index("chan")
    start = 16 * (me // 2) - 16
    table[pl.ds(16 + 8 * odd, 8)] = grad_ref[...]
    table[pl.ds(24 - 8 * odd, 8)] = par_ref[...]
    table[48] = jnp.zeros((48, 256), BF16)
    fill_edges(table, near_ref, far_ref, 32)
    for t in range(8):
        center = 16 + 8 * odd + t
        entries = [jnp.where(adj[t, k] < 512, adj[t, k] - start, 48) for k in range(8)]
        gather_tile(table, up_g, mid_g, down_g, t, center, entries)
    build_padded(pad, up_g, mid_g, down_g, up_p, mid_p, down_p)
    convolve(pad, taps, result, True)
    back = result[...].T.reshape(8, 48, 256)
    gin_ref[...] = (cot_ref[...].astype(F32) + back).astype(BF16)
    scale = column(scale_ref[...])
    for j, ref in enumerate((r0, r1, r2, r3)):
        first = 2 * ((mine + 4 - j) & 3)
        for i in range(2):
            out_ref[first + i] = (
                owned_ref[first + i].astype(F32) + scale * ref[384 + 48 * i : 432 + 48 * i].astype(F32)
            ).astype(BF16)


def call(kernel, shapes, scratch=(), smem=0, n_in=0, name=None, near=()):
    vmem = pl.BlockSpec(memory_space=pltpu.VMEM)
    scalar = pl.BlockSpec(memory_space=pltpu.SMEM)
    many = isinstance(shapes, (list, tuple))
    inner = pl.pallas_call(
        kernel,
        out_shape=shapes,
        in_specs=[scalar] * smem + [vmem] * (n_in - smem),
        out_specs=[vmem] * len(shapes) if many else vmem,
        scratch_shapes=list(scratch),
        compiler_params=pltpu.CompilerParams(vmem_limit_bytes=24 << 20),
        name=name,
    )

    def run(*args):
        held = [
            pltpu.with_memory_space_constraint(a, pltpu.VMEM) if i in near else a
            for i, a in enumerate(args)
        ]
        return inner(*held)

    return run


def shape(*dims, dtype=BF16):
    return jax.ShapeDtypeStruct(dims, dtype)


def held(*dims, dtype=BF16):
    return pltpu.VMEM(dims, dtype)


def along_chan(values):
    got = [values[0]]
    for j in range(1, 4):
        got.append(lax.ppermute(values[j], "chan", [(i, (i + j) % 4) for i in range(4)]))
    return got


def body(
    x_scan, slot_owner, adjacency, cotangent, dw_weight, ln_gain, w_in, b_in, w_out, layer_scale
):
    devices = lax.axis_size("chip") * 2
    up_p, mid_p, down_p = (jnp.asarray(v) for v in placement_tables())
    fold_map = (np.arange(384)[:, None] % 48 == np.arange(128)[None, :]).astype(np.float32)
    fold = jnp.asarray(fold_map)
    spread_map = jnp.asarray(np.ascontiguousarray(fold_map.T))
    scale_row = layer_scale.reshape(1, 48)
    owners = ("chip", "core")

    def after(value, *first):
        return lax.optimization_barrier((value, first))[0]

    def partner(value):
        return lax.ppermute(value, "core", [(0, 1), (1, 0)])

    def next_chip(value):
        pairs = [(i, i + 1 if i & 1 else i - 1) for i in range(devices)]
        return lax.ppermute(value, owners, [p for p in pairs if 0 <= p[1] < devices])

    tile_chunk = held(2, 48, 256)
    par_x = partner(x_scan)
    par_slots = partner(slot_owner)
    strips = call(strips_kernel, held(8, 48, 128), n_in=1, name="strips")(x_scan)
    near = next_chip(strips)
    far = partner(near)
    *sends, taps = call(
        sends_kernel,
        [held(400, 256)] * 4 + [held(56, 384, dtype=F32)],
        scratch=[pltpu.VMEM((16, 256), F32), pltpu.VMEM((128, 128), F32)],
        n_in=8,
        name="sends",
    )(
        cotangent, after(scale_row, strips, par_x, par_slots), w_in, w_out,
        b_in.reshape(1, 192), ln_gain.reshape(1, 48), dw_weight, spread_map,
    )
    all_sends = along_chan(after(sends, near))

    grid_scratch = lambda entries: [
        pltpu.VMEM((entries, 48, 256), BF16),
        pltpu.VMEM((384, 384), BF16),
        pltpu.VMEM((384, 768), BF16),
        pltpu.VMEM((384, 384), BF16),
        pltpu.VMEM((22, WIDE, 384), F32),
        pltpu.VMEM((256, 384), F32),
    ]
    mix = call(
        mix_kernel,
        [shape(8, 48, 256), shape(22, WIDE, 384)] + [tile_chunk] * 4,
        scratch=[pltpu.SMEM((8,), jnp.int32)] + grid_scratch(65) + [pltpu.VMEM((8, 48, 256), BF16)],
        smem=3,
        n_in=11,
        name="mix",
        near=(4, 5, 6, 7),
    )
    owned, padded, *mixed = mix(
        slot_owner, par_slots, adjacency, x_scan, par_x, near, far, taps, up_p, mid_p, down_p
    )
    all_mixed = along_chan(mixed)

    square = held(4, 192, 192)
    turn = call(
        turn_kernel,
        [square] * 4
        + [held(4, 192, 128, dtype=F32), held(4, 48, 128, dtype=F32), held(4, 48, 512)],
        n_in=4,
        name="turn",
        near=(0, 1, 2, 3),
    )
    turned = turn(*after(all_sends, mixed[0]))

    results = call(
        mlp_kernel,
        [held(480, 256)] * 4,
        scratch=[pltpu.VMEM((4, 48, 512), BF16)] * 3,
        n_in=11,
        name="mlp",
        near=range(11),
    )(*all_mixed, *turned)
    all_back = along_chan(results)
    grads = call(land_kernel, held(8, 48, 256), n_in=4, name="land", near=range(4))(*all_back)
    par_grads = partner(grads)
    pieces = call(
        pieces_kernel,
        held(64, 16, 128),
        scratch=[
            pltpu.VMEM((22, WIDE, 384), F32),
            pltpu.VMEM((256, 384), F32),
            pltpu.VMEM((64, 384), F32),
            pltpu.VMEM((288, 256), F32),
            pltpu.VMEM((64, 16, 128), F32),
        ],
        n_in=7,
        name="pieces",
        near=range(5),
    )(*all_back, grads, padded, fold)

    edges = call(edges_kernel, held(8, 48, 128), n_in=2, name="edges", near=(0, 1))(
        after(grads, pieces), par_grads
    )
    near_grads = next_chip(edges)
    arrived = lax.all_to_all(after(pieces, edges), owners, 0, 0, tiled=True)

    factor = 1.0 / math.sqrt(adjacency.shape[0] * devices * PIX)
    arrived, near_grads = lax.optimization_barrier((arrived, near_grads))
    far_grads = partner(near_grads)
    totals = call(
        functools.partial(total_kernel, factor), held(64, 16, 128), n_in=1, name="totals", near=(0,)
    )(arrived)
    spread = lax.all_to_all(totals, owners, 0, 0, tiled=True)

    unmix = call(
        unmix_kernel,
        [shape(8, 48, 256), shape(8, 48, 256)],
        scratch=grid_scratch(49),
        smem=1,
        n_in=16,
        name="unmix",
        near=(1, 2, 3, 4, 12, 13, 14, 15),
    )
    output, grad_in = unmix(
        adjacency, grads, par_grads, near_grads, far_grads,
        cotangent, taps, up_p, mid_p, down_p, owned, after(scale_row, totals), *all_back
    )
    grad_dw, grad_w1, grad_w2 = call(
        finish_kernel,
        [shape(48, 49, dtype=F32), shape(192, 192, dtype=F32), shape(192, 192, dtype=F32)],
        scratch=[pltpu.VMEM((64, 16, 128), F32), pltpu.VMEM((576, 128), F32)],
        n_in=1,
        name="finish",
        near=(0,),
    )(spread)
    return (output, grad_in, grad_dw, grad_w1, grad_w2)


def solution(mesh):
    chips, chan = mesh.devices.shape[0] // 2, mesh.devices.shape[1]
    parts = Mesh(mesh.devices.reshape(chips, 2, chan), ("chip", "core", "chan"))
    tiles = ("chip", "core")
    in_specs = (
        P(tiles, "chan", None),
        P(tiles),
        P(tiles, None),
        P(tiles, "chan", None),
        P("chan", None),
        P("chan"),
        P(None, "chan"),
        P("chan"),
        P("chan", None),
        P("chan"),
    )
    out_specs = (
        P(tiles, "chan", None),
        P(tiles, "chan", None),
        P("chan", None),
        P(None, "chan"),
        P("chan", None),
    )
    return jax.shard_map(body, mesh=parts, in_specs=in_specs, out_specs=out_specs, check_vma=False)
```

```python
import functools
import math

import jax
import jax.numpy as jnp
import numpy as np
from jax import lax
from jax.experimental import pallas as pl
from jax.experimental.pallas import tpu as pltpu
from jax.sharding import Mesh
from jax.sharding import PartitionSpec as P

CHANNELS = 192
SIDE = 16
PIX = 256
WIDE = 24
EPSILON = 1e-06
GELU_SCALE = 0.7978845608
GELU_CUBIC = 0.044715

F32 = jnp.float32
BF16 = jnp.bfloat16
NT = (((1,), (1,)), ((), ()))
NN = (((1,), (0,)), ((), ()))


def dot(a, b, dims):
    return lax.dot_general(a, b, dims, preferred_element_type=F32)


def placement_tables():
    up = np.zeros((72, 384), np.float32)
    mid = np.zeros((384, 768), np.float32)
    down = np.zeros((72, 384), np.float32)
    for j in range(22):
        if j < 3:
            side, col = 0, 13 + j
        elif j < 19:
            side, col = 1, j - 3
        else:
            side, col = 2, j - 19
        for i in range(3):
            up[i * WIDE + j, 128 * side + 16 * (13 + i) + col - 128] = 1
            down[i * WIDE + j, 128 * side + 16 * i + col] = 1
        for i in range(16):
            block = (1, 0, 2)[side]
            mid[i * WIDE + j, 256 * block + 16 * i + col] = 1
    return up.astype(jnp.bfloat16), mid.astype(jnp.bfloat16), down.astype(jnp.bfloat16)


def column(row):
    n = row.shape[1]
    same = lax.broadcasted_iota(jnp.int32, (n, n), 0) == lax.broadcasted_iota(jnp.int32, (n, n), 1)
    return jnp.sum(jnp.where(same, jnp.broadcast_to(row, (n, n)), 0.0), axis=1, keepdims=True)


def eye(n):
    same = lax.broadcasted_iota(jnp.int32, (n, n), 0) == lax.broadcasted_iota(jnp.int32, (n, n), 1)
    return same.astype(F32).astype(BF16)


def swap_halves(value):
    return pltpu.roll(value.astype(F32), 64, 1)


def low_lanes(shape):
    return lax.broadcasted_iota(jnp.int32, shape, 1) < 64


def pack_pair(natural, other, natural_low):
    shape = natural.shape
    keep = low_lanes(shape) if natural_low else jnp.logical_not(low_lanes(shape))
    return jnp.where(keep, natural.astype(F32), swap_halves(other)).astype(BF16)


def my_owner():
    return 2 * lax.axis_index("chip") + lax.axis_index("core")


def strips_kernel(x_ref, strips_ref, half, sem):
    odd = lax.axis_index("core")
    copy = pltpu.make_async_copy(
        x_ref.at[:, :, pl.ds(pl.multiple_of(128 * odd, 128), 128)], half, sem
    )
    copy.start()
    copy.wait()

    @pl.when(odd == 1)
    def _():
        for s in range(8):
            strips_ref[s] = pack_pair(half[s], half[s + 8], False)

    @pl.when(odd == 0)
    def _():
        for s in range(8):
            strips_ref[s] = pack_pair(half[s], half[s + 8], True)


def pack_tail(value):
    return jnp.concatenate([value[0:96], value[96:192]], axis=1)


def unpack_tail(value):
    return jnp.concatenate([value[:, 0:64], value[:, 64:128]], axis=0)


def sends_kernel(cot_ref, scale_ref, in_ref, w_out_ref, b_ref, gain_ref, dw_ref, spread, *rest):
    outs, taps_ref, small, turned = rest[0:4], rest[4], rest[5], rest[6]
    turned[...] = jnp.zeros((128, 128), F32)
    turned[0:48, 0:49] = dw_ref[...]
    taps_ref[...] = lax.dot_general(
        turned[...].T[0:56], spread[...], NN,
        precision=lax.Precision.HIGHEST, preferred_element_type=F32,
    )
    mine = lax.axis_index("chan")
    scale = column(scale_ref[...])
    small[...] = jnp.zeros((16, 256), F32)
    small[0:1, 0:192] = b_ref[...].astype(F32)
    small[1:2, 0:48] = gain_ref[...].astype(F32)
    tails = []
    for ref in (in_ref, w_out_ref):
        tails.append(pack_tail(ref[:, 128:192].astype(F32)).astype(BF16))
    for j, out in enumerate(outs):
        first = 2 * ((mine + j) & 3)
        for i in range(2):
            out[48 * i : 48 * i + 48] = (cot_ref[first + i].astype(F32) * scale).astype(BF16)
        out[96:288, 0:128] = in_ref[:, 0:128]
        out[96:288, 128:256] = w_out_ref[:, 0:128]
        out[288:384, 0:128] = tails[0]
        out[288:384, 128:256] = tails[1]
        out[384:400] = small[...].astype(BF16)


def gather_tile(table, up_g, mid_g, down_g, t, center, entries):
    rows = pl.ds(48 * t, 48)
    mid_g[rows, 0:256] = table[center]
    mid_g[rows, 256:512] = table[entries[3]]
    mid_g[rows, 512:768] = table[entries[4]]
    for k in range(3):
        up_g[rows, 128 * k : 128 * k + 128] = table[entries[k], :, 128:256]
        down_g[rows, 128 * k : 128 * k + 128] = table[entries[5 + k], :, 0:128]


def build_padded(pad, up_g, mid_g, down_g, up_p, mid_p, down_p):
    pad[0:3] = dot(up_p[...], up_g[...], NT).reshape(3, WIDE, 384)
    pad[3:19] = dot(mid_p[...], mid_g[...], NT).reshape(16, WIDE, 384)
    pad[19:22] = dot(down_p[...], down_g[...], NT).reshape(3, WIDE, 384)


def convolve(pad, taps, result, flip):
    def lane_block(block, carry):
        lanes = pl.ds(pl.multiple_of(block * 128, 128), 128)
        acc = [jnp.zeros((16, 128), F32) for _ in range(16)]
        for b in range(7):
            weights = []
            for a in range(7):
                tap = 7 * a + b
                weights.append(taps[pl.ds(48 - tap if flip else tap, 1), lanes])
            for r in range(22):
                line = pad[r, pl.ds(b, 16), lanes]
                for a in range(7):
                    i = r - a
                    if 0 <= i < 16:
                        acc[i] = acc[i] + line * weights[a]
        for i in range(16):
            result[pl.ds(16 * i, 16), lanes] = acc[i]
        return carry

    lax.fori_loop(0, 3, lane_block, 0)


def fill_edges(table, near_ref, far_ref, below):
    odd = lax.axis_index("core")

    def fill(upper, lower):
        for s in range(8):
            up = upper[s]
            table[s, :, 128:256] = up
            table[s + 8, :, 128:256] = swap_halves(up).astype(BF16)
            down = lower[s]
            table[below + s, :, 0:128] = down
            table[below + 8 + s, :, 0:128] = swap_halves(down).astype(BF16)

    @pl.when(odd == 0)
    def _():
        fill(near_ref, far_ref)

    @pl.when(odd == 1)
    def _():
        fill(far_ref, near_ref)


OFFSETS = (-17, -16, -15, -1, 1, 15, 16, 17)


def mix_kernel(
    own_slots, par_slots, adj, x_ref, par_ref, near_ref, far_ref, taps, up_p, mid_p, down_p,
    owned_ref, pad_out, m0, m1, m2, m3,
    place, table, up_g, mid_g, down_g, pad, result, flat,
):
    me = my_owner()
    odd = lax.axis_index("core")
    mine = lax.axis_index("chan")
    base = 8 * me
    for t in range(8):
        place[t] = 0
    for s in range(16):
        for slots, row in ((own_slots, odd), (par_slots, 1 - odd)):
            t = slots[s] - base

            @pl.when((t >= 0) & (t < 8))
            def _():
                place[t] = 16 + 16 * row + s

    table[pl.ds(16 + 16 * odd, 16)] = x_ref[...]
    table[pl.ds(32 - 16 * odd, 16)] = par_ref[...]
    table[64] = jnp.zeros((48, 256), BF16)

    fill_edges(table, near_ref, far_ref, 48)
    for t in range(8):
        center = place[t]
        entries = [jnp.where(adj[t, k] < 512, center + OFFSETS[k], 64) for k in range(8)]
        gather_tile(table, up_g, mid_g, down_g, t, center, entries)
    owned_ref[...] = mid_g[:, 0:256].reshape(8, 48, 256)
    build_padded(pad, up_g, mid_g, down_g, up_p, mid_p, down_p)
    pad_out[...] = pad[...].astype(BF16)
    convolve(pad, taps, result, False)
    flat[...] = result[...].T.astype(BF16).reshape(8, 48, 256)
    for j, out in enumerate((m0, m1, m2, m3)):
        first = 2 * ((mine + j) & 3)
        out[0] = flat[first]
        out[1] = flat[first + 1]


def turn_kernel(p0, p1, p2, p3, w_in, w_out, in_t, out_t, bias, gain, dbranch):
    mine = lax.axis_index("chan")
    unit = eye(192)
    for j, ref in enumerate((p0, p1, p2, p3)):
        a = (mine + 4 - j) & 3
        for i in range(2):
            dbranch[a, :, 256 * i : 256 * i + 256] = ref[48 * i : 48 * i + 48]
        for full, turned, lanes in ((w_in, in_t, 0), (w_out, out_t, 128)):
            tail = ref[288:384, lanes : lanes + 128].astype(F32)
            whole = jnp.concatenate(
                [
                    ref[96:288, lanes : lanes + 128].astype(F32),
                    unpack_tail(tail),
                ],
                axis=1,
            ).astype(BF16)
            full[j] = whole
            turned[j] = dot(unit, whole, NT).astype(BF16)
        cols = dot(unit, ref[384:400, 0:192], NT)
        bias[j] = jnp.broadcast_to(cols[:, 0:1], (192, 128))
        gain[a] = jnp.broadcast_to(cols[0:48, 1:2], (48, 128))


def across(col_block):
    return jnp.concatenate([col_block] * 4, axis=1)


def mlp_kernel(
    m0, m1, m2, m3, w_in, w_out, in_t, out_t, bias, gain, db_ref,
    g0, g1, g2, g3, keep_ref, give_ref, mixed_s, back_s, branch_s, halves,
):
    mine = lax.axis_index("chan")
    for j, m_ref in enumerate((m0, m1, m2, m3)):
        a = (mine + 4 - j) & 3
        for i in range(2):
            mixed_s[a, :, 256 * i : 256 * i + 256] = m_ref[i]
    mixed = mixed_s[...].reshape(192, 512).astype(F32)
    dbranch = db_ref[...].reshape(192, 512)
    mean = jnp.sum(mixed, axis=0, keepdims=True) / CHANNELS
    inv = lax.rsqrt(
        jnp.sum(mixed * mixed, axis=0, keepdims=True) / CHANNELS - mean * mean + EPSILON
    )
    x_hat = (mixed - mean) * inv
    gain_full = across(gain[...].reshape(192, 128))
    normed = (x_hat * gain_full).astype(BF16)
    branch = jnp.zeros((192, 512), F32)
    dnormed = jnp.zeros((192, 512), F32)
    for j in range(4):
        preact = dot(in_t[j], normed, NN) + across(bias[j])
        square = preact * preact
        tangent = jnp.tanh(GELU_SCALE * (preact + GELU_CUBIC * square * preact))
        half = 0.5 * (1.0 + tangent)
        act = (preact * half).astype(BF16)
        slope = half + 0.5 * preact * (1.0 - tangent * tangent) * (
            GELU_SCALE * (1.0 + 3.0 * GELU_CUBIC * square)
        )
        branch = branch + dot(out_t[j], act, NN)
        pre_grad = (dot(w_out[j], dbranch, NN) * slope).astype(BF16)
        dnormed = dnormed + dot(w_in[j], pre_grad, NN)
        for side, grad in enumerate((dot(normed, pre_grad, NT), dot(act, dbranch, NT))):
            halves[side, j, 0:192] = grad[:, 0:128].astype(BF16)
            halves[side, j, 192:288] = pack_tail(grad[:, 128:192]).astype(BF16)
    core = lax.axis_index("core")
    keep_ref[...] = halves[core]
    give_ref[...] = halves[1 - core]
    xhat_grad = dnormed * gain_full
    first = jnp.sum(xhat_grad, axis=0, keepdims=True) / CHANNELS
    second = jnp.sum(xhat_grad * x_hat, axis=0, keepdims=True) / CHANNELS
    dmixed = (inv * (xhat_grad - first - x_hat * second)).astype(BF16)
    back_s[...] = dmixed.reshape(4, 48, 512)
    branch_s[...] = branch.astype(BF16).reshape(4, 48, 512)
    for j, g_ref in enumerate((g0, g1, g2, g3)):
        a = (mine + j) & 3
        for i in range(2):
            g_ref[48 * i : 48 * i + 48] = back_s[a, :, 256 * i : 256 * i + 256]
            g_ref[96 + 48 * i : 144 + 48 * i] = branch_s[a, :, 256 * i : 256 * i + 256]


def land_kernel(g0, g1, g2, g3, grad_ref):
    mine = lax.axis_index("chan")
    for j, ref in enumerate((g0, g1, g2, g3)):
        first = 2 * ((mine + 4 - j) & 3)
        for i in range(2):
            grad_ref[first + i] = ref[48 * i : 48 * i + 48]


def merge_kernel(t0, t1, t2, t3, keep_ref, got_ref, g0, g1, g2, g3):
    for j, (tiles, out) in enumerate(zip((t0, t1, t2, t3), (g0, g1, g2, g3))):
        below = (4 - j) & 3
        both = (keep_ref[below].astype(F32) + got_ref[below].astype(F32)).astype(BF16)
        out[0:192] = tiles[...]
        out[192:336, 0:128] = both[0:144]
        out[192:336, 128:256] = both[144:288]


def taps_kernel(grad_ref, pad_ref, fold, out_ref, pad, grad_t, sums):
    pad[...] = pad_ref[...].astype(F32)
    grad_t[...] = grad_ref[...].reshape(384, 256).astype(F32).T
    sums[...] = jnp.zeros((64, 384), F32)

    def lane_block(block, carry):
        lanes = pl.ds(pl.multiple_of(block * 128, 128), 128)
        lines = [grad_t[pl.ds(16 * i, 16), lanes] for i in range(16)]
        for b in range(7):
            acc = [jnp.zeros((16, 128), F32) for _ in range(7)]
            for r in range(22):
                line = pad[r, pl.ds(b, 16), lanes]
                for a in range(7):
                    i = r - a
                    if 0 <= i < 16:
                        acc[a] = acc[a] + line * lines[i]
            for a in range(7):
                sums[pl.ds(7 * a + b, 1), lanes] = jnp.sum(acc[a], axis=0, keepdims=True)
        return carry

    lax.fori_loop(0, 3, lane_block, 0)
    out_ref[...] = lax.dot_general(
        sums[...], fold[...], NN, precision=lax.Precision.HIGHEST, preferred_element_type=F32
    )


def pieces_kernel(g0, g1, g2, g3, taps_ref, out_ref, total, rows):
    for half in range(2):
        lanes = slice(128 * half, 128 * half + 128)
        total[144 * half : 144 * half + 144] = sum(
            ref[192:336, lanes].astype(F32) for ref in (g0, g1, g2, g3)
        )
    total[288:352] = taps_ref[...]
    rows[...] = jnp.zeros((32, 16, 128), F32)
    for q in range(11):
        rows[:, q, :] = total[32 * q : 32 * q + 32]
    out_ref[...] = rows[...].astype(BF16)


def edges_kernel(own_ref, par_ref, edge_ref):
    odd = lax.axis_index("core")

    @pl.when(odd == 1)
    def _():
        for t in range(8):
            edge_ref[t] = pack_pair(par_ref[t, :, 128:256], own_ref[t, :, 128:256], False)

    @pl.when(odd == 0)
    def _():
        for t in range(8):
            edge_ref[t] = pack_pair(own_ref[t, :, 0:128], par_ref[t, :, 0:128], True)


def total_kernel(factor, in_ref, out_ref):
    total = jnp.sum(in_ref[...].astype(F32), axis=0, keepdims=True) * factor
    out_ref[...] = jnp.broadcast_to(total, in_ref.shape).astype(out_ref.dtype)


def finish_kernel(in_ref, other_ref, dw_ref, w1_ref, w2_ref, rows, flat):
    core = lax.axis_index("core")
    for ref, side in ((in_ref, core), (other_ref, 1 - core)):
        rows[...] = ref[...].astype(F32)
        for q in range(11):
            flat[side, 32 * q : 32 * q + 32] = rows[:, q, :]
    for out, side in ((w1_ref, 0), (w2_ref, 1)):
        out[:, 0:128] = flat[side, 0:192]
        out[:, 128:192] = unpack_tail(flat[side, 192:288])
    dw = flat[0, 288:352] + flat[1, 288:352]
    dw_ref[...] = dw.T[0:48, 0:49]


def unmix_kernel(
    adj, grad_ref, par_ref, near_ref, far_ref, cot_ref, taps, up_p, mid_p, down_p,
    owned_ref, scale_ref, r0, r1, r2, r3,
    out_ref, gin_ref,
    table, up_g, mid_g, down_g, pad, result,
):
    me = my_owner()
    odd = lax.axis_index("core")
    mine = lax.axis_index("chan")
    start = 16 * (me // 2) - 16
    table[pl.ds(16 + 8 * odd, 8)] = grad_ref[...]
    table[pl.ds(24 - 8 * odd, 8)] = par_ref[...]
    table[48] = jnp.zeros((48, 256), BF16)
    fill_edges(table, near_ref, far_ref, 32)
    for t in range(8):
        center = 16 + 8 * odd + t
        entries = [jnp.where(adj[t, k] < 512, adj[t, k] - start, 48) for k in range(8)]
        gather_tile(table, up_g, mid_g, down_g, t, center, entries)
    build_padded(pad, up_g, mid_g, down_g, up_p, mid_p, down_p)
    convolve(pad, taps, result, True)
    back = result[...].T.reshape(8, 48, 256)
    gin_ref[...] = (cot_ref[...].astype(F32) + back).astype(BF16)
    scale = column(scale_ref[...])
    for j, ref in enumerate((r0, r1, r2, r3)):
        first = 2 * ((mine + 4 - j) & 3)
        for i in range(2):
            out_ref[first + i] = (
                owned_ref[first + i].astype(F32) + scale * ref[96 + 48 * i : 144 + 48 * i].astype(F32)
            ).astype(BF16)


def fetching(kernel, fetch, n_in):
    def outer(*refs):
        inputs, rest = list(refs[:n_in]), refs[n_in:]
        rest, local, sems = rest[: -len(fetch) - 1], rest[-len(fetch) - 1 : -1], rest[-1]
        copies = [
            pltpu.make_async_copy(inputs[i], buf, sems.at[n])
            for n, (i, buf) in enumerate(zip(fetch, local))
        ]
        for copy in copies:
            copy.start()
        for copy in copies:
            copy.wait()
        for i, buf in zip(fetch, local):
            inputs[i] = buf
        kernel(*inputs, *rest)

    return outer


def call(kernel, shapes, scratch=(), smem=0, n_in=0, name=None, near=(), fetch=()):
    vmem = pl.BlockSpec(memory_space=pltpu.VMEM)
    scalar = pl.BlockSpec(memory_space=pltpu.SMEM)
    many = isinstance(shapes, (list, tuple))

    def run(*args):
        specs = [
            pl.BlockSpec(memory_space=pltpu.HBM) if i in fetch else scalar if i < smem else vmem
            for i in range(n_in)
        ]
        scratches = list(scratch)
        if fetch:
            scratches += [pltpu.VMEM(args[i].shape, args[i].dtype) for i in fetch]
            scratches.append(pltpu.SemaphoreType.DMA((len(fetch),)))
        inner = pl.pallas_call(
            fetching(kernel, fetch, n_in) if fetch else kernel,
            out_shape=shapes,
            in_specs=specs,
            out_specs=[vmem] * len(shapes) if many else vmem,
            scratch_shapes=scratches,
            compiler_params=pltpu.CompilerParams(vmem_limit_bytes=24 << 20),
            name=name,
        )
        spaces = {**{i: pltpu.VMEM for i in near}, **{i: pltpu.HBM for i in fetch}}
        return inner(
            *(
                pltpu.with_memory_space_constraint(a, spaces[i]) if i in spaces else a
                for i, a in enumerate(args)
            )
        )

    return run


def shape(*dims, dtype=BF16):
    return jax.ShapeDtypeStruct(dims, dtype)


def held(*dims, dtype=BF16):
    return pltpu.VMEM(dims, dtype)


def along_chan(values):
    got = [values[0]]
    for j in range(1, 4):
        got.append(lax.ppermute(values[j], "chan", [(i, (i + j) % 4) for i in range(4)]))
    return got


def body(
    x_scan, slot_owner, adjacency, cotangent, dw_weight, ln_gain, w_in, b_in, w_out, layer_scale
):
    devices = lax.axis_size("chip") * 2
    up_p, mid_p, down_p = (jnp.asarray(v) for v in placement_tables())
    fold_map = (np.arange(384)[:, None] % 48 == np.arange(128)[None, :]).astype(np.float32)
    fold = jnp.asarray(fold_map)
    spread_map = jnp.asarray(np.ascontiguousarray(fold_map.T))
    scale_row = layer_scale.reshape(1, 48)
    owners = ("chip", "core")

    def after(value, *first):
        return lax.optimization_barrier((value, first))[0]

    def partner(value):
        return lax.ppermute(value, "core", [(0, 1), (1, 0)])

    def next_chip(value):
        pairs = [(i, i + 1 if i & 1 else i - 1) for i in range(devices)]
        return lax.ppermute(value, owners, [p for p in pairs if 0 <= p[1] < devices])

    tile_chunk = held(2, 48, 256)
    par_x = partner(x_scan)
    par_slots = partner(slot_owner)
    strips = pl.pallas_call(
        strips_kernel,
        out_shape=held(8, 48, 128),
        in_specs=[pl.BlockSpec(memory_space=pltpu.HBM)],
        out_specs=pl.BlockSpec(memory_space=pltpu.VMEM),
        scratch_shapes=[pltpu.VMEM((16, 48, 128), BF16), pltpu.SemaphoreType.DMA(())],
        name="strips",
    )(pltpu.with_memory_space_constraint(x_scan, pltpu.HBM))
    near = next_chip(strips)
    far = partner(near)
    *sends, taps = call(
        sends_kernel,
        [held(400, 256)] * 4 + [held(56, 384, dtype=F32)],
        scratch=[pltpu.VMEM((16, 256), F32), pltpu.VMEM((128, 128), F32)],
        n_in=8,
        name="sends",
        fetch=range(8),
    )(
        cotangent, after(scale_row, strips, par_x, par_slots), w_in, w_out,
        b_in.reshape(1, 192), ln_gain.reshape(1, 48), dw_weight, spread_map,
    )
    all_sends = along_chan(after(sends, near))

    grid_scratch = lambda entries: [
        pltpu.VMEM((entries, 48, 256), BF16),
        pltpu.VMEM((384, 384), BF16),
        pltpu.VMEM((384, 768), BF16),
        pltpu.VMEM((384, 384), BF16),
        pltpu.VMEM((22, WIDE, 384), F32),
        pltpu.VMEM((256, 384), F32),
    ]
    mix = call(
        mix_kernel,
        [shape(8, 48, 256), shape(22, WIDE, 384)] + [tile_chunk] * 4,
        scratch=[pltpu.SMEM((8,), jnp.int32)] + grid_scratch(65) + [pltpu.VMEM((8, 48, 256), BF16)],
        smem=3,
        n_in=11,
        name="mix",
        near=(4, 5, 6, 7),
    )
    owned, padded, *mixed = mix(
        slot_owner, par_slots, adjacency, x_scan, par_x, near, far, taps, up_p, mid_p, down_p
    )
    all_mixed = along_chan(mixed)

    square = held(4, 192, 192)
    turn = call(
        turn_kernel,
        [square] * 4
        + [held(4, 192, 128, dtype=F32), held(4, 48, 128, dtype=F32), held(4, 48, 512)],
        n_in=4,
        name="turn",
        near=(0, 1, 2, 3),
    )
    turned = turn(*after(all_sends, mixed[0]))

    *packets, keep, give = call(
        mlp_kernel,
        [held(192, 256)] * 4 + [held(4, 288, 128)] * 2,
        scratch=[pltpu.VMEM((4, 48, 512), BF16)] * 3 + [pltpu.VMEM((2, 4, 288, 128), BF16)],
        n_in=11,
        name="mlp",
        near=range(11),
    )(*all_mixed, *turned)
    packets = call(
        merge_kernel, [held(336, 256)] * 4, n_in=6, name="merge", near=range(6)
    )(*packets, keep, partner(give))
    all_back = along_chan(packets)
    grads = call(land_kernel, held(8, 48, 256), n_in=4, name="land", near=range(4))(*all_back)
    par_grads = partner(grads)
    tap_sums = call(
        taps_kernel,
        held(64, 128, dtype=F32),
        scratch=[
            pltpu.VMEM((22, WIDE, 384), F32),
            pltpu.VMEM((256, 384), F32),
            pltpu.VMEM((64, 384), F32),
        ],
        n_in=3,
        name="tap_sums",
        near=(0,),
    )(grads, padded, fold)
    edges = call(edges_kernel, held(8, 48, 128), n_in=2, name="edges", near=(0, 1))(
        after(grads, tap_sums), par_grads
    )
    near_grads = next_chip(edges)
    pieces = call(
        pieces_kernel,
        held(32, 16, 128),
        scratch=[pltpu.VMEM((352, 128), F32), pltpu.VMEM((32, 16, 128), F32)],
        n_in=5,
        name="pieces",
        near=range(5),
    )(*all_back, tap_sums)
    arrived = lax.all_to_all(after(pieces, edges), "chip", 0, 0, tiled=True)
    arrived, near_grads = lax.optimization_barrier((arrived, near_grads))

    factor = 1.0 / math.sqrt(adjacency.shape[0] * devices * PIX)
    far_grads = partner(near_grads)
    totals = call(
        functools.partial(total_kernel, factor), held(32, 16, 128), n_in=1, name="totals", near=(0,)
    )(arrived)
    spread = lax.all_to_all(totals, "chip", 0, 0, tiled=True)

    unmix = call(
        unmix_kernel,
        [shape(8, 48, 256), shape(8, 48, 256)],
        scratch=grid_scratch(49),
        smem=1,
        n_in=16,
        name="unmix",
        near=(1, 2, 3, 4, 12, 13, 14, 15),
    )
    output, grad_in = unmix(
        adjacency, grads, par_grads, near_grads, far_grads,
        cotangent, taps, up_p, mid_p, down_p, owned, after(scale_row, totals), *all_back
    )
    spread = after(spread, output)
    grad_dw, grad_w1, grad_w2 = call(
        finish_kernel,
        [shape(48, 49, dtype=F32), shape(192, 192, dtype=F32), shape(192, 192, dtype=F32)],
        scratch=[pltpu.VMEM((32, 16, 128), F32), pltpu.VMEM((2, 352, 128), F32)],
        n_in=2,
        name="finish",
        near=(0, 1),
    )(spread, partner(spread))
    return (output, grad_in, grad_dw, grad_w1, grad_w2)


def solution(mesh):
    chips, chan = mesh.devices.shape[0] // 2, mesh.devices.shape[1]
    parts = Mesh(mesh.devices.reshape(chips, 2, chan), ("chip", "core", "chan"))
    tiles = ("chip", "core")
    in_specs = (
        P(tiles, "chan", None),
        P(tiles),
        P(tiles, None),
        P(tiles, "chan", None),
        P("chan", None),
        P("chan"),
        P(None, "chan"),
        P("chan"),
        P("chan", None),
        P("chan"),
    )
    out_specs = (
        P(tiles, "chan", None),
        P(tiles, "chan", None),
        P("chan", None),
        P(None, "chan"),
        P("chan", None),
    )
    return jax.shard_map(body, mesh=parts, in_specs=in_specs, out_specs=out_specs, check_vma=False)
```

```python
import functools
import math

import jax
import jax.numpy as jnp
import numpy as np
from jax import lax
from jax.experimental import pallas as pl
from jax.experimental.pallas import tpu as pltpu
from jax.sharding import Mesh
from jax.sharding import PartitionSpec as P

CHANNELS = 192
SIDE = 16
PIX = 256
WIDE = 24
EPSILON = 1e-06
GELU_SCALE = 0.7978845608
GELU_CUBIC = 0.044715

F32 = jnp.float32
BF16 = jnp.bfloat16
NT = (((1,), (1,)), ((), ()))
NN = (((1,), (0,)), ((), ()))


def dot(a, b, dims):
    return lax.dot_general(a, b, dims, preferred_element_type=F32)


def placement_tables():
    up = np.zeros((72, 384), np.float32)
    mid = np.zeros((384, 768), np.float32)
    down = np.zeros((72, 384), np.float32)
    for j in range(22):
        if j < 3:
            side, col = 0, 13 + j
        elif j < 19:
            side, col = 1, j - 3
        else:
            side, col = 2, j - 19
        for i in range(3):
            up[i * WIDE + j, 128 * side + 16 * (13 + i) + col - 128] = 1
            down[i * WIDE + j, 128 * side + 16 * i + col] = 1
        for i in range(16):
            block = (1, 0, 2)[side]
            mid[i * WIDE + j, 256 * block + 16 * i + col] = 1
    return up.astype(jnp.bfloat16), mid.astype(jnp.bfloat16), down.astype(jnp.bfloat16)


def column(row):
    n = row.shape[1]
    same = lax.broadcasted_iota(jnp.int32, (n, n), 0) == lax.broadcasted_iota(jnp.int32, (n, n), 1)
    return jnp.sum(jnp.where(same, jnp.broadcast_to(row, (n, n)), 0.0), axis=1, keepdims=True)


def eye(n):
    same = lax.broadcasted_iota(jnp.int32, (n, n), 0) == lax.broadcasted_iota(jnp.int32, (n, n), 1)
    return same.astype(F32).astype(BF16)


def swap_halves(value):
    return pltpu.roll(value.astype(F32), 64, 1)


def low_lanes(shape):
    return lax.broadcasted_iota(jnp.int32, shape, 1) < 64


def pack_pair(natural, other, natural_low):
    shape = natural.shape
    keep = low_lanes(shape) if natural_low else jnp.logical_not(low_lanes(shape))
    return jnp.where(keep, natural.astype(F32), swap_halves(other)).astype(BF16)


def my_owner():
    return 2 * lax.axis_index("chip") + lax.axis_index("core")


def strips_kernel(x_ref, strips_ref, half, sem):
    odd = lax.axis_index("core")
    copy = pltpu.make_async_copy(
        x_ref.at[:, :, pl.ds(pl.multiple_of(128 * odd, 128), 128)], half, sem
    )
    copy.start()
    copy.wait()

    @pl.when(odd == 1)
    def _():
        for s in range(8):
            strips_ref[s] = pack_pair(half[s], half[s + 8], False)

    @pl.when(odd == 0)
    def _():
        for s in range(8):
            strips_ref[s] = pack_pair(half[s], half[s + 8], True)


def pack_tail(value):
    return jnp.concatenate([value[0:96], value[96:192]], axis=1)


def unpack_tail(value):
    return jnp.concatenate([value[:, 0:64], value[:, 64:128]], axis=0)


def sends_kernel(cot_ref, scale_ref, in_ref, w_out_ref, b_ref, gain_ref, dw_ref, spread, *rest):
    outs, taps_ref, small, turned = rest[0:4], rest[4], rest[5], rest[6]
    turned[...] = jnp.zeros((128, 128), F32)
    turned[0:48, 0:49] = dw_ref[...]
    taps_ref[...] = lax.dot_general(
        turned[...].T[0:56], spread[...], NN,
        precision=lax.Precision.HIGHEST, preferred_element_type=F32,
    )
    mine = lax.axis_index("chan")
    scale = column(scale_ref[...])
    small[...] = jnp.zeros((16, 256), F32)
    small[0:1, 0:192] = b_ref[...].astype(F32)
    small[1:2, 0:48] = gain_ref[...].astype(F32)
    tails = []
    for ref in (in_ref, w_out_ref):
        tails.append(pack_tail(ref[:, 128:192].astype(F32)).astype(BF16))
    for j, out in enumerate(outs):
        first = 2 * ((mine + j) & 3)
        for i in range(2):
            out[48 * i : 48 * i + 48] = (cot_ref[first + i].astype(F32) * scale).astype(BF16)
        out[96:288, 0:128] = in_ref[:, 0:128]
        out[96:288, 128:256] = w_out_ref[:, 0:128]
        out[288:384, 0:128] = tails[0]
        out[288:384, 128:256] = tails[1]
        out[384:400] = small[...].astype(BF16)


def gather_tile(table, up_g, mid_g, down_g, t, center, entries):
    rows = pl.ds(48 * t, 48)
    mid_g[rows, 0:256] = table[center]
    mid_g[rows, 256:512] = table[entries[3]]
    mid_g[rows, 512:768] = table[entries[4]]
    for k in range(3):
        up_g[rows, 128 * k : 128 * k + 128] = table[entries[k], :, 128:256]
        down_g[rows, 128 * k : 128 * k + 128] = table[entries[5 + k], :, 0:128]


def build_padded(pad, up_g, mid_g, down_g, up_p, mid_p, down_p):
    for maps, cells, lo, hi in ((up_p, up_g, 0, 72), (mid_p, mid_g, 72, 456), (down_p, down_g, 456, 528)):
        rows = dot(maps[...], cells[...], NT)
        for block in range(3):
            pad[block, lo:hi] = rows[:, 128 * block : 128 * block + 128]


def convolve(pad, taps, result, flip):
    def lane_block(block, carry):
        lanes = pl.ds(pl.multiple_of(block * 128, 128), 128)
        acc = [jnp.zeros((16, 128), F32) for _ in range(16)]
        for b in range(7):
            weights = []
            for a in range(7):
                tap = 7 * a + b
                weights.append(taps[pl.ds(48 - tap if flip else tap, 1), lanes])
            for r in range(22):
                line = pad[block, pl.ds(WIDE * r + b, 16)]
                for a in range(7):
                    i = r - a
                    if 0 <= i < 16:
                        acc[i] = acc[i] + line * weights[a]
        for i in range(16):
            result[pl.ds(16 * i, 16), lanes] = acc[i]
        return carry

    lax.fori_loop(0, 3, lane_block, 0)


def fill_edges(table, near_ref, far_ref, below):
    odd = lax.axis_index("core")

    def fill(upper, lower):
        for s in range(8):
            up = upper[s]
            table[s, :, 128:256] = up
            table[s + 8, :, 128:256] = swap_halves(up).astype(BF16)
            down = lower[s]
            table[below + s, :, 0:128] = down
            table[below + 8 + s, :, 0:128] = swap_halves(down).astype(BF16)

    @pl.when(odd == 0)
    def _():
        fill(near_ref, far_ref)

    @pl.when(odd == 1)
    def _():
        fill(far_ref, near_ref)


OFFSETS = (-17, -16, -15, -1, 1, 15, 16, 17)


def mix_kernel(
    own_slots, par_slots, adj, x_ref, par_ref, near_ref, far_ref, taps, up_p, mid_p, down_p,
    owned_ref, pad_out, m0, m1, m2, m3,
    place, table, up_g, mid_g, down_g, pad, result, flat,
):
    me = my_owner()
    odd = lax.axis_index("core")
    mine = lax.axis_index("chan")
    base = 8 * me
    for t in range(8):
        place[t] = 0
    for s in range(16):
        for slots, row in ((own_slots, odd), (par_slots, 1 - odd)):
            t = slots[s] - base

            @pl.when((t >= 0) & (t < 8))
            def _():
                place[t] = 16 + 16 * row + s

    table[pl.ds(16 + 16 * odd, 16)] = x_ref[...]
    table[pl.ds(32 - 16 * odd, 16)] = par_ref[...]
    table[64] = jnp.zeros((48, 256), BF16)

    fill_edges(table, near_ref, far_ref, 48)
    for t in range(8):
        center = place[t]
        entries = [jnp.where(adj[t, k] < 512, center + OFFSETS[k], 64) for k in range(8)]
        gather_tile(table, up_g, mid_g, down_g, t, center, entries)
    owned_ref[...] = mid_g[:, 0:256].reshape(8, 48, 256)
    build_padded(pad, up_g, mid_g, down_g, up_p, mid_p, down_p)
    pad_out[...] = pad[...].astype(BF16)
    convolve(pad, taps, result, False)
    flat[...] = result[...].T.astype(BF16).reshape(8, 48, 256)
    for j, out in enumerate((m0, m1, m2, m3)):
        first = 2 * ((mine + j) & 3)
        out[0] = flat[first]
        out[1] = flat[first + 1]


def turn_kernel(p0, p1, p2, p3, w_in, w_out, in_t, out_t, bias, gain, dbranch):
    mine = lax.axis_index("chan")
    unit = eye(192)
    for j, ref in enumerate((p0, p1, p2, p3)):
        a = (mine + 4 - j) & 3
        for i in range(2):
            dbranch[a, :, 256 * i : 256 * i + 256] = ref[48 * i : 48 * i + 48]
        for full, turned, lanes in ((w_in, in_t, 0), (w_out, out_t, 128)):
            tail = ref[288:384, lanes : lanes + 128].astype(F32)
            whole = jnp.concatenate(
                [
                    ref[96:288, lanes : lanes + 128].astype(F32),
                    unpack_tail(tail),
                ],
                axis=1,
            ).astype(BF16)
            full[j] = whole
            turned[j] = dot(unit, whole, NT).astype(BF16)
        cols = dot(unit, ref[384:400, 0:192], NT)
        bias[j] = jnp.broadcast_to(cols[:, 0:1], (192, 128))
        gain[a] = jnp.broadcast_to(cols[0:48, 1:2], (48, 128))


def across(col_block):
    return jnp.concatenate([col_block] * 4, axis=1)


def mlp_kernel(
    m0, m1, m2, m3, w_in, w_out, in_t, out_t, bias, gain, db_ref,
    g0, g1, g2, g3, keep_ref, give_ref, mixed_s, back_s, branch_s, halves,
):
    mine = lax.axis_index("chan")
    for j, m_ref in enumerate((m0, m1, m2, m3)):
        a = (mine + 4 - j) & 3
        for i in range(2):
            mixed_s[a, :, 256 * i : 256 * i + 256] = m_ref[i]
    mixed = mixed_s[...].reshape(192, 512).astype(F32)
    dbranch = db_ref[...].reshape(192, 512)
    mean = jnp.sum(mixed, axis=0, keepdims=True) / CHANNELS
    inv = lax.rsqrt(
        jnp.sum(mixed * mixed, axis=0, keepdims=True) / CHANNELS - mean * mean + EPSILON
    )
    x_hat = (mixed - mean) * inv
    gain_full = across(gain[...].reshape(192, 128))
    normed = (x_hat * gain_full).astype(BF16)
    branch = jnp.zeros((192, 512), F32)
    dnormed = jnp.zeros((192, 512), F32)
    for j in range(4):
        preact = dot(in_t[j], normed, NN) + across(bias[j])
        square = preact * preact
        tangent = jnp.tanh(GELU_SCALE * (preact + GELU_CUBIC * square * preact))
        half = 0.5 * (1.0 + tangent)
        act = (preact * half).astype(BF16)
        slope = half + 0.5 * preact * (1.0 - tangent * tangent) * (
            GELU_SCALE * (1.0 + 3.0 * GELU_CUBIC * square)
        )
        branch = branch + dot(out_t[j], act, NN)
        pre_grad = (dot(w_out[j], dbranch, NN) * slope).astype(BF16)
        dnormed = dnormed + dot(w_in[j], pre_grad, NN)
        for side, grad in enumerate((dot(normed, pre_grad, NT), dot(act, dbranch, NT))):
            halves[side, j, 0:192] = grad[:, 0:128].astype(BF16)
            halves[side, j, 192:288] = pack_tail(grad[:, 128:192]).astype(BF16)
    core = lax.axis_index("core")
    keep_ref[...] = halves[core]
    give_ref[...] = halves[1 - core]
    xhat_grad = dnormed * gain_full
    first = jnp.sum(xhat_grad, axis=0, keepdims=True) / CHANNELS
    second = jnp.sum(xhat_grad * x_hat, axis=0, keepdims=True) / CHANNELS
    dmixed = (inv * (xhat_grad - first - x_hat * second)).astype(BF16)
    back_s[...] = dmixed.reshape(4, 48, 512)
    branch_s[...] = branch.astype(BF16).reshape(4, 48, 512)
    for j, g_ref in enumerate((g0, g1, g2, g3)):
        a = (mine + j) & 3
        for i in range(2):
            g_ref[48 * i : 48 * i + 48] = back_s[a, :, 256 * i : 256 * i + 256]
            g_ref[96 + 48 * i : 144 + 48 * i] = branch_s[a, :, 256 * i : 256 * i + 256]


def land_kernel(g0, g1, g2, g3, grad_ref):
    mine = lax.axis_index("chan")
    for j, ref in enumerate((g0, g1, g2, g3)):
        first = 2 * ((mine + 4 - j) & 3)
        for i in range(2):
            grad_ref[first + i] = ref[48 * i : 48 * i + 48]


def merge_kernel(keep_ref, got_ref, out_ref):
    mine = lax.axis_index("chan")
    for j in range(4):
        both = keep_ref[j].astype(F32) + got_ref[j].astype(F32)
        out_ref[(mine + 4 - j) & 3] = both.astype(BF16)


def taps_kernel(grad_ref, pad_ref, fold, out_ref, pad, grad_t, sums):
    pad[...] = pad_ref[...].astype(F32)
    grad_t[...] = grad_ref[...].reshape(384, 256).astype(F32).T
    sums[...] = jnp.zeros((64, 384), F32)

    def lane_block(block, carry):
        lanes = pl.ds(pl.multiple_of(block * 128, 128), 128)
        lines = [grad_t[pl.ds(16 * i, 16), lanes] for i in range(16)]
        for b in range(7):
            acc = [jnp.zeros((16, 128), F32) for _ in range(7)]
            for r in range(22):
                line = pad[block, pl.ds(WIDE * r + b, 16)]
                for a in range(7):
                    i = r - a
                    if 0 <= i < 16:
                        acc[a] = acc[a] + line * lines[i]
            for a in range(7):
                sums[pl.ds(7 * a + b, 1), lanes] = jnp.sum(acc[a], axis=0, keepdims=True)
        return carry

    lax.fori_loop(0, 3, lane_block, 0)
    out_ref[...] = lax.dot_general(
        sums[...], fold[...], NN, precision=lax.Precision.HIGHEST, preferred_element_type=F32
    )


def pieces_kernel(parts_ref, taps_ref, out_ref, total, rows):
    total[0:288] = jnp.sum(parts_ref[...].astype(F32), axis=0)
    total[288:352] = taps_ref[...]
    rows[...] = jnp.zeros((32, 16, 128), F32)
    for q in range(11):
        rows[:, q, :] = total[32 * q : 32 * q + 32]
    out_ref[...] = rows[...].astype(BF16)


def edges_kernel(own_ref, par_ref, edge_ref):
    odd = lax.axis_index("core")

    @pl.when(odd == 1)
    def _():
        for t in range(8):
            edge_ref[t] = pack_pair(par_ref[t, :, 128:256], own_ref[t, :, 128:256], False)

    @pl.when(odd == 0)
    def _():
        for t in range(8):
            edge_ref[t] = pack_pair(own_ref[t, :, 0:128], par_ref[t, :, 0:128], True)


def total_kernel(factor, in_ref, out_ref):
    total = jnp.sum(in_ref[...].astype(F32), axis=0, keepdims=True) * factor
    out_ref[...] = jnp.broadcast_to(total, in_ref.shape).astype(out_ref.dtype)


def finish_kernel(in_ref, other_ref, dw_ref, w1_ref, w2_ref, rows, flat):
    core = lax.axis_index("core")
    for ref, side in ((in_ref, core), (other_ref, 1 - core)):
        rows[...] = ref[...].astype(F32)
        for q in range(11):
            flat[side, 32 * q : 32 * q + 32] = rows[:, q, :]
    for out, side in ((w1_ref, 0), (w2_ref, 1)):
        out[:, 0:128] = flat[side, 0:192]
        out[:, 128:192] = unpack_tail(flat[side, 192:288])
    dw = flat[0, 288:352] + flat[1, 288:352]
    dw_ref[...] = dw.T[0:48, 0:49]


def unmix_kernel(
    adj, grad_ref, par_ref, near_ref, far_ref, cot_ref, taps, up_p, mid_p, down_p,
    owned_ref, scale_ref, r0, r1, r2, r3,
    out_ref, gin_ref,
    table, up_g, mid_g, down_g, pad, result,
):
    me = my_owner()
    odd = lax.axis_index("core")
    mine = lax.axis_index("chan")
    start = 16 * (me // 2) - 16
    table[pl.ds(16 + 8 * odd, 8)] = grad_ref[...]
    table[pl.ds(24 - 8 * odd, 8)] = par_ref[...]
    table[48] = jnp.zeros((48, 256), BF16)
    fill_edges(table, near_ref, far_ref, 32)
    for t in range(8):
        center = 16 + 8 * odd + t
        entries = [jnp.where(adj[t, k] < 512, adj[t, k] - start, 48) for k in range(8)]
        gather_tile(table, up_g, mid_g, down_g, t, center, entries)
    build_padded(pad, up_g, mid_g, down_g, up_p, mid_p, down_p)
    convolve(pad, taps, result, True)
    back = result[...].T.reshape(8, 48, 256)
    gin_ref[...] = (cot_ref[...].astype(F32) + back).astype(BF16)
    scale = column(scale_ref[...])
    for j, ref in enumerate((r0, r1, r2, r3)):
        first = 2 * ((mine + 4 - j) & 3)
        for i in range(2):
            out_ref[first + i] = (
                owned_ref[first + i].astype(F32) + scale * ref[96 + 48 * i : 144 + 48 * i].astype(F32)
            ).astype(BF16)


def fetching(kernel, fetch, n_in):
    def outer(*refs):
        inputs, rest = list(refs[:n_in]), refs[n_in:]
        rest, local, sems = rest[: -len(fetch) - 1], rest[-len(fetch) - 1 : -1], rest[-1]
        copies = [
            pltpu.make_async_copy(inputs[i], buf, sems.at[n])
            for n, (i, buf) in enumerate(zip(fetch, local))
        ]
        for copy in copies:
            copy.start()
        for copy in copies:
            copy.wait()
        for i, buf in zip(fetch, local):
            inputs[i] = buf
        kernel(*inputs, *rest)

    return outer


def call(kernel, shapes, scratch=(), smem=0, n_in=0, name=None, near=(), fetch=()):
    vmem = pl.BlockSpec(memory_space=pltpu.VMEM)
    scalar = pl.BlockSpec(memory_space=pltpu.SMEM)
    many = isinstance(shapes, (list, tuple))

    def run(*args):
        specs = [
            pl.BlockSpec(memory_space=pltpu.HBM) if i in fetch else scalar if i < smem else vmem
            for i in range(n_in)
        ]
        scratches = list(scratch)
        if fetch:
            scratches += [pltpu.VMEM(args[i].shape, args[i].dtype) for i in fetch]
            scratches.append(pltpu.SemaphoreType.DMA((len(fetch),)))
        inner = pl.pallas_call(
            fetching(kernel, fetch, n_in) if fetch else kernel,
            out_shape=shapes,
            in_specs=specs,
            out_specs=[vmem] * len(shapes) if many else vmem,
            scratch_shapes=scratches,
            compiler_params=pltpu.CompilerParams(vmem_limit_bytes=24 << 20),
            name=name,
        )
        spaces = {**{i: pltpu.VMEM for i in near}, **{i: pltpu.HBM for i in fetch}}
        return inner(
            *(
                pltpu.with_memory_space_constraint(a, spaces[i]) if i in spaces else a
                for i, a in enumerate(args)
            )
        )

    return run


def shape(*dims, dtype=BF16):
    return jax.ShapeDtypeStruct(dims, dtype)


def held(*dims, dtype=BF16):
    return pltpu.VMEM(dims, dtype)


def along_chan(values):
    got = [values[0]]
    for j in range(1, 4):
        got.append(lax.ppermute(values[j], "chan", [(i, (i + j) % 4) for i in range(4)]))
    return got


def body(
    x_scan, slot_owner, adjacency, cotangent, dw_weight, ln_gain, w_in, b_in, w_out, layer_scale
):
    devices = lax.axis_size("chip") * 2
    up_p, mid_p, down_p = (jnp.asarray(v) for v in placement_tables())
    fold_map = (np.arange(384)[:, None] % 48 == np.arange(128)[None, :]).astype(np.float32)
    fold = jnp.asarray(fold_map)
    spread_map = jnp.asarray(np.ascontiguousarray(fold_map.T))
    scale_row = layer_scale.reshape(1, 48)
    owners = ("chip", "core")

    def after(value, *first):
        return lax.optimization_barrier((value, first))[0]

    def partner(value):
        return lax.ppermute(value, "core", [(0, 1), (1, 0)])

    def next_chip(value):
        pairs = [(i, i + 1 if i & 1 else i - 1) for i in range(devices)]
        return lax.ppermute(value, owners, [p for p in pairs if 0 <= p[1] < devices])

    tile_chunk = held(2, 48, 256)
    par_x = partner(x_scan)
    par_slots = partner(slot_owner)
    strips = pl.pallas_call(
        strips_kernel,
        out_shape=held(8, 48, 128),
        in_specs=[pl.BlockSpec(memory_space=pltpu.HBM)],
        out_specs=pl.BlockSpec(memory_space=pltpu.VMEM),
        scratch_shapes=[pltpu.VMEM((16, 48, 128), BF16), pltpu.SemaphoreType.DMA(())],
        name="strips",
    )(pltpu.with_memory_space_constraint(x_scan, pltpu.HBM))
    near = next_chip(strips)
    far = partner(near)
    *sends, taps = call(
        sends_kernel,
        [held(400, 256)] * 4 + [held(56, 384, dtype=F32)],
        scratch=[pltpu.VMEM((16, 256), F32), pltpu.VMEM((128, 128), F32)],
        n_in=8,
        name="sends",
        fetch=range(8),
    )(
        cotangent, after(scale_row, strips, par_x, par_slots), w_in, w_out,
        b_in.reshape(1, 192), ln_gain.reshape(1, 48), dw_weight, spread_map,
    )
    all_sends = along_chan(after(sends, near))

    grid_scratch = lambda entries: [
        pltpu.VMEM((entries, 48, 256), BF16),
        pltpu.VMEM((384, 384), BF16),
        pltpu.VMEM((384, 768), BF16),
        pltpu.VMEM((384, 384), BF16),
        pltpu.VMEM((3, 22 * WIDE, 128), F32),
        pltpu.VMEM((256, 384), F32),
    ]
    mix = call(
        mix_kernel,
        [shape(8, 48, 256), shape(3, 22 * WIDE, 128)] + [tile_chunk] * 4,
        scratch=[pltpu.SMEM((8,), jnp.int32)] + grid_scratch(65) + [pltpu.VMEM((8, 48, 256), BF16)],
        smem=3,
        n_in=11,
        name="mix",
        near=(4, 5, 6, 7),
    )
    owned, padded, *mixed = mix(
        slot_owner, par_slots, adjacency, x_scan, par_x, near, far, taps, up_p, mid_p, down_p
    )
    all_mixed = along_chan(mixed)

    square = held(4, 192, 192)
    turn = call(
        turn_kernel,
        [square] * 4
        + [held(4, 192, 128, dtype=F32), held(4, 48, 128, dtype=F32), held(4, 48, 512)],
        n_in=4,
        name="turn",
        near=(0, 1, 2, 3),
    )
    turned = turn(*after(all_sends, mixed[0]))

    *packets, keep, give = call(
        mlp_kernel,
        [held(192, 256)] * 4 + [held(4, 288, 128)] * 2,
        scratch=[pltpu.VMEM((4, 48, 512), BF16)] * 3 + [pltpu.VMEM((2, 4, 288, 128), BF16)],
        n_in=11,
        name="mlp",
        near=range(11),
    )(*all_mixed, *turned)
    all_back = along_chan(packets)
    merged = call(merge_kernel, held(4, 288, 128), n_in=2, name="merge", near=range(2))(
        keep, partner(give)
    )
    partials = lax.all_to_all(merged, "chan", 0, 0, tiled=True)
    grads = call(land_kernel, held(8, 48, 256), n_in=4, name="land", near=range(4))(*all_back)
    par_grads = partner(grads)
    tap_sums = call(
        taps_kernel,
        held(64, 128, dtype=F32),
        scratch=[
            pltpu.VMEM((3, 22 * WIDE, 128), F32),
            pltpu.VMEM((256, 384), F32),
            pltpu.VMEM((64, 384), F32),
        ],
        n_in=3,
        name="tap_sums",
        near=(0,),
    )(grads, padded, fold)
    edges = call(edges_kernel, held(8, 48, 128), n_in=2, name="edges", near=(0, 1))(
        after(grads, tap_sums), par_grads
    )
    near_grads = next_chip(edges)
    pieces = call(
        pieces_kernel,
        held(32, 16, 128),
        scratch=[pltpu.VMEM((352, 128), F32), pltpu.VMEM((32, 16, 128), F32)],
        n_in=2,
        name="pieces",
        near=range(2),
    )(partials, tap_sums)
    arrived = lax.all_to_all(after(pieces, edges), "chip", 0, 0, tiled=True)
    arrived, near_grads = lax.optimization_barrier((arrived, near_grads))

    factor = 1.0 / math.sqrt(adjacency.shape[0] * devices * PIX)
    far_grads = partner(near_grads)
    totals = call(
        functools.partial(total_kernel, factor), held(32, 16, 128), n_in=1, name="totals", near=(0,)
    )(arrived)
    spread = lax.all_to_all(totals, "chip", 0, 0, tiled=True)

    unmix = call(
        unmix_kernel,
        [shape(8, 48, 256), shape(8, 48, 256)],
        scratch=grid_scratch(49),
        smem=1,
        n_in=16,
        name="unmix",
        near=(1, 2, 3, 4, 12, 13, 14, 15),
    )
    output, grad_in = unmix(
        adjacency, grads, par_grads, near_grads, far_grads,
        cotangent, taps, up_p, mid_p, down_p, owned, after(scale_row, totals), *all_back
    )
    spread = after(spread, output)
    grad_dw, grad_w1, grad_w2 = call(
        finish_kernel,
        [shape(48, 49, dtype=F32), shape(192, 192, dtype=F32), shape(192, 192, dtype=F32)],
        scratch=[pltpu.VMEM((32, 16, 128), F32), pltpu.VMEM((2, 352, 128), F32)],
        n_in=2,
        name="finish",
        near=(0, 1),
    )(spread, partner(spread))
    return (output, grad_in, grad_dw, grad_w1, grad_w2)


def solution(mesh):
    chips, chan = mesh.devices.shape[0] // 2, mesh.devices.shape[1]
    parts = Mesh(mesh.devices.reshape(chips, 2, chan), ("chip", "core", "chan"))
    tiles = ("chip", "core")
    in_specs = (
        P(tiles, "chan", None),
        P(tiles),
        P(tiles, None),
        P(tiles, "chan", None),
        P("chan", None),
        P("chan"),
        P(None, "chan"),
        P("chan"),
        P("chan", None),
        P("chan"),
    )
    out_specs = (
        P(tiles, "chan", None),
        P(tiles, "chan", None),
        P("chan", None),
        P(None, "chan"),
        P("chan", None),
    )
    return jax.shard_map(body, mesh=parts, in_specs=in_specs, out_specs=out_specs, check_vma=False)
```

```python
import functools
import math

import jax
import jax.numpy as jnp
import numpy as np
from jax import lax
from jax.experimental import pallas as pl
from jax.experimental.pallas import tpu as pltpu
from jax.sharding import Mesh
from jax.sharding import PartitionSpec as P

CHANNELS = 192
SIDE = 16
PIX = 256
WIDE = 24
EPSILON = 1e-06
GELU_SCALE = 0.7978845608
GELU_CUBIC = 0.044715

F32 = jnp.float32
BF16 = jnp.bfloat16
NT = (((1,), (1,)), ((), ()))
NN = (((1,), (0,)), ((), ()))


def dot(a, b, dims):
    return lax.dot_general(a, b, dims, preferred_element_type=F32)


def placement_tables():
    maps = np.zeros((22 * WIDE, 768), np.float32)
    up, mid, down = maps[0:72], maps[72:456], maps[456:528]
    for j in range(22):
        if j < 3:
            side, col = 0, 13 + j
        elif j < 19:
            side, col = 1, j - 3
        else:
            side, col = 2, j - 19
        for i in range(3):
            up[i * WIDE + j, 128 * side + 16 * (13 + i) + col - 128] = 1
            down[i * WIDE + j, 128 * side + 16 * i + col] = 1
        for i in range(16):
            block = (1, 0, 2)[side]
            mid[i * WIDE + j, 256 * block + 16 * i + col] = 1
    return maps.astype(jnp.bfloat16)


def column(row):
    n = row.shape[1]
    same = lax.broadcasted_iota(jnp.int32, (n, n), 0) == lax.broadcasted_iota(jnp.int32, (n, n), 1)
    return jnp.sum(jnp.where(same, jnp.broadcast_to(row, (n, n)), 0.0), axis=1, keepdims=True)


def eye(n):
    same = lax.broadcasted_iota(jnp.int32, (n, n), 0) == lax.broadcasted_iota(jnp.int32, (n, n), 1)
    return same.astype(F32).astype(BF16)


def swap_halves(value):
    return pltpu.roll(value.astype(F32), 64, 1)


def low_lanes(shape):
    return lax.broadcasted_iota(jnp.int32, shape, 1) < 64


def pack_pair(natural, other, natural_low):
    shape = natural.shape
    keep = low_lanes(shape) if natural_low else jnp.logical_not(low_lanes(shape))
    return jnp.where(keep, natural.astype(F32), swap_halves(other)).astype(BF16)


def my_owner():
    return 2 * lax.axis_index("chip") + lax.axis_index("core")


def pack_tail(value):
    return jnp.concatenate([value[0:96], value[96:192]], axis=1)


def unpack_tail(value):
    return jnp.concatenate([value[:, 0:64], value[:, 64:128]], axis=0)


def open_kernel(
    x_hbm, cot_hbm, scale_hbm, in_hbm, w_out_hbm, b_hbm, gain_hbm, dw_hbm, spread_hbm,
    strips_ref, s0, s1, s2, s3, taps_ref, spread, x_ref,
    cot_ref, scale_ref, in_ref, w_out_ref, b_ref, gain_ref, dw_ref, small, turned, sems,
):
    outs = (s0, s1, s2, s3)
    mine = lax.axis_index("chan")
    odd = lax.axis_index("core")
    sources = (x_hbm, cot_hbm, scale_hbm, in_hbm, w_out_hbm, b_hbm, gain_hbm, dw_hbm, spread_hbm)
    targets = (x_ref, cot_ref, scale_ref, in_ref, w_out_ref, b_ref, gain_ref, dw_ref, spread)
    copies = [
        pltpu.make_async_copy(source, target, sems.at[n])
        for n, (source, target) in enumerate(zip(sources, targets))
    ]
    for copy in copies:
        copy.start()
    copies[0].wait()

    @pl.when(odd == 1)
    def _():
        for s in range(8):
            strips_ref[s] = pack_pair(x_ref[s, :, 128:256], x_ref[s + 8, :, 128:256], False)

    @pl.when(odd == 0)
    def _():
        for s in range(8):
            strips_ref[s] = pack_pair(x_ref[s, :, 0:128], x_ref[s + 8, :, 0:128], True)

    for copy in copies[1:]:
        copy.wait()
    turned[...] = jnp.zeros((128, 128), F32)
    turned[0:48, 0:49] = dw_ref[...]
    taps_ref[...] = lax.dot_general(
        turned[...].T[0:56], spread[...], NN,
        precision=lax.Precision.HIGHEST, preferred_element_type=F32,
    )
    scale = column(scale_ref[...])
    small[...] = jnp.zeros((16, 256), F32)
    small[0:1, 0:192] = b_ref[...].astype(F32).reshape(1, 192)
    small[1:2, 0:48] = gain_ref[...].astype(F32)
    tails = []
    for ref in (in_ref, w_out_ref):
        tails.append(pack_tail(ref[:, 128:192].astype(F32)).astype(BF16))
    for j, out in enumerate(outs):
        first = 2 * ((mine + j) & 3)
        for i in range(2):
            out[48 * i : 48 * i + 48] = (cot_ref[first + i].astype(F32) * scale).astype(BF16)
        out[96:288, 0:128] = in_ref[:, 0:128]
        out[96:288, 128:256] = w_out_ref[:, 0:128]
        out[288:384, 0:128] = tails[0]
        out[288:384, 128:256] = tails[1]
        out[384:400] = small[...].astype(BF16)


def gather_tile(table, up_g, mid_g, down_g, t, center, entries):
    rows = pl.ds(48 * t, 48)
    mid_g[rows, 0:256] = table[center]
    mid_g[rows, 256:512] = table[entries[3]]
    mid_g[rows, 512:768] = table[entries[4]]
    for k in range(3):
        up_g[rows, 128 * k : 128 * k + 128] = table[entries[k], :, 128:256]
        down_g[rows, 128 * k : 128 * k + 128] = table[entries[5 + k], :, 0:128]


def build_padded(pad, up_g, mid_g, down_g, maps):
    for cells, lo, hi in ((up_g, 0, 72), (mid_g, 72, 456), (down_g, 456, 528)):
        rows = dot(maps[lo:hi, 0 : cells.shape[1]], cells[...], NT)
        for block in range(3):
            pad[block, lo:hi] = rows[:, 128 * block : 128 * block + 128]


def convolve(pad, taps, result, flip):
    def lane_block(block, carry):
        lanes = pl.ds(pl.multiple_of(block * 128, 128), 128)
        acc = [jnp.zeros((16, 128), F32) for _ in range(16)]
        for b in range(7):
            weights = []
            for a in range(7):
                tap = 7 * a + b
                weights.append(taps[pl.ds(48 - tap if flip else tap, 1), lanes])
            for r in range(22):
                line = pad[block, pl.ds(WIDE * r + b, 16)]
                for a in range(7):
                    i = r - a
                    if 0 <= i < 16:
                        acc[i] = acc[i] + line * weights[a]
        for i in range(16):
            result[pl.ds(16 * i, 16), lanes] = acc[i]
        return carry

    lax.fori_loop(0, 3, lane_block, 0)


def fill_edges(table, near_ref, far_ref, below):
    odd = lax.axis_index("core")

    def fill(upper, lower):
        for s in range(8):
            up = upper[s]
            table[s, :, 128:256] = up
            table[s + 8, :, 128:256] = swap_halves(up).astype(BF16)
            down = lower[s]
            table[below + s, :, 0:128] = down
            table[below + 8 + s, :, 0:128] = swap_halves(down).astype(BF16)

    @pl.when(odd == 0)
    def _():
        fill(near_ref, far_ref)

    @pl.when(odd == 1)
    def _():
        fill(far_ref, near_ref)


OFFSETS = (-17, -16, -15, -1, 1, 15, 16, 17)


def mix_kernel(
    own_slots, par_slots, adj, x_ref, par_ref, near_ref, far_ref, taps, maps,
    owned_ref, pad_out, m0, m1, m2, m3,
    place, table, up_g, mid_g, down_g, pad, result, flat,
):
    me = my_owner()
    odd = lax.axis_index("core")
    mine = lax.axis_index("chan")
    base = 8 * me
    for t in range(8):
        place[t] = 0
    for s in range(16):
        for slots, row in ((own_slots, odd), (par_slots, 1 - odd)):
            t = slots[s] - base

            @pl.when((t >= 0) & (t < 8))
            def _():
                place[t] = 16 + 16 * row + s

    table[pl.ds(16 + 16 * odd, 16)] = x_ref[...]
    table[pl.ds(32 - 16 * odd, 16)] = par_ref[...]
    table[64] = jnp.zeros((48, 256), BF16)

    fill_edges(table, near_ref, far_ref, 48)
    for t in range(8):
        center = place[t]
        entries = [jnp.where(adj[t, k] < 512, center + OFFSETS[k], 64) for k in range(8)]
        gather_tile(table, up_g, mid_g, down_g, t, center, entries)
    owned_ref[...] = mid_g[:, 0:256].reshape(8, 48, 256)
    build_padded(pad, up_g, mid_g, down_g, maps)
    pad_out[...] = pad[...].astype(BF16)
    convolve(pad, taps, result, False)
    flat[...] = result[...].T.astype(BF16).reshape(8, 48, 256)
    for j, out in enumerate((m0, m1, m2, m3)):
        first = 2 * ((mine + j) & 3)
        out[0] = flat[first]
        out[1] = flat[first + 1]


def turn_kernel(p0, p1, p2, p3, w_in, w_out, in_t, out_t, bias, gain, dbranch):
    mine = lax.axis_index("chan")
    unit = eye(192)
    for j, ref in enumerate((p0, p1, p2, p3)):
        a = (mine + 4 - j) & 3
        for i in range(2):
            dbranch[a, :, 256 * i : 256 * i + 256] = ref[48 * i : 48 * i + 48]
        for full, turned, lanes in ((w_in, in_t, 0), (w_out, out_t, 128)):
            tail = ref[288:384, lanes : lanes + 128].astype(F32)
            whole = jnp.concatenate(
                [
                    ref[96:288, lanes : lanes + 128].astype(F32),
                    unpack_tail(tail),
                ],
                axis=1,
            ).astype(BF16)
            full[j] = whole
            turned[j] = dot(unit, whole, NT).astype(BF16)
        cols = dot(unit, ref[384:400, 0:192], NT)
        bias[j] = jnp.broadcast_to(cols[:, 0:1], (192, 128))
        gain[a] = jnp.broadcast_to(cols[0:48, 1:2], (48, 128))


def across(col_block):
    return jnp.concatenate([col_block] * 4, axis=1)


def mlp_kernel(
    m0, m1, m2, m3, w_in, w_out, in_t, out_t, bias, gain, db_ref,
    g0, g1, g2, g3, keep_ref, give_ref, mixed_s, back_s, branch_s, halves,
):
    mine = lax.axis_index("chan")
    for j, m_ref in enumerate((m0, m1, m2, m3)):
        a = (mine + 4 - j) & 3
        for i in range(2):
            mixed_s[a, :, 256 * i : 256 * i + 256] = m_ref[i]
    mixed = mixed_s[...].reshape(192, 512).astype(F32)
    dbranch = db_ref[...].reshape(192, 512)
    mean = jnp.sum(mixed, axis=0, keepdims=True) / CHANNELS
    inv = lax.rsqrt(
        jnp.sum(mixed * mixed, axis=0, keepdims=True) / CHANNELS - mean * mean + EPSILON
    )
    x_hat = (mixed - mean) * inv
    gain_full = across(gain[...].reshape(192, 128))
    normed = (x_hat * gain_full).astype(BF16)
    branch = jnp.zeros((192, 512), F32)
    dnormed = jnp.zeros((192, 512), F32)
    for j in range(4):
        preact = dot(in_t[j], normed, NN) + across(bias[j])
        square = preact * preact
        tangent = jnp.tanh(GELU_SCALE * (preact + GELU_CUBIC * square * preact))
        half = 0.5 * (1.0 + tangent)
        act = (preact * half).astype(BF16)
        slope = half + 0.5 * preact * (1.0 - tangent * tangent) * (
            GELU_SCALE * (1.0 + 3.0 * GELU_CUBIC * square)
        )
        branch = branch + dot(out_t[j], act, NN)
        pre_grad = (dot(w_out[j], dbranch, NN) * slope).astype(BF16)
        dnormed = dnormed + dot(w_in[j], pre_grad, NN)
        for side, grad in enumerate((dot(normed, pre_grad, NT), dot(act, dbranch, NT))):
            halves[side, j, 0:192] = grad[:, 0:128].astype(BF16)
            halves[side, j, 192:288] = pack_tail(grad[:, 128:192]).astype(BF16)
    core = lax.axis_index("core")
    keep_ref[...] = halves[core]
    give_ref[...] = halves[1 - core]
    xhat_grad = dnormed * gain_full
    first = jnp.sum(xhat_grad, axis=0, keepdims=True) / CHANNELS
    second = jnp.sum(xhat_grad * x_hat, axis=0, keepdims=True) / CHANNELS
    dmixed = (inv * (xhat_grad - first - x_hat * second)).astype(BF16)
    back_s[...] = dmixed.reshape(4, 48, 512)
    branch_s[...] = branch.astype(BF16).reshape(4, 48, 512)
    for j, g_ref in enumerate((g0, g1, g2, g3)):
        a = (mine + j) & 3
        for i in range(2):
            g_ref[48 * i : 48 * i + 48] = back_s[a, :, 256 * i : 256 * i + 256]
            g_ref[96 + 48 * i : 144 + 48 * i] = branch_s[a, :, 256 * i : 256 * i + 256]


def land_kernel(g0, g1, g2, g3, grad_ref):
    mine = lax.axis_index("chan")
    for j, ref in enumerate((g0, g1, g2, g3)):
        first = 2 * ((mine + 4 - j) & 3)
        for i in range(2):
            grad_ref[first + i] = ref[48 * i : 48 * i + 48]


def merge_kernel(keep_ref, got_ref, out_ref):
    mine = lax.axis_index("chan")
    for j in range(4):
        both = keep_ref[j].astype(F32) + got_ref[j].astype(F32)
        out_ref[(mine + 4 - j) & 3] = both.astype(BF16)


def taps_kernel(grad_ref, pad_ref, fold, out_ref, pad, grad_t, sums):
    pad[...] = pad_ref[...].astype(F32)
    grad_t[...] = grad_ref[...].reshape(384, 256).astype(F32).T
    sums[...] = jnp.zeros((64, 384), F32)

    def lane_block(block, carry):
        lanes = pl.ds(pl.multiple_of(block * 128, 128), 128)
        lines = [grad_t[pl.ds(16 * i, 16), lanes] for i in range(16)]
        for b in range(7):
            acc = [jnp.zeros((16, 128), F32) for _ in range(7)]
            for r in range(22):
                line = pad[block, pl.ds(WIDE * r + b, 16)]
                for a in range(7):
                    i = r - a
                    if 0 <= i < 16:
                        acc[a] = acc[a] + line * lines[i]
            for a in range(7):
                sums[pl.ds(7 * a + b, 1), lanes] = jnp.sum(acc[a], axis=0, keepdims=True)
        return carry

    lax.fori_loop(0, 3, lane_block, 0)
    out_ref[...] = lax.dot_general(
        sums[...], fold[...], NT, precision=lax.Precision.HIGHEST, preferred_element_type=F32
    )


def pieces_kernel(parts_ref, taps_ref, out_ref, total, rows):
    total[0:288] = jnp.sum(parts_ref[...].astype(F32), axis=0)
    total[288:352] = taps_ref[...]
    rows[...] = jnp.zeros((32, 16, 128), F32)
    for q in range(11):
        rows[:, q, :] = total[32 * q : 32 * q + 32]
    out_ref[...] = rows[...].astype(BF16)


def edges_kernel(own_ref, par_ref, edge_ref):
    odd = lax.axis_index("core")

    @pl.when(odd == 1)
    def _():
        for t in range(8):
            edge_ref[t] = pack_pair(par_ref[t, :, 128:256], own_ref[t, :, 128:256], False)

    @pl.when(odd == 0)
    def _():
        for t in range(8):
            edge_ref[t] = pack_pair(own_ref[t, :, 0:128], par_ref[t, :, 0:128], True)


def total_kernel(factor, in_ref, out_ref):
    total = jnp.sum(in_ref[...].astype(F32), axis=0, keepdims=True) * factor
    out_ref[...] = jnp.broadcast_to(total, in_ref.shape).astype(out_ref.dtype)


def finish_kernel(in_ref, other_ref, dw_ref, w1_ref, w2_ref, rows, flat):
    core = lax.axis_index("core")
    for ref, side in ((in_ref, core), (other_ref, 1 - core)):
        rows[...] = ref[...].astype(F32)
        for q in range(11):
            flat[side, 32 * q : 32 * q + 32] = rows[:, q, :]
    for out, side in ((w1_ref, 0), (w2_ref, 1)):
        out[:, 0:128] = flat[side, 0:192]
        out[:, 128:192] = unpack_tail(flat[side, 192:288])
    dw = flat[0, 288:352] + flat[1, 288:352]
    dw_ref[...] = dw.T[0:48, 0:49]


def unmix_kernel(
    adj, grad_ref, par_ref, near_ref, far_ref, cot_ref, taps, maps,
    owned_ref, scale_ref, r0, r1, r2, r3,
    out_ref, gin_ref,
    table, up_g, mid_g, down_g, pad, result,
):
    me = my_owner()
    odd = lax.axis_index("core")
    mine = lax.axis_index("chan")
    start = 16 * (me // 2) - 16
    table[pl.ds(16 + 8 * odd, 8)] = grad_ref[...]
    table[pl.ds(24 - 8 * odd, 8)] = par_ref[...]
    table[48] = jnp.zeros((48, 256), BF16)
    fill_edges(table, near_ref, far_ref, 32)
    for t in range(8):
        center = 16 + 8 * odd + t
        entries = [jnp.where(adj[t, k] < 512, adj[t, k] - start, 48) for k in range(8)]
        gather_tile(table, up_g, mid_g, down_g, t, center, entries)
    build_padded(pad, up_g, mid_g, down_g, maps)
    convolve(pad, taps, result, True)
    back = result[...].T.reshape(8, 48, 256)
    gin_ref[...] = (cot_ref[...].astype(F32) + back).astype(BF16)
    scale = column(scale_ref[...])
    for j, ref in enumerate((r0, r1, r2, r3)):
        first = 2 * ((mine + 4 - j) & 3)
        for i in range(2):
            out_ref[first + i] = (
                owned_ref[first + i].astype(F32) + scale * ref[96 + 48 * i : 144 + 48 * i].astype(F32)
            ).astype(BF16)


def call(kernel, shapes, scratch=(), smem=0, n_in=0, name=None, near=()):
    vmem = pl.BlockSpec(memory_space=pltpu.VMEM)
    scalar = pl.BlockSpec(memory_space=pltpu.SMEM)
    many = isinstance(shapes, (list, tuple))

    inner = pl.pallas_call(
        kernel,
        out_shape=shapes,
        in_specs=[scalar] * smem + [vmem] * (n_in - smem),
        out_specs=[vmem] * len(shapes) if many else vmem,
        scratch_shapes=list(scratch),
        compiler_params=pltpu.CompilerParams(vmem_limit_bytes=24 << 20),
        name=name,
    )

    def run(*args):
        return inner(
            *(
                pltpu.with_memory_space_constraint(a, pltpu.VMEM) if i in near else a
                for i, a in enumerate(args)
            )
        )

    return run


def shape(*dims, dtype=BF16):
    return jax.ShapeDtypeStruct(dims, dtype)


def held(*dims, dtype=BF16):
    return pltpu.VMEM(dims, dtype)


def along_chan(values):
    got = [values[0]]
    for j in range(1, 4):
        got.append(lax.ppermute(values[j], "chan", [(i, (i + j) % 4) for i in range(4)]))
    return got


def body(
    x_scan, slot_owner, adjacency, cotangent, dw_weight, ln_gain, w_in, b_in, w_out, layer_scale
):
    devices = lax.axis_size("chip") * 2
    maps = jnp.asarray(placement_tables())
    fold_map = (np.arange(384)[:, None] % 48 == np.arange(128)[None, :]).astype(np.float32)
    spread_map = jnp.asarray(np.ascontiguousarray(fold_map.T))
    scale_row = layer_scale.reshape(1, 48)
    owners = ("chip", "core")

    def after(value, *first):
        return lax.optimization_barrier((value, first))[0]

    def partner(value):
        return lax.ppermute(value, "core", [(0, 1), (1, 0)])

    def next_chip(value):
        pairs = [(i, i + 1 if i & 1 else i - 1) for i in range(devices)]
        return lax.ppermute(value, owners, [p for p in pairs if 0 <= p[1] < devices])

    tile_chunk = held(2, 48, 256)
    par_x = partner(x_scan)
    par_slots = partner(slot_owner)
    opening = (
        x_scan, cotangent, scale_row, w_in, w_out, b_in, ln_gain.reshape(1, 48), dw_weight, spread_map
    )
    strips, *sends, taps, fold, own_x = pl.pallas_call(
        open_kernel,
        out_shape=[held(8, 48, 128)] + [held(400, 256)] * 4
        + [held(56, 384, dtype=F32), held(128, 384, dtype=F32), held(16, 48, 256)],
        in_specs=[pl.BlockSpec(memory_space=pltpu.HBM)] * 9,
        out_specs=[pl.BlockSpec(memory_space=pltpu.VMEM)] * 8,
        scratch_shapes=[pltpu.VMEM(v.shape, v.dtype) for v in opening[1:-1]]
        + [
            pltpu.VMEM((16, 256), F32),
            pltpu.VMEM((128, 128), F32),
            pltpu.SemaphoreType.DMA((9,)),
        ],
        compiler_params=pltpu.CompilerParams(vmem_limit_bytes=24 << 20),
        name="open",
    )(*(pltpu.with_memory_space_constraint(v, pltpu.HBM) for v in opening))
    near = next_chip(strips)
    far = partner(near)
    sends[1] = after(sends[1], near, par_slots)
    all_sends = along_chan(sends)

    grid_scratch = lambda entries: [
        pltpu.VMEM((entries, 48, 256), BF16),
        pltpu.VMEM((384, 384), BF16),
        pltpu.VMEM((384, 768), BF16),
        pltpu.VMEM((384, 384), BF16),
        pltpu.VMEM((3, 22 * WIDE, 128), F32),
        pltpu.VMEM((256, 384), F32),
    ]
    mix = call(
        mix_kernel,
        [shape(8, 48, 256), shape(3, 22 * WIDE, 128)] + [tile_chunk] * 4,
        scratch=[pltpu.SMEM((8,), jnp.int32)] + grid_scratch(65) + [pltpu.VMEM((8, 48, 256), BF16)],
        smem=3,
        n_in=9,
        name="mix",
        near=(3, 4, 5, 6, 7),
    )
    owned, padded, *mixed = mix(
        slot_owner, par_slots, adjacency, own_x, par_x, near, far, taps, maps
    )
    all_mixed = along_chan(mixed)

    square = held(4, 192, 192)
    turn = call(
        turn_kernel,
        [square] * 4
        + [held(4, 192, 128, dtype=F32), held(4, 48, 128, dtype=F32), held(4, 48, 512)],
        n_in=4,
        name="turn",
        near=(0, 1, 2, 3),
    )
    turned = turn(*after(all_sends, mixed[0]))

    *packets, keep, give = call(
        mlp_kernel,
        [held(192, 256)] * 4 + [held(4, 288, 128)] * 2,
        scratch=[pltpu.VMEM((4, 48, 512), BF16)] * 3 + [pltpu.VMEM((2, 4, 288, 128), BF16)],
        n_in=11,
        name="mlp",
        near=range(11),
    )(*all_mixed, *turned)
    all_back = along_chan(packets)
    merged = call(merge_kernel, held(4, 288, 128), n_in=2, name="merge", near=range(2))(
        keep, partner(give)
    )
    partials = lax.all_to_all(merged, "chan", 0, 0, tiled=True)
    grads = call(land_kernel, held(8, 48, 256), n_in=4, name="land", near=range(4))(*all_back)
    par_grads = partner(grads)
    tap_sums = call(
        taps_kernel,
        held(64, 128, dtype=F32),
        scratch=[
            pltpu.VMEM((3, 22 * WIDE, 128), F32),
            pltpu.VMEM((256, 384), F32),
            pltpu.VMEM((64, 384), F32),
        ],
        n_in=3,
        name="tap_sums",
        near=(0, 2),
    )(grads, padded, fold)
    edges = call(edges_kernel, held(8, 48, 128), n_in=2, name="edges", near=(0, 1))(
        after(grads, tap_sums), par_grads
    )
    near_grads = next_chip(edges)
    pieces = call(
        pieces_kernel,
        held(32, 16, 128),
        scratch=[pltpu.VMEM((352, 128), F32), pltpu.VMEM((32, 16, 128), F32)],
        n_in=2,
        name="pieces",
        near=range(2),
    )(partials, tap_sums)
    arrived = lax.all_to_all(after(pieces, edges), "chip", 0, 0, tiled=True)
    arrived, near_grads = lax.optimization_barrier((arrived, near_grads))

    factor = 1.0 / math.sqrt(adjacency.shape[0] * devices * PIX)
    far_grads = partner(near_grads)
    totals = call(
        functools.partial(total_kernel, factor), held(32, 16, 128), n_in=1, name="totals", near=(0,)
    )(arrived)
    spread = lax.all_to_all(totals, "chip", 0, 0, tiled=True)

    unmix = call(
        unmix_kernel,
        [shape(8, 48, 256), shape(8, 48, 256)],
        scratch=grid_scratch(49),
        smem=1,
        n_in=14,
        name="unmix",
        near=(1, 2, 3, 4, 10, 11, 12, 13),
    )
    output, grad_in = unmix(
        adjacency, grads, par_grads, near_grads, far_grads,
        cotangent, taps, maps, owned, after(scale_row, totals), *all_back
    )
    spread = after(spread, output)
    grad_dw, grad_w1, grad_w2 = call(
        finish_kernel,
        [shape(48, 49, dtype=F32), shape(192, 192, dtype=F32), shape(192, 192, dtype=F32)],
        scratch=[pltpu.VMEM((32, 16, 128), F32), pltpu.VMEM((2, 352, 128), F32)],
        n_in=2,
        name="finish",
        near=(0, 1),
    )(spread, partner(spread))
    return (output, grad_in, grad_dw, grad_w1, grad_w2)


def solution(mesh):
    chips, chan = mesh.devices.shape[0] // 2, mesh.devices.shape[1]
    parts = Mesh(mesh.devices.reshape(chips, 2, chan), ("chip", "core", "chan"))
    tiles = ("chip", "core")
    in_specs = (
        P(tiles, "chan", None),
        P(tiles),
        P(tiles, None),
        P(tiles, "chan", None),
        P("chan", None),
        P("chan"),
        P(None, "chan"),
        P("chan"),
        P("chan", None),
        P("chan"),
    )
    out_specs = (
        P(tiles, "chan", None),
        P(tiles, "chan", None),
        P("chan", None),
        P(None, "chan"),
        P("chan", None),
    )
    return jax.shard_map(body, mesh=parts, in_specs=in_specs, out_specs=out_specs, check_vma=False)
```

```python
import functools
import math

import jax
import jax.numpy as jnp
import numpy as np
from jax import lax
from jax.experimental import pallas as pl
from jax.experimental.pallas import tpu as pltpu
from jax.sharding import Mesh
from jax.sharding import PartitionSpec as P

CHANNELS = 192
SIDE = 16
PIX = 256
WIDE = 24
EPSILON = 1e-06
GELU_SCALE = 0.7978845608
GELU_CUBIC = 0.044715

F32 = jnp.float32
BF16 = jnp.bfloat16
NT = (((1,), (1,)), ((), ()))
NN = (((1,), (0,)), ((), ()))


def dot(a, b, dims):
    return lax.dot_general(a, b, dims, preferred_element_type=F32)


def placement_tables():
    maps = np.zeros((22 * WIDE, 768), np.float32)
    up, mid, down = maps[0:72], maps[72:456], maps[456:528]
    for j in range(22):
        if j < 3:
            side, col = 0, 13 + j
        elif j < 19:
            side, col = 1, j - 3
        else:
            side, col = 2, j - 19
        for i in range(3):
            up[i * WIDE + j, 128 * side + 16 * (13 + i) + col - 128] = 1
            down[i * WIDE + j, 128 * side + 16 * i + col] = 1
        for i in range(16):
            block = (1, 0, 2)[side]
            mid[i * WIDE + j, 256 * block + 16 * i + col] = 1
    return maps.astype(jnp.bfloat16)


def column(row):
    n = row.shape[1]
    same = lax.broadcasted_iota(jnp.int32, (n, n), 0) == lax.broadcasted_iota(jnp.int32, (n, n), 1)
    return jnp.sum(jnp.where(same, jnp.broadcast_to(row, (n, n)), 0.0), axis=1, keepdims=True)


def eye(n):
    same = lax.broadcasted_iota(jnp.int32, (n, n), 0) == lax.broadcasted_iota(jnp.int32, (n, n), 1)
    return same.astype(F32).astype(BF16)


def swap_halves(value):
    return pltpu.roll(value.astype(F32), 64, 1)


def low_lanes(shape):
    return lax.broadcasted_iota(jnp.int32, shape, 1) < 64


def pack_pair(natural, other, natural_low):
    shape = natural.shape
    keep = low_lanes(shape) if natural_low else jnp.logical_not(low_lanes(shape))
    return jnp.where(keep, natural.astype(F32), swap_halves(other)).astype(BF16)


def my_owner():
    return 2 * lax.axis_index("chip") + lax.axis_index("core")


def pack_tail(value):
    return jnp.concatenate([value[0:96], value[96:192]], axis=1)


def unpack_tail(value):
    return jnp.concatenate([value[:, 0:64], value[:, 64:128]], axis=0)


def open_kernel(
    x_hbm, cot_hbm, scale_hbm, in_hbm, w_out_hbm, b_hbm, gain_hbm, dw_hbm, spread_hbm,
    strips_ref, s0, s1, s2, s3, taps_ref, spread, x_ref,
    cot_ref, scale_ref, in_ref, w_out_ref, b_ref, gain_ref, dw_ref, small, turned, sems,
):
    outs = (s0, s1, s2, s3)
    mine = lax.axis_index("chan")
    odd = lax.axis_index("core")
    sources = (x_hbm, cot_hbm, scale_hbm, in_hbm, w_out_hbm, b_hbm, gain_hbm, dw_hbm, spread_hbm)
    targets = (x_ref, cot_ref, scale_ref, in_ref, w_out_ref, b_ref, gain_ref, dw_ref, spread)
    copies = [
        pltpu.make_async_copy(source, target, sems.at[n])
        for n, (source, target) in enumerate(zip(sources, targets))
    ]
    for copy in copies:
        copy.start()
    copies[0].wait()

    @pl.when(odd == 1)
    def _():
        for s in range(8):
            strips_ref[s] = pack_pair(x_ref[s, :, 128:256], x_ref[s + 8, :, 128:256], False)

    @pl.when(odd == 0)
    def _():
        for s in range(8):
            strips_ref[s] = pack_pair(x_ref[s, :, 0:128], x_ref[s + 8, :, 0:128], True)

    for copy in copies[1:]:
        copy.wait()
    turned[...] = jnp.zeros((128, 128), F32)
    turned[0:48, 0:49] = dw_ref[...]
    taps_ref[...] = lax.dot_general(
        turned[...].T[0:56], spread[...], NN,
        precision=lax.Precision.HIGHEST, preferred_element_type=F32,
    )
    scale = column(scale_ref[...])
    small[...] = jnp.zeros((16, 256), F32)
    small[0:1, 0:192] = b_ref[...].astype(F32).reshape(1, 192)
    small[1:2, 0:48] = gain_ref[...].astype(F32)
    tails = []
    for ref in (in_ref, w_out_ref):
        tails.append(pack_tail(ref[:, 128:192].astype(F32)).astype(BF16))
    for j, out in enumerate(outs):
        first = 2 * ((mine + j) & 3)
        for i in range(2):
            out[48 * i : 48 * i + 48] = (cot_ref[first + i].astype(F32) * scale).astype(BF16)
        out[96:288, 0:128] = in_ref[:, 0:128]
        out[96:288, 128:256] = w_out_ref[:, 0:128]
        out[288:384, 0:128] = tails[0]
        out[288:384, 128:256] = tails[1]
        out[384:400] = small[...].astype(BF16)


def gather_tile(table, up_g, mid_g, down_g, t, center, entries):
    rows = pl.ds(48 * t, 48)
    mid_g[rows, 0:256] = table[center]
    mid_g[rows, 256:512] = table[entries[3]]
    mid_g[rows, 512:768] = table[entries[4]]
    for k in range(3):
        up_g[rows, 128 * k : 128 * k + 128] = table[entries[k], :, 128:256]
        down_g[rows, 128 * k : 128 * k + 128] = table[entries[5 + k], :, 0:128]


def build_padded(pad, up_g, mid_g, down_g, maps):
    for cells, lo, hi in ((up_g, 0, 72), (mid_g, 72, 456), (down_g, 456, 528)):
        rows = dot(maps[lo:hi, 0 : cells.shape[1]], cells[...], NT)
        for block in range(3):
            pad[block, lo:hi] = rows[:, 128 * block : 128 * block + 128]


def convolve(pad, taps, result, flip):
    def lane_block(block, carry):
        lanes = pl.ds(pl.multiple_of(block * 128, 128), 128)
        acc = [jnp.zeros((16, 128), F32) for _ in range(16)]
        for b in range(7):
            weights = []
            for a in range(7):
                tap = 7 * a + b
                weights.append(taps[pl.ds(48 - tap if flip else tap, 1), lanes])
            for r in range(22):
                line = pad[block, pl.ds(WIDE * r + b, 16)]
                for a in range(7):
                    i = r - a
                    if 0 <= i < 16:
                        acc[i] = acc[i] + line * weights[a]
        for i in range(16):
            result[pl.ds(16 * i, 16), lanes] = acc[i]
        return carry

    lax.fori_loop(0, 3, lane_block, 0)


def fill_edges(table, near_ref, far_ref, below):
    odd = lax.axis_index("core")

    def fill(upper, lower):
        for s in range(8):
            up = upper[s]
            table[s, :, 128:256] = up
            table[s + 8, :, 128:256] = swap_halves(up).astype(BF16)
            down = lower[s]
            table[below + s, :, 0:128] = down
            table[below + 8 + s, :, 0:128] = swap_halves(down).astype(BF16)

    @pl.when(odd == 0)
    def _():
        fill(near_ref, far_ref)

    @pl.when(odd == 1)
    def _():
        fill(far_ref, near_ref)


OFFSETS = (-17, -16, -15, -1, 1, 15, 16, 17)


def mix_kernel(
    own_slots, par_slots, adj, x_ref, par_ref, near_ref, far_ref, taps, maps,
    owned_ref, pad_out, m0, m1, m2, m3,
    place, table, up_g, mid_g, down_g, pad, result, flat,
):
    me = my_owner()
    odd = lax.axis_index("core")
    mine = lax.axis_index("chan")
    base = 8 * me
    for t in range(8):
        place[t] = 0
    for s in range(16):
        for slots, row in ((own_slots, odd), (par_slots, 1 - odd)):
            t = slots[s] - base

            @pl.when((t >= 0) & (t < 8))
            def _():
                place[t] = 16 + 16 * row + s

    table[pl.ds(16 + 16 * odd, 16)] = x_ref[...]
    table[pl.ds(32 - 16 * odd, 16)] = par_ref[...]
    table[64] = jnp.zeros((48, 256), BF16)

    fill_edges(table, near_ref, far_ref, 48)
    for t in range(8):
        center = place[t]
        entries = [jnp.where(adj[t, k] < 512, center + OFFSETS[k], 64) for k in range(8)]
        gather_tile(table, up_g, mid_g, down_g, t, center, entries)
    owned_ref[...] = mid_g[:, 0:256].reshape(8, 48, 256)
    build_padded(pad, up_g, mid_g, down_g, maps)
    pad_out[...] = pad[...].astype(BF16)
    convolve(pad, taps, result, False)
    flat[...] = result[...].T.astype(BF16).reshape(8, 48, 256)
    for j, out in enumerate((m0, m1, m2, m3)):
        first = 2 * ((mine + j) & 3)
        out[0] = flat[first]
        out[1] = flat[first + 1]


def turn_kernel(p0, p1, p2, p3, w_in, w_out, in_t, out_t, bias, gain, dbranch):
    mine = lax.axis_index("chan")
    unit = eye(192)
    for j, ref in enumerate((p0, p1, p2, p3)):
        a = (mine + 4 - j) & 3
        for i in range(2):
            dbranch[a, :, 256 * i : 256 * i + 256] = ref[48 * i : 48 * i + 48]
        for full, turned, lanes in ((w_in, in_t, 0), (w_out, out_t, 128)):
            tail = ref[288:384, lanes : lanes + 128].astype(F32)
            whole = jnp.concatenate(
                [
                    ref[96:288, lanes : lanes + 128].astype(F32),
                    unpack_tail(tail),
                ],
                axis=1,
            ).astype(BF16)
            full[j] = whole
            turned[j] = dot(unit, whole, NT).astype(BF16)
        cols = dot(unit, ref[384:400, 0:192], NT)
        bias[j] = jnp.broadcast_to(cols[:, 0:1], (192, 128))
        gain[a] = jnp.broadcast_to(cols[0:48, 1:2], (48, 128))


def across(col_block):
    return jnp.concatenate([col_block] * 4, axis=1)


def mlp_kernel(
    m0, m1, m2, m3, w_in, w_out, in_t, out_t, bias, gain, db_ref,
    g0, g1, g2, g3, keep_ref, give_ref, mixed_s, back_s, branch_s, halves,
):
    mine = lax.axis_index("chan")
    for j, m_ref in enumerate((m0, m1, m2, m3)):
        a = (mine + 4 - j) & 3
        for i in range(2):
            mixed_s[a, :, 256 * i : 256 * i + 256] = m_ref[i]
    mixed = mixed_s[...].reshape(192, 512).astype(F32)
    dbranch = db_ref[...].reshape(192, 512)
    mean = jnp.sum(mixed, axis=0, keepdims=True) / CHANNELS
    inv = lax.rsqrt(
        jnp.sum(mixed * mixed, axis=0, keepdims=True) / CHANNELS - mean * mean + EPSILON
    )
    x_hat = (mixed - mean) * inv
    gain_full = across(gain[...].reshape(192, 128))
    normed = (x_hat * gain_full).astype(BF16)
    branch = jnp.zeros((192, 512), F32)
    dnormed = jnp.zeros((192, 512), F32)
    for j in range(4):
        preact = dot(in_t[j], normed, NN) + across(bias[j])
        square = preact * preact
        tangent = jnp.tanh(GELU_SCALE * (preact + GELU_CUBIC * square * preact))
        half = 0.5 * (1.0 + tangent)
        act = (preact * half).astype(BF16)
        slope = half + 0.5 * preact * (1.0 - tangent * tangent) * (
            GELU_SCALE * (1.0 + 3.0 * GELU_CUBIC * square)
        )
        branch = branch + dot(out_t[j], act, NN)
        pre_grad = (dot(w_out[j], dbranch, NN) * slope).astype(BF16)
        dnormed = dnormed + dot(w_in[j], pre_grad, NN)
        for side, grad in enumerate((dot(normed, pre_grad, NT), dot(act, dbranch, NT))):
            halves[side, j, 0:192] = grad[:, 0:128].astype(BF16)
            halves[side, j, 192:288] = pack_tail(grad[:, 128:192]).astype(BF16)
    core = lax.axis_index("core")
    keep_ref[...] = halves[core]
    give_ref[...] = halves[1 - core]
    xhat_grad = dnormed * gain_full
    first = jnp.sum(xhat_grad, axis=0, keepdims=True) / CHANNELS
    second = jnp.sum(xhat_grad * x_hat, axis=0, keepdims=True) / CHANNELS
    dmixed = (inv * (xhat_grad - first - x_hat * second)).astype(BF16)
    back_s[...] = dmixed.reshape(4, 48, 512)
    branch_s[...] = branch.astype(BF16).reshape(4, 48, 512)
    for j, g_ref in enumerate((g0, g1, g2, g3)):
        a = (mine + j) & 3
        for i in range(2):
            g_ref[48 * i : 48 * i + 48] = back_s[a, :, 256 * i : 256 * i + 256]
            g_ref[96 + 48 * i : 144 + 48 * i] = branch_s[a, :, 256 * i : 256 * i + 256]


def land_kernel(g0, g1, g2, g3, grad_ref):
    mine = lax.axis_index("chan")
    for j, ref in enumerate((g0, g1, g2, g3)):
        first = 2 * ((mine + 4 - j) & 3)
        for i in range(2):
            grad_ref[first + i] = ref[48 * i : 48 * i + 48]


def merge_kernel(keep_ref, got_ref, out_ref):
    mine = lax.axis_index("chan")
    for j in range(4):
        both = keep_ref[j].astype(F32) + got_ref[j].astype(F32)
        out_ref[(mine + 4 - j) & 3] = both.astype(BF16)


def taps_kernel(grad_ref, pad_ref, fold, out_ref, pad, grad_t, sums):
    pad[...] = pad_ref[...].astype(F32)
    grad_t[...] = grad_ref[...].reshape(384, 256).astype(F32).T
    sums[...] = jnp.zeros((64, 384), F32)

    def lane_block(block, carry):
        lanes = pl.ds(pl.multiple_of(block * 128, 128), 128)
        lines = [grad_t[pl.ds(16 * i, 16), lanes] for i in range(16)]
        for b in range(7):
            acc = [jnp.zeros((16, 128), F32) for _ in range(7)]
            for r in range(22):
                line = pad[block, pl.ds(WIDE * r + b, 16)]
                for a in range(7):
                    i = r - a
                    if 0 <= i < 16:
                        acc[a] = acc[a] + line * lines[i]
            for a in range(7):
                sums[pl.ds(7 * a + b, 1), lanes] = jnp.sum(acc[a], axis=0, keepdims=True)
        return carry

    lax.fori_loop(0, 3, lane_block, 0)
    out_ref[...] = lax.dot_general(
        sums[...], fold[...], NT, precision=lax.Precision.HIGHEST, preferred_element_type=F32
    )


def pieces_kernel(parts_ref, taps_ref, out_ref, total, rows):
    total[0:288] = jnp.sum(parts_ref[...].astype(F32), axis=0)
    total[288:352] = taps_ref[...]
    rows[...] = jnp.zeros((32, 16, 128), F32)
    for q in range(11):
        rows[:, q, :] = total[32 * q : 32 * q + 32]
    out_ref[...] = rows[...].astype(BF16)


def edges_kernel(own_ref, par_ref, edge_ref):
    odd = lax.axis_index("core")

    @pl.when(odd == 1)
    def _():
        for t in range(8):
            edge_ref[t] = pack_pair(par_ref[t, :, 128:256], own_ref[t, :, 128:256], False)

    @pl.when(odd == 0)
    def _():
        for t in range(8):
            edge_ref[t] = pack_pair(own_ref[t, :, 0:128], par_ref[t, :, 0:128], True)


def total_kernel(factor, in_ref, out_ref):
    total = jnp.sum(in_ref[...].astype(F32), axis=0, keepdims=True) * factor
    out_ref[...] = jnp.broadcast_to(total, in_ref.shape).astype(out_ref.dtype)


def finish_kernel(in_ref, other_ref, dw_ref, w1_ref, w2_ref, rows, flat):
    core = lax.axis_index("core")
    for ref, side in ((in_ref, core), (other_ref, 1 - core)):
        rows[...] = ref[...].astype(F32)
        for q in range(11):
            flat[side, 32 * q : 32 * q + 32] = rows[:, q, :]
    for out, side in ((w1_ref, 0), (w2_ref, 1)):
        out[:, 0:128] = flat[side, 0:192]
        out[:, 128:192] = unpack_tail(flat[side, 192:288])
    dw = flat[0, 288:352] + flat[1, 288:352]
    dw_ref[...] = dw.T[0:48, 0:49]


def surround_kernel(
    adj, grad_ref, par_ref, near_ref, far_ref, maps, pad, table, up_g, mid_g, down_g
):
    me = my_owner()
    odd = lax.axis_index("core")
    start = 16 * (me // 2) - 16
    table[pl.ds(16 + 8 * odd, 8)] = grad_ref[...]
    table[pl.ds(24 - 8 * odd, 8)] = par_ref[...]
    table[48] = jnp.zeros((48, 256), BF16)
    fill_edges(table, near_ref, far_ref, 32)
    for t in range(8):
        center = 16 + 8 * odd + t
        entries = [jnp.where(adj[t, k] < 512, adj[t, k] - start, 48) for k in range(8)]
        gather_tile(table, up_g, mid_g, down_g, t, center, entries)
    build_padded(pad, up_g, mid_g, down_g, maps)


def unmix_kernel(
    pad, cot_ref, taps, owned_ref, scale_ref, r0, r1, r2, r3, out_ref, gin_ref, result
):
    mine = lax.axis_index("chan")
    convolve(pad, taps, result, True)
    back = result[...].T.reshape(8, 48, 256)
    gin_ref[...] = (cot_ref[...].astype(F32) + back).astype(BF16)
    scale = column(scale_ref[...])
    for j, ref in enumerate((r0, r1, r2, r3)):
        first = 2 * ((mine + 4 - j) & 3)
        for i in range(2):
            out_ref[first + i] = (
                owned_ref[first + i].astype(F32)
                + scale * ref[96 + 48 * i : 144 + 48 * i].astype(F32)
            ).astype(BF16)


def call(kernel, shapes, scratch=(), smem=0, n_in=0, name=None, near=(), micros=None):
    vmem = pl.BlockSpec(memory_space=pltpu.VMEM)
    scalar = pl.BlockSpec(memory_space=pltpu.SMEM)
    many = isinstance(shapes, (list, tuple))

    inner = pl.pallas_call(
        kernel,
        out_shape=shapes,
        in_specs=[scalar] * smem + [vmem] * (n_in - smem),
        out_specs=[vmem] * len(shapes) if many else vmem,
        scratch_shapes=list(scratch),
        compiler_params=pltpu.CompilerParams(vmem_limit_bytes=24 << 20),
        cost_estimate=None if micros is None else pl.CostEstimate(
            flops=int(micros * 1e9), transcendentals=0, bytes_accessed=int(micros * 3.69e6)
        ),
        name=name,
    )

    def run(*args):
        return inner(
            *(
                pltpu.with_memory_space_constraint(a, pltpu.VMEM) if i in near else a
                for i, a in enumerate(args)
            )
        )

    return run


def shape(*dims, dtype=BF16):
    return jax.ShapeDtypeStruct(dims, dtype)


def held(*dims, dtype=BF16):
    return pltpu.VMEM(dims, dtype)


def along_chan(values):
    got = [values[0]]
    for j in range(1, 4):
        got.append(lax.ppermute(values[j], "chan", [(i, (i + j) % 4) for i in range(4)]))
    return got


def body(
    x_scan, slot_owner, adjacency, cotangent, dw_weight, ln_gain, w_in, b_in, w_out, layer_scale
):
    devices = lax.axis_size("chip") * 2
    maps = jnp.asarray(placement_tables())
    fold_map = (np.arange(384)[:, None] % 48 == np.arange(128)[None, :]).astype(np.float32)
    spread_map = jnp.asarray(np.ascontiguousarray(fold_map.T))
    scale_row = layer_scale.reshape(1, 48)
    owners = ("chip", "core")

    def after(value, *first):
        return lax.optimization_barrier((value, first))[0]

    def partner(value):
        return lax.ppermute(value, "core", [(0, 1), (1, 0)])

    def next_chip(value):
        pairs = [(i, i + 1 if i & 1 else i - 1) for i in range(devices)]
        return lax.ppermute(value, owners, [p for p in pairs if 0 <= p[1] < devices])

    tile_chunk = held(2, 48, 256)
    par_x = partner(x_scan)
    par_slots = partner(slot_owner)
    opening = (
        x_scan, cotangent, scale_row, w_in, w_out, b_in, ln_gain.reshape(1, 48), dw_weight, spread_map
    )
    strips, *sends, taps, fold, own_x = pl.pallas_call(
        open_kernel,
        out_shape=[held(8, 48, 128)] + [held(400, 256)] * 4
        + [held(56, 384, dtype=F32), held(128, 384, dtype=F32), held(16, 48, 256)],
        in_specs=[pl.BlockSpec(memory_space=pltpu.HBM)] * 9,
        out_specs=[pl.BlockSpec(memory_space=pltpu.VMEM)] * 8,
        scratch_shapes=[pltpu.VMEM(v.shape, v.dtype) for v in opening[1:-1]]
        + [
            pltpu.VMEM((16, 256), F32),
            pltpu.VMEM((128, 128), F32),
            pltpu.SemaphoreType.DMA((9,)),
        ],
        compiler_params=pltpu.CompilerParams(vmem_limit_bytes=24 << 20),
        name="open",
    )(*(pltpu.with_memory_space_constraint(v, pltpu.HBM) for v in opening))
    near = next_chip(strips)
    far = partner(near)
    sends[1] = after(sends[1], near, par_slots)
    all_sends = along_chan(sends)

    grid_scratch = lambda entries: [
        pltpu.VMEM((entries, 48, 256), BF16),
        pltpu.VMEM((384, 384), BF16),
        pltpu.VMEM((384, 768), BF16),
        pltpu.VMEM((384, 384), BF16),
        pltpu.VMEM((3, 22 * WIDE, 128), F32),
        pltpu.VMEM((256, 384), F32),
    ]
    mix = call(
        mix_kernel,
        [shape(8, 48, 256), shape(3, 22 * WIDE, 128)] + [tile_chunk] * 4,
        scratch=[pltpu.SMEM((8,), jnp.int32)] + grid_scratch(65) + [pltpu.VMEM((8, 48, 256), BF16)],
        smem=3,
        n_in=9,
        name="mix",
        near=(3, 4, 5, 6, 7),
    )
    owned, padded, *mixed = mix(
        slot_owner, par_slots, adjacency, own_x, par_x, near, far, taps, maps
    )
    all_mixed = along_chan(mixed)

    square = held(4, 192, 192)
    turn = call(
        turn_kernel,
        [square] * 4
        + [held(4, 192, 128, dtype=F32), held(4, 48, 128, dtype=F32), held(4, 48, 512)],
        n_in=4,
        name="turn",
        near=(0, 1, 2, 3),
    )
    turned = turn(*after(all_sends, mixed[0]))

    *packets, keep, give = call(
        mlp_kernel,
        [held(192, 256)] * 4 + [held(4, 288, 128)] * 2,
        scratch=[pltpu.VMEM((4, 48, 512), BF16)] * 3 + [pltpu.VMEM((2, 4, 288, 128), BF16)],
        n_in=11,
        name="mlp",
        near=range(11),
    )(*all_mixed, *turned)
    all_back = along_chan(packets)
    merged = call(merge_kernel, held(4, 288, 128), n_in=2, name="merge", near=range(2))(
        keep, partner(give)
    )
    partials = lax.all_to_all(merged, "chan", 0, 0, tiled=True)
    grads = call(land_kernel, held(8, 48, 256), n_in=4, name="land", near=range(4))(*all_back)
    par_grads = partner(grads)
    tap_sums = call(
        taps_kernel,
        held(64, 128, dtype=F32),
        scratch=[
            pltpu.VMEM((3, 22 * WIDE, 128), F32),
            pltpu.VMEM((256, 384), F32),
            pltpu.VMEM((64, 384), F32),
        ],
        n_in=3,
        name="tap_sums",
        near=(0, 2),
    )(grads, padded, fold)
    edges = call(edges_kernel, held(8, 48, 128), n_in=2, name="edges", near=(0, 1))(
        after(grads, tap_sums), par_grads
    )
    near_grads = next_chip(edges)
    pieces = call(
        pieces_kernel,
        held(32, 16, 128),
        scratch=[pltpu.VMEM((352, 128), F32), pltpu.VMEM((32, 16, 128), F32)],
        n_in=2,
        name="pieces",
        near=range(2),
    )(partials, tap_sums)
    arrived = lax.all_to_all(after(pieces, edges), "chip", 0, 0, tiled=True)

    factor = 1.0 / math.sqrt(adjacency.shape[0] * devices * PIX)
    far_grads = partner(near_grads)
    surrounded = call(
        surround_kernel,
        held(3, 22 * WIDE, 128, dtype=F32),
        scratch=grid_scratch(49)[0:4],
        smem=1,
        n_in=6,
        name="surround",
        near=(1, 2, 3, 4),
        micros=0.7,
    )(adjacency, grads, par_grads, near_grads, far_grads, maps)
    arrived, surrounded = lax.optimization_barrier((arrived, surrounded))
    totals = call(
        functools.partial(total_kernel, factor), held(32, 16, 128), n_in=1, name="totals", near=(0,)
    )(arrived)
    spread = lax.all_to_all(totals, "chip", 0, 0, tiled=True)

    output, grad_in = call(
        unmix_kernel,
        [shape(8, 48, 256), shape(8, 48, 256)],
        scratch=[pltpu.VMEM((256, 384), F32)],
        n_in=9,
        name="unmix",
        near=(0, 5, 6, 7, 8),
    )(surrounded, cotangent, taps, owned, after(scale_row, totals), *all_back)
    spread = after(spread, output)
    grad_dw, grad_w1, grad_w2 = call(
        finish_kernel,
        [shape(48, 49, dtype=F32), shape(192, 192, dtype=F32), shape(192, 192, dtype=F32)],
        scratch=[pltpu.VMEM((32, 16, 128), F32), pltpu.VMEM((2, 352, 128), F32)],
        n_in=2,
        name="finish",
        near=(0, 1),
    )(spread, partner(spread))
    return (output, grad_in, grad_dw, grad_w1, grad_w2)


def solution(mesh):
    chips, chan = mesh.devices.shape[0] // 2, mesh.devices.shape[1]
    parts = Mesh(mesh.devices.reshape(chips, 2, chan), ("chip", "core", "chan"))
    tiles = ("chip", "core")
    in_specs = (
        P(tiles, "chan", None),
        P(tiles),
        P(tiles, None),
        P(tiles, "chan", None),
        P("chan", None),
        P("chan"),
        P(None, "chan"),
        P("chan"),
        P("chan", None),
        P("chan"),
    )
    out_specs = (
        P(tiles, "chan", None),
        P(tiles, "chan", None),
        P("chan", None),
        P(None, "chan"),
        P("chan", None),
    )
    return jax.shard_map(body, mesh=parts, in_specs=in_specs, out_specs=out_specs, check_vma=False)
```

```python
import functools
import math

import jax
import jax.numpy as jnp
import numpy as np
from jax import lax
from jax.experimental import pallas as pl
from jax.experimental.pallas import tpu as pltpu
from jax.sharding import Mesh
from jax.sharding import PartitionSpec as P

CHANNELS = 192
SIDE = 16
PIX = 256
WIDE = 24
EPSILON = 1e-06
GELU_SCALE = 0.7978845608
GELU_CUBIC = 0.044715

F32 = jnp.float32
BF16 = jnp.bfloat16
NT = (((1,), (1,)), ((), ()))
NN = (((1,), (0,)), ((), ()))


def dot(a, b, dims):
    return lax.dot_general(a, b, dims, preferred_element_type=F32)


def placement_tables():
    maps = np.zeros((22 * WIDE, 768), np.float32)
    up, mid, down = maps[0:72], maps[72:456], maps[456:528]
    for j in range(22):
        if j < 3:
            side, col = 0, 13 + j
        elif j < 19:
            side, col = 1, j - 3
        else:
            side, col = 2, j - 19
        for i in range(3):
            up[i * WIDE + j, 128 * side + 16 * (13 + i) + col - 128] = 1
            down[i * WIDE + j, 128 * side + 16 * i + col] = 1
        for i in range(16):
            block = (1, 0, 2)[side]
            mid[i * WIDE + j, 256 * block + 16 * i + col] = 1
    return maps.astype(jnp.bfloat16)


def column(row):
    n = row.shape[1]
    same = lax.broadcasted_iota(jnp.int32, (n, n), 0) == lax.broadcasted_iota(jnp.int32, (n, n), 1)
    return jnp.sum(jnp.where(same, jnp.broadcast_to(row, (n, n)), 0.0), axis=1, keepdims=True)


def eye(n):
    same = lax.broadcasted_iota(jnp.int32, (n, n), 0) == lax.broadcasted_iota(jnp.int32, (n, n), 1)
    return same.astype(F32).astype(BF16)


def swap_halves(value):
    return pltpu.roll(value.astype(F32), 64, 1)


def low_lanes(shape):
    return lax.broadcasted_iota(jnp.int32, shape, 1) < 64


def pack_pair(natural, other, natural_low):
    shape = natural.shape
    keep = low_lanes(shape) if natural_low else jnp.logical_not(low_lanes(shape))
    return jnp.where(keep, natural.astype(F32), swap_halves(other)).astype(BF16)


def my_owner():
    return 2 * lax.axis_index("chip") + lax.axis_index("core")


def pack_tail(value):
    return jnp.concatenate([value[0:96], value[96:192]], axis=1)


def unpack_tail(value):
    return jnp.concatenate([value[:, 0:64], value[:, 64:128]], axis=0)


def open_kernel(
    x_hbm, cot_hbm, scale_hbm, in_hbm, w_out_hbm, b_hbm, gain_hbm, dw_hbm, spread_hbm,
    strips_ref, s0, s1, s2, s3, taps_ref, spread, x_ref,
    cot_ref, scale_ref, in_ref, w_out_ref, b_ref, gain_ref, dw_ref, small, turned, sems,
):
    outs = (s0, s1, s2, s3)
    mine = lax.axis_index("chan")
    odd = lax.axis_index("core")
    sources = (x_hbm, cot_hbm, scale_hbm, in_hbm, w_out_hbm, b_hbm, gain_hbm, dw_hbm, spread_hbm)
    targets = (x_ref, cot_ref, scale_ref, in_ref, w_out_ref, b_ref, gain_ref, dw_ref, spread)
    copies = [
        pltpu.make_async_copy(source, target, sems.at[n])
        for n, (source, target) in enumerate(zip(sources, targets))
    ]
    for copy in copies:
        copy.start()
    copies[0].wait()

    @pl.when(odd == 1)
    def _():
        for s in range(8):
            strips_ref[s] = pack_pair(x_ref[s, :, 128:256], x_ref[s + 8, :, 128:256], False)

    @pl.when(odd == 0)
    def _():
        for s in range(8):
            strips_ref[s] = pack_pair(x_ref[s, :, 0:128], x_ref[s + 8, :, 0:128], True)

    for copy in copies[1:]:
        copy.wait()
    turned[...] = jnp.zeros((128, 128), F32)
    turned[0:48, 0:49] = dw_ref[...]
    taps_ref[...] = lax.dot_general(
        turned[...].T[0:56], spread[...], NN,
        precision=lax.Precision.HIGHEST, preferred_element_type=F32,
    )
    scale = column(scale_ref[...])
    small[...] = jnp.zeros((16, 256), F32)
    small[0:1, 0:192] = b_ref[...].astype(F32).reshape(1, 192)
    small[1:2, 0:48] = gain_ref[...].astype(F32)
    tails = []
    for ref in (in_ref, w_out_ref):
        tails.append(pack_tail(ref[:, 128:192].astype(F32)).astype(BF16))
    for j, out in enumerate(outs):
        first = 2 * ((mine + j) & 3)
        for i in range(2):
            out[48 * i : 48 * i + 48] = (cot_ref[first + i].astype(F32) * scale).astype(BF16)
        out[96:288, 0:128] = in_ref[:, 0:128]
        out[96:288, 128:256] = w_out_ref[:, 0:128]
        out[288:384, 0:128] = tails[0]
        out[288:384, 128:256] = tails[1]
        out[384:400] = small[...].astype(BF16)


def gather_tile(table, up_g, mid_g, down_g, t, center, entries):
    rows = pl.ds(48 * t, 48)
    mid_g[rows, 0:256] = table[center]
    mid_g[rows, 256:512] = table[entries[3]]
    mid_g[rows, 512:768] = table[entries[4]]
    for k in range(3):
        up_g[rows, 128 * k : 128 * k + 128] = table[entries[k], :, 128:256]
        down_g[rows, 128 * k : 128 * k + 128] = table[entries[5 + k], :, 0:128]


def build_padded(pad, up_g, mid_g, down_g, maps):
    for cells, lo, hi in ((up_g, 0, 72), (mid_g, 72, 456), (down_g, 456, 528)):
        rows = dot(maps[lo:hi, 0 : cells.shape[1]], cells[...], NT)
        for block in range(3):
            pad[block, lo:hi] = rows[:, 128 * block : 128 * block + 128]


def convolve(pad, taps, result, flip):
    def lane_block(block, carry):
        lanes = pl.ds(pl.multiple_of(block * 128, 128), 128)
        acc = [jnp.zeros((16, 128), F32) for _ in range(16)]
        for b in range(7):
            weights = []
            for a in range(7):
                tap = 7 * a + b
                weights.append(taps[pl.ds(48 - tap if flip else tap, 1), lanes])
            for r in range(22):
                line = pad[block, pl.ds(WIDE * r + b, 16)]
                for a in range(7):
                    i = r - a
                    if 0 <= i < 16:
                        acc[i] = acc[i] + line * weights[a]
        for i in range(16):
            result[pl.ds(16 * i, 16), lanes] = acc[i]
        return carry

    lax.fori_loop(0, 3, lane_block, 0)


def fill_edges(table, near_ref, far_ref, below):
    odd = lax.axis_index("core")

    def fill(upper, lower):
        for s in range(8):
            up = upper[s]
            table[s, :, 128:256] = up
            table[s + 8, :, 128:256] = swap_halves(up).astype(BF16)
            down = lower[s]
            table[below + s, :, 0:128] = down
            table[below + 8 + s, :, 0:128] = swap_halves(down).astype(BF16)

    @pl.when(odd == 0)
    def _():
        fill(near_ref, far_ref)

    @pl.when(odd == 1)
    def _():
        fill(far_ref, near_ref)


OFFSETS = (-17, -16, -15, -1, 1, 15, 16, 17)


def mix_kernel(
    own_slots, par_slots, adj, x_ref, par_ref, near_ref, far_ref, taps, maps,
    owned_ref, pad_out, m0, m1, m2, m3,
    place, table, up_g, mid_g, down_g, pad, result, flat,
):
    me = my_owner()
    odd = lax.axis_index("core")
    mine = lax.axis_index("chan")
    base = 8 * me
    for t in range(8):
        place[t] = 0
    for s in range(16):
        for slots, row in ((own_slots, odd), (par_slots, 1 - odd)):
            t = slots[s] - base

            @pl.when((t >= 0) & (t < 8))
            def _():
                place[t] = 16 + 16 * row + s

    table[pl.ds(16 + 16 * odd, 16)] = x_ref[...]
    table[pl.ds(32 - 16 * odd, 16)] = par_ref[...]
    table[64] = jnp.zeros((48, 256), BF16)

    fill_edges(table, near_ref, far_ref, 48)
    for t in range(8):
        center = place[t]
        entries = [jnp.where(adj[t, k] < 512, center + OFFSETS[k], 64) for k in range(8)]
        gather_tile(table, up_g, mid_g, down_g, t, center, entries)
    owned_ref[...] = mid_g[:, 0:256].reshape(8, 48, 256)
    build_padded(pad, up_g, mid_g, down_g, maps)
    pad_out[...] = pad[...].astype(BF16)
    convolve(pad, taps, result, False)
    flat[...] = result[...].T.astype(BF16).reshape(8, 48, 256)
    for j, out in enumerate((m0, m1, m2, m3)):
        first = 2 * ((mine + j) & 3)
        out[0] = flat[first]
        out[1] = flat[first + 1]


def turn_kernel(p0, p1, p2, p3, w_in, w_out, in_t, out_t, bias, gain, dbranch):
    mine = lax.axis_index("chan")
    unit = eye(192)
    for j, ref in enumerate((p0, p1, p2, p3)):
        a = (mine + 4 - j) & 3
        for i in range(2):
            dbranch[a, :, 256 * i : 256 * i + 256] = ref[48 * i : 48 * i + 48]
        for full, turned, lanes in ((w_in, in_t, 0), (w_out, out_t, 128)):
            tail = ref[288:384, lanes : lanes + 128].astype(F32)
            whole = jnp.concatenate(
                [
                    ref[96:288, lanes : lanes + 128].astype(F32),
                    unpack_tail(tail),
                ],
                axis=1,
            ).astype(BF16)
            full[j] = whole
            turned[j] = dot(unit, whole, NT).astype(BF16)
        cols = dot(unit, ref[384:400, 0:192], NT)
        bias[j] = jnp.broadcast_to(cols[:, 0:1], (192, 128))
        gain[a] = jnp.broadcast_to(cols[0:48, 1:2], (48, 128))


def across(col_block):
    return jnp.concatenate([col_block] * 4, axis=1)


def mlp_kernel(
    m0, m1, m2, m3, w_in, w_out, in_t, out_t, bias, gain, db_ref,
    g0, g1, g2, g3, r0, r1, r2, r3, keep_ref, give_ref, mixed_s, back_s, branch_s, halves,
):
    mine = lax.axis_index("chan")
    for j, m_ref in enumerate((m0, m1, m2, m3)):
        a = (mine + 4 - j) & 3
        for i in range(2):
            mixed_s[a, :, 256 * i : 256 * i + 256] = m_ref[i]
    mixed = mixed_s[...].reshape(192, 512).astype(F32)
    dbranch = db_ref[...].reshape(192, 512)
    mean = jnp.sum(mixed, axis=0, keepdims=True) / CHANNELS
    inv = lax.rsqrt(
        jnp.sum(mixed * mixed, axis=0, keepdims=True) / CHANNELS - mean * mean + EPSILON
    )
    x_hat = (mixed - mean) * inv
    gain_full = across(gain[...].reshape(192, 128))
    normed = (x_hat * gain_full).astype(BF16)
    branch = jnp.zeros((192, 512), F32)
    dnormed = jnp.zeros((192, 512), F32)
    for j in range(4):
        preact = dot(in_t[j], normed, NN) + across(bias[j])
        square = preact * preact
        tangent = jnp.tanh(GELU_SCALE * (preact + GELU_CUBIC * square * preact))
        half = 0.5 * (1.0 + tangent)
        act = (preact * half).astype(BF16)
        slope = half + 0.5 * preact * (1.0 - tangent * tangent) * (
            GELU_SCALE * (1.0 + 3.0 * GELU_CUBIC * square)
        )
        branch = branch + dot(out_t[j], act, NN)
        pre_grad = (dot(w_out[j], dbranch, NN) * slope).astype(BF16)
        dnormed = dnormed + dot(w_in[j], pre_grad, NN)
        for side, grad in enumerate((dot(normed, pre_grad, NT), dot(act, dbranch, NT))):
            halves[side, j, 0:192] = grad[:, 0:128].astype(BF16)
            halves[side, j, 192:288] = pack_tail(grad[:, 128:192]).astype(BF16)
    core = lax.axis_index("core")
    keep_ref[...] = halves[core]
    give_ref[...] = halves[1 - core]
    xhat_grad = dnormed * gain_full
    first = jnp.sum(xhat_grad, axis=0, keepdims=True) / CHANNELS
    second = jnp.sum(xhat_grad * x_hat, axis=0, keepdims=True) / CHANNELS
    dmixed = (inv * (xhat_grad - first - x_hat * second)).astype(BF16)
    back_s[...] = dmixed.reshape(4, 48, 512)
    branch_s[...] = branch.astype(BF16).reshape(4, 48, 512)
    for j, (g_ref, r_ref) in enumerate(((g0, r0), (g1, r1), (g2, r2), (g3, r3))):
        a = (mine + j) & 3
        for i in range(2):
            g_ref[48 * i : 48 * i + 48] = back_s[a, :, 256 * i : 256 * i + 256]
            r_ref[48 * i : 48 * i + 48] = branch_s[a, :, 256 * i : 256 * i + 256]


def land_kernel(g0, g1, g2, g3, grad_ref):
    mine = lax.axis_index("chan")
    for j, ref in enumerate((g0, g1, g2, g3)):
        first = 2 * ((mine + 4 - j) & 3)
        for i in range(2):
            grad_ref[first + i] = ref[48 * i : 48 * i + 48]


def merge_kernel(keep_ref, got_ref, out_ref):
    mine = lax.axis_index("chan")
    for j in range(4):
        both = keep_ref[j].astype(F32) + got_ref[j].astype(F32)
        out_ref[(mine + 4 - j) & 3] = both.astype(BF16)


def taps_kernel(grad_ref, pad_ref, fold, out_ref, pad, grad_t, sums):
    pad[...] = pad_ref[...].astype(F32)
    grad_t[...] = grad_ref[...].reshape(384, 256).astype(F32).T
    sums[...] = jnp.zeros((64, 384), F32)

    def lane_block(block, carry):
        lanes = pl.ds(pl.multiple_of(block * 128, 128), 128)
        lines = [grad_t[pl.ds(16 * i, 16), lanes] for i in range(16)]
        for b in range(7):
            acc = [jnp.zeros((16, 128), F32) for _ in range(7)]
            for r in range(22):
                line = pad[block, pl.ds(WIDE * r + b, 16)]
                for a in range(7):
                    i = r - a
                    if 0 <= i < 16:
                        acc[a] = acc[a] + line * lines[i]
            for a in range(7):
                sums[pl.ds(7 * a + b, 1), lanes] = jnp.sum(acc[a], axis=0, keepdims=True)
        return carry

    lax.fori_loop(0, 3, lane_block, 0)
    out_ref[...] = lax.dot_general(
        sums[...], fold[...], NT, precision=lax.Precision.HIGHEST, preferred_element_type=F32
    )


def pieces_kernel(parts_ref, taps_ref, out_ref, total, rows):
    total[0:288] = jnp.sum(parts_ref[...].astype(F32), axis=0)
    total[288:352] = taps_ref[...]
    rows[...] = jnp.zeros((32, 16, 128), F32)
    for q in range(11):
        rows[:, q, :] = total[32 * q : 32 * q + 32]
    out_ref[...] = rows[...].astype(BF16)


def edges_kernel(own_ref, par_ref, edge_ref):
    odd = lax.axis_index("core")

    @pl.when(odd == 1)
    def _():
        for t in range(8):
            edge_ref[t] = pack_pair(par_ref[t, :, 128:256], own_ref[t, :, 128:256], False)

    @pl.when(odd == 0)
    def _():
        for t in range(8):
            edge_ref[t] = pack_pair(own_ref[t, :, 0:128], par_ref[t, :, 0:128], True)


def total_kernel(factor, in_ref, out_ref):
    total = jnp.sum(in_ref[...].astype(F32), axis=0, keepdims=True) * factor
    out_ref[...] = jnp.broadcast_to(total, in_ref.shape).astype(out_ref.dtype)


def finish_kernel(in_ref, other_ref, dw_ref, w1_ref, w2_ref, rows, flat):
    core = lax.axis_index("core")
    for ref, side in ((in_ref, core), (other_ref, 1 - core)):
        rows[...] = ref[...].astype(F32)
        for q in range(11):
            flat[side, 32 * q : 32 * q + 32] = rows[:, q, :]
    for out, side in ((w1_ref, 0), (w2_ref, 1)):
        out[:, 0:128] = flat[side, 0:192]
        out[:, 128:192] = unpack_tail(flat[side, 192:288])
    dw = flat[0, 288:352] + flat[1, 288:352]
    dw_ref[...] = dw.T[0:48, 0:49]


def surround_kernel(
    adj, grad_ref, par_ref, near_ref, far_ref, maps, pad, table, up_g, mid_g, down_g
):
    me = my_owner()
    odd = lax.axis_index("core")
    start = 16 * (me // 2) - 16
    table[pl.ds(16 + 8 * odd, 8)] = grad_ref[...]
    table[pl.ds(24 - 8 * odd, 8)] = par_ref[...]
    table[48] = jnp.zeros((48, 256), BF16)
    fill_edges(table, near_ref, far_ref, 32)
    for t in range(8):
        center = 16 + 8 * odd + t
        entries = [jnp.where(adj[t, k] < 512, adj[t, k] - start, 48) for k in range(8)]
        gather_tile(table, up_g, mid_g, down_g, t, center, entries)
    build_padded(pad, up_g, mid_g, down_g, maps)


def unmix_kernel(
    pad, cot_ref, taps, owned_ref, scale_ref, r0, r1, r2, r3, out_ref, gin_ref, result
):
    mine = lax.axis_index("chan")
    convolve(pad, taps, result, True)
    back = result[...].T.reshape(8, 48, 256)
    gin_ref[...] = (cot_ref[...].astype(F32) + back).astype(BF16)
    scale = column(scale_ref[...])
    for j, ref in enumerate((r0, r1, r2, r3)):
        first = 2 * ((mine + 4 - j) & 3)
        for i in range(2):
            out_ref[first + i] = (
                owned_ref[first + i].astype(F32)
                + scale * ref[48 * i : 48 * i + 48].astype(F32)
            ).astype(BF16)


def call(kernel, shapes, scratch=(), smem=0, n_in=0, name=None, near=(), micros=None):
    vmem = pl.BlockSpec(memory_space=pltpu.VMEM)
    scalar = pl.BlockSpec(memory_space=pltpu.SMEM)
    many = isinstance(shapes, (list, tuple))

    inner = pl.pallas_call(
        kernel,
        out_shape=shapes,
        in_specs=[scalar] * smem + [vmem] * (n_in - smem),
        out_specs=[vmem] * len(shapes) if many else vmem,
        scratch_shapes=list(scratch),
        compiler_params=pltpu.CompilerParams(vmem_limit_bytes=24 << 20),
        cost_estimate=None if micros is None else pl.CostEstimate(
            flops=int(micros * 1e9), transcendentals=0, bytes_accessed=int(micros * 3.69e6)
        ),
        name=name,
    )

    def run(*args):
        return inner(
            *(
                pltpu.with_memory_space_constraint(a, pltpu.VMEM) if i in near else a
                for i, a in enumerate(args)
            )
        )

    return run


def shape(*dims, dtype=BF16):
    return jax.ShapeDtypeStruct(dims, dtype)


def held(*dims, dtype=BF16):
    return pltpu.VMEM(dims, dtype)


def along_chan(values):
    got = [values[0]]
    for j in range(1, 4):
        got.append(lax.ppermute(values[j], "chan", [(i, (i + j) % 4) for i in range(4)]))
    return got


def body(
    x_scan, slot_owner, adjacency, cotangent, dw_weight, ln_gain, w_in, b_in, w_out, layer_scale
):
    devices = lax.axis_size("chip") * 2
    maps = jnp.asarray(placement_tables())
    fold_map = (np.arange(384)[:, None] % 48 == np.arange(128)[None, :]).astype(np.float32)
    spread_map = jnp.asarray(np.ascontiguousarray(fold_map.T))
    scale_row = layer_scale.reshape(1, 48)
    owners = ("chip", "core")

    def after(value, *first):
        return lax.optimization_barrier((value, first))[0]

    def partner(value):
        return lax.ppermute(value, "core", [(0, 1), (1, 0)])

    def next_chip(value):
        pairs = [(i, i + 1 if i & 1 else i - 1) for i in range(devices)]
        return lax.ppermute(value, owners, [p for p in pairs if 0 <= p[1] < devices])

    tile_chunk = held(2, 48, 256)
    par_x = partner(x_scan)
    par_slots = partner(slot_owner)
    opening = (
        x_scan, cotangent, scale_row, w_in, w_out, b_in, ln_gain.reshape(1, 48), dw_weight, spread_map
    )
    strips, *sends, taps, fold, own_x = pl.pallas_call(
        open_kernel,
        out_shape=[held(8, 48, 128)] + [held(400, 256)] * 4
        + [held(56, 384, dtype=F32), held(128, 384, dtype=F32), held(16, 48, 256)],
        in_specs=[pl.BlockSpec(memory_space=pltpu.HBM)] * 9,
        out_specs=[pl.BlockSpec(memory_space=pltpu.VMEM)] * 8,
        scratch_shapes=[pltpu.VMEM(v.shape, v.dtype) for v in opening[1:-1]]
        + [
            pltpu.VMEM((16, 256), F32),
            pltpu.VMEM((128, 128), F32),
            pltpu.SemaphoreType.DMA((9,)),
        ],
        compiler_params=pltpu.CompilerParams(vmem_limit_bytes=24 << 20),
        name="open",
    )(*(pltpu.with_memory_space_constraint(v, pltpu.HBM) for v in opening))
    near = next_chip(strips)
    far = partner(near)
    sends[1] = after(sends[1], near, par_slots)
    all_sends = along_chan(sends)

    grid_scratch = lambda entries: [
        pltpu.VMEM((entries, 48, 256), BF16),
        pltpu.VMEM((384, 384), BF16),
        pltpu.VMEM((384, 768), BF16),
        pltpu.VMEM((384, 384), BF16),
        pltpu.VMEM((3, 22 * WIDE, 128), F32),
        pltpu.VMEM((256, 384), F32),
    ]
    mix = call(
        mix_kernel,
        [shape(8, 48, 256), shape(3, 22 * WIDE, 128)] + [tile_chunk] * 4,
        scratch=[pltpu.SMEM((8,), jnp.int32)] + grid_scratch(65) + [pltpu.VMEM((8, 48, 256), BF16)],
        smem=3,
        n_in=9,
        name="mix",
        near=(3, 4, 5, 6, 7),
    )
    owned, padded, *mixed = mix(
        slot_owner, par_slots, adjacency, own_x, par_x, near, far, taps, maps
    )
    all_mixed = along_chan(mixed)

    square = held(4, 192, 192)
    turn = call(
        turn_kernel,
        [square] * 4
        + [held(4, 192, 128, dtype=F32), held(4, 48, 128, dtype=F32), held(4, 48, 512)],
        n_in=4,
        name="turn",
        near=(0, 1, 2, 3),
    )
    turned = turn(*after(all_sends, mixed[0]))

    *tiles, keep, give = call(
        mlp_kernel,
        [held(96, 256)] * 8 + [held(4, 288, 128)] * 2,
        scratch=[pltpu.VMEM((4, 48, 512), BF16)] * 3 + [pltpu.VMEM((2, 4, 288, 128), BF16)],
        n_in=11,
        name="mlp",
        near=range(11),
    )(*all_mixed, *turned)
    all_back = along_chan(tiles[0:4])
    merged = call(merge_kernel, held(4, 288, 128), n_in=2, name="merge", near=range(2))(
        keep, partner(give)
    )
    partials = lax.all_to_all(merged, "chan", 0, 0, tiled=True)
    grads = call(land_kernel, held(8, 48, 256), n_in=4, name="land", near=range(4))(*all_back)
    par_grads = partner(grads)
    tap_sums = call(
        taps_kernel,
        held(64, 128, dtype=F32),
        scratch=[
            pltpu.VMEM((3, 22 * WIDE, 128), F32),
            pltpu.VMEM((256, 384), F32),
            pltpu.VMEM((64, 384), F32),
        ],
        n_in=3,
        name="tap_sums",
        near=(0, 2),
    )(grads, padded, fold)
    edges = call(edges_kernel, held(8, 48, 128), n_in=2, name="edges", near=(0, 1))(
        after(grads, tap_sums), par_grads
    )
    near_grads = next_chip(edges)
    pieces = call(
        pieces_kernel,
        held(32, 16, 128),
        scratch=[pltpu.VMEM((352, 128), F32), pltpu.VMEM((32, 16, 128), F32)],
        n_in=2,
        name="pieces",
        near=range(2),
    )(partials, tap_sums)
    arrived = lax.all_to_all(after(pieces, edges), "chip", 0, 0, tiled=True)

    factor = 1.0 / math.sqrt(adjacency.shape[0] * devices * PIX)
    far_grads = partner(near_grads)
    all_branch = along_chan(after(tiles[4:8], pieces))
    surrounded = call(
        surround_kernel,
        held(3, 22 * WIDE, 128, dtype=F32),
        scratch=grid_scratch(49)[0:4],
        smem=1,
        n_in=6,
        name="surround",
        near=(1, 2, 3, 4),
        micros=0.7,
    )(adjacency, grads, par_grads, near_grads, far_grads, maps)
    arrived, surrounded = lax.optimization_barrier((arrived, surrounded))
    totals = call(
        functools.partial(total_kernel, factor), held(32, 16, 128), n_in=1, name="totals", near=(0,)
    )(arrived)
    spread = lax.all_to_all(totals, "chip", 0, 0, tiled=True)

    output, grad_in = call(
        unmix_kernel,
        [shape(8, 48, 256), shape(8, 48, 256)],
        scratch=[pltpu.VMEM((256, 384), F32)],
        n_in=9,
        name="unmix",
        near=(0, 5, 6, 7, 8),
    )(surrounded, cotangent, taps, owned, after(scale_row, totals), *all_branch)
    spread = after(spread, output)
    grad_dw, grad_w1, grad_w2 = call(
        finish_kernel,
        [shape(48, 49, dtype=F32), shape(192, 192, dtype=F32), shape(192, 192, dtype=F32)],
        scratch=[pltpu.VMEM((32, 16, 128), F32), pltpu.VMEM((2, 352, 128), F32)],
        n_in=2,
        name="finish",
        near=(0, 1),
    )(spread, partner(spread))
    return (output, grad_in, grad_dw, grad_w1, grad_w2)


def solution(mesh):
    chips, chan = mesh.devices.shape[0] // 2, mesh.devices.shape[1]
    parts = Mesh(mesh.devices.reshape(chips, 2, chan), ("chip", "core", "chan"))
    tiles = ("chip", "core")
    in_specs = (
        P(tiles, "chan", None),
        P(tiles),
        P(tiles, None),
        P(tiles, "chan", None),
        P("chan", None),
        P("chan"),
        P(None, "chan"),
        P("chan"),
        P("chan", None),
        P("chan"),
    )
    out_specs = (
        P(tiles, "chan", None),
        P(tiles, "chan", None),
        P("chan", None),
        P(None, "chan"),
        P("chan", None),
    )
    return jax.shard_map(body, mesh=parts, in_specs=in_specs, out_specs=out_specs, check_vma=False)
```

```python
import functools
import math

import jax
import jax.numpy as jnp
import numpy as np
from jax import lax
from jax.experimental import pallas as pl
from jax.experimental.pallas import tpu as pltpu
from jax.sharding import Mesh
from jax.sharding import PartitionSpec as P

CHANNELS = 192
SIDE = 16
PIX = 256
WIDE = 24
EPSILON = 1e-06
GELU_SCALE = 0.7978845608
GELU_CUBIC = 0.044715

F32 = jnp.float32
BF16 = jnp.bfloat16
NT = (((1,), (1,)), ((), ()))
NN = (((1,), (0,)), ((), ()))


def dot(a, b, dims):
    return lax.dot_general(a, b, dims, preferred_element_type=F32)


def placement_tables():
    maps = np.zeros((22 * WIDE, 768), np.float32)
    up, mid, down = maps[0:72], maps[72:456], maps[456:528]
    for j in range(22):
        if j < 3:
            side, col = 0, 13 + j
        elif j < 19:
            side, col = 1, j - 3
        else:
            side, col = 2, j - 19
        for i in range(3):
            up[i * WIDE + j, 128 * side + 16 * (13 + i) + col - 128] = 1
            down[i * WIDE + j, 128 * side + 16 * i + col] = 1
        for i in range(16):
            block = (1, 0, 2)[side]
            mid[i * WIDE + j, 256 * block + 16 * i + col] = 1
    return maps.astype(jnp.bfloat16)


def column(row):
    n = row.shape[1]
    same = lax.broadcasted_iota(jnp.int32, (n, n), 0) == lax.broadcasted_iota(jnp.int32, (n, n), 1)
    return jnp.sum(jnp.where(same, jnp.broadcast_to(row, (n, n)), 0.0), axis=1, keepdims=True)


def eye(n):
    same = lax.broadcasted_iota(jnp.int32, (n, n), 0) == lax.broadcasted_iota(jnp.int32, (n, n), 1)
    return same.astype(F32).astype(BF16)


def swap_halves(value):
    return pltpu.roll(value.astype(F32), 64, 1)


def low_lanes(shape):
    return lax.broadcasted_iota(jnp.int32, shape, 1) < 64


def pack_pair(natural, other, natural_low):
    shape = natural.shape
    keep = low_lanes(shape) if natural_low else jnp.logical_not(low_lanes(shape))
    return jnp.where(keep, natural.astype(F32), swap_halves(other)).astype(BF16)


def my_owner():
    return 2 * lax.axis_index("chip") + lax.axis_index("core")


def pack_tail(value):
    return jnp.concatenate([value[0:96], value[96:192]], axis=1)


def unpack_tail(value):
    return jnp.concatenate([value[:, 0:64], value[:, 64:128]], axis=0)


def open_kernel(
    x_hbm, cot_hbm, scale_hbm, in_hbm, w_out_hbm, b_hbm, gain_hbm, dw_hbm, spread_hbm,
    strips_ref, s0, s1, s2, s3, taps_ref, spread, x_ref,
    cot_ref, scale_ref, in_ref, w_out_ref, b_ref, gain_ref, dw_ref, small, turned, sems,
):
    outs = (s0, s1, s2, s3)
    mine = lax.axis_index("chan")
    odd = lax.axis_index("core")
    sources = (x_hbm, cot_hbm, scale_hbm, in_hbm, w_out_hbm, b_hbm, gain_hbm, dw_hbm, spread_hbm)
    targets = (x_ref, cot_ref, scale_ref, in_ref, w_out_ref, b_ref, gain_ref, dw_ref, spread)
    copies = [
        pltpu.make_async_copy(source, target, sems.at[n])
        for n, (source, target) in enumerate(zip(sources, targets))
    ]
    for copy in copies:
        copy.start()
    copies[0].wait()

    @pl.when(odd == 1)
    def _():
        for s in range(8):
            strips_ref[s] = pack_pair(x_ref[s, :, 128:256], x_ref[s + 8, :, 128:256], False)

    @pl.when(odd == 0)
    def _():
        for s in range(8):
            strips_ref[s] = pack_pair(x_ref[s, :, 0:128], x_ref[s + 8, :, 0:128], True)

    for copy in copies[1:]:
        copy.wait()
    turned[...] = jnp.zeros((128, 128), F32)
    turned[0:48, 0:49] = dw_ref[...]
    taps_ref[...] = lax.dot_general(
        turned[...].T[0:56], spread[...], NN,
        precision=lax.Precision.HIGHEST, preferred_element_type=F32,
    )
    scale = column(scale_ref[...])
    small[...] = jnp.zeros((16, 256), F32)
    small[0:1, 0:192] = b_ref[...].astype(F32).reshape(1, 192)
    small[1:2, 0:48] = gain_ref[...].astype(F32)
    tails = []
    for ref in (in_ref, w_out_ref):
        tails.append(pack_tail(ref[:, 128:192].astype(F32)).astype(BF16))
    for j, out in enumerate(outs):
        first = 2 * ((mine + j) & 3)
        for i in range(2):
            out[48 * i : 48 * i + 48] = (cot_ref[first + i].astype(F32) * scale).astype(BF16)
        out[96:288, 0:128] = in_ref[:, 0:128]
        out[96:288, 128:256] = w_out_ref[:, 0:128]
        out[288:384, 0:128] = tails[0]
        out[288:384, 128:256] = tails[1]
        out[384:400] = small[...].astype(BF16)


def gather_tile(table, up_g, mid_g, down_g, t, center, entries):
    rows = pl.ds(48 * t, 48)
    mid_g[rows, 0:256] = table[center]
    mid_g[rows, 256:512] = table[entries[3]]
    mid_g[rows, 512:768] = table[entries[4]]
    for k in range(3):
        up_g[rows, 128 * k : 128 * k + 128] = table[entries[k], :, 128:256]
        down_g[rows, 128 * k : 128 * k + 128] = table[entries[5 + k], :, 0:128]


def build_padded(pad, up_g, mid_g, down_g, maps):
    for cells, lo, hi in ((up_g, 0, 72), (mid_g, 72, 456), (down_g, 456, 528)):
        rows = dot(maps[lo:hi, 0 : cells.shape[1]], cells[...], NT)
        for block in range(3):
            pad[block, lo:hi] = rows[:, 128 * block : 128 * block + 128]


def convolve(pad, taps, result, flip):
    def lane_block(block, carry):
        lanes = pl.ds(pl.multiple_of(block * 128, 128), 128)
        acc = [jnp.zeros((16, 128), F32) for _ in range(16)]
        for b in range(7):
            weights = []
            for a in range(7):
                tap = 7 * a + b
                weights.append(taps[pl.ds(48 - tap if flip else tap, 1), lanes])
            for r in range(22):
                line = pad[block, pl.ds(WIDE * r + b, 16)]
                for a in range(7):
                    i = r - a
                    if 0 <= i < 16:
                        acc[i] = acc[i] + line * weights[a]
        for i in range(16):
            result[pl.ds(16 * i, 16), lanes] = acc[i]
        return carry

    lax.fori_loop(0, 3, lane_block, 0)


def fill_edges(table, near_ref, far_ref, below):
    odd = lax.axis_index("core")

    def fill(upper, lower):
        for s in range(8):
            up = upper[s]
            table[s, :, 128:256] = up
            table[s + 8, :, 128:256] = swap_halves(up).astype(BF16)
            down = lower[s]
            table[below + s, :, 0:128] = down
            table[below + 8 + s, :, 0:128] = swap_halves(down).astype(BF16)

    @pl.when(odd == 0)
    def _():
        fill(near_ref, far_ref)

    @pl.when(odd == 1)
    def _():
        fill(far_ref, near_ref)


OFFSETS = (-17, -16, -15, -1, 1, 15, 16, 17)


def mix_kernel(
    own_slots, par_slots, adj, x_ref, par_ref, near_ref, far_ref, taps, maps,
    owned_ref, pad, m0, m1, m2, m3,
    place, table, up_g, mid_g, down_g, result, flat,
):
    me = my_owner()
    odd = lax.axis_index("core")
    mine = lax.axis_index("chan")
    base = 8 * me
    for t in range(8):
        place[t] = 0
    for s in range(16):
        for slots, row in ((own_slots, odd), (par_slots, 1 - odd)):
            t = slots[s] - base

            @pl.when((t >= 0) & (t < 8))
            def _():
                place[t] = 16 + 16 * row + s

    table[pl.ds(16 + 16 * odd, 16)] = x_ref[...]
    table[pl.ds(32 - 16 * odd, 16)] = par_ref[...]
    table[64] = jnp.zeros((48, 256), BF16)

    fill_edges(table, near_ref, far_ref, 48)
    for t in range(8):
        center = place[t]
        entries = [jnp.where(adj[t, k] < 512, center + OFFSETS[k], 64) for k in range(8)]
        gather_tile(table, up_g, mid_g, down_g, t, center, entries)
    owned_ref[...] = mid_g[:, 0:256].reshape(8, 48, 256)
    build_padded(pad, up_g, mid_g, down_g, maps)
    convolve(pad, taps, result, False)
    flat[...] = result[...].T.astype(BF16).reshape(8, 48, 256)
    for j, out in enumerate((m0, m1, m2, m3)):
        first = 2 * ((mine + j) & 3)
        out[0] = flat[first]
        out[1] = flat[first + 1]


def turn_kernel(p0, p1, p2, p3, w_in, w_out, in_t, out_t, bias, gain, dbranch):
    mine = lax.axis_index("chan")
    unit = eye(192)
    for j, ref in enumerate((p0, p1, p2, p3)):
        a = (mine + 4 - j) & 3
        for i in range(2):
            dbranch[a, :, 256 * i : 256 * i + 256] = ref[48 * i : 48 * i + 48]
        for full, turned, lanes in ((w_in, in_t, 0), (w_out, out_t, 128)):
            tail = ref[288:384, lanes : lanes + 128].astype(F32)
            whole = jnp.concatenate(
                [
                    ref[96:288, lanes : lanes + 128].astype(F32),
                    unpack_tail(tail),
                ],
                axis=1,
            ).astype(BF16)
            full[j] = whole
            turned[j] = dot(unit, whole, NT).astype(BF16)
        cols = dot(unit, ref[384:400, 0:192], NT)
        bias[j] = jnp.broadcast_to(cols[:, 0:1], (192, 128))
        gain[a] = jnp.broadcast_to(cols[0:48, 1:2], (48, 128))


def across(col_block):
    return jnp.concatenate([col_block] * 4, axis=1)


def mlp_kernel(
    m0, m1, m2, m3, w_in, w_out, in_t, out_t, bias, gain, db_ref,
    g0, g1, g2, g3, keep_ref, give_ref, mixed_s, back_s, branch_s, halves,
):
    mine = lax.axis_index("chan")
    for j, m_ref in enumerate((m0, m1, m2, m3)):
        a = (mine + 4 - j) & 3
        for i in range(2):
            mixed_s[a, :, 256 * i : 256 * i + 256] = m_ref[i]
    mixed = mixed_s[...].reshape(192, 512).astype(F32)
    dbranch = db_ref[...].reshape(192, 512)
    mean = jnp.sum(mixed, axis=0, keepdims=True) / CHANNELS
    inv = lax.rsqrt(
        jnp.sum(mixed * mixed, axis=0, keepdims=True) / CHANNELS - mean * mean + EPSILON
    )
    x_hat = (mixed - mean) * inv
    gain_full = across(gain[...].reshape(192, 128))
    normed = (x_hat * gain_full).astype(BF16)
    branch = jnp.zeros((192, 512), F32)
    dnormed = jnp.zeros((192, 512), F32)
    for j in range(4):
        preact = dot(in_t[j], normed, NN) + across(bias[j])
        square = preact * preact
        tangent = jnp.tanh(preact * (GELU_SCALE + (GELU_SCALE * GELU_CUBIC) * square))
        half = 0.5 + 0.5 * tangent
        value = preact * half
        act = value.astype(BF16)
        slope = half + value * (1.0 - tangent) * (
            GELU_SCALE + (3.0 * GELU_SCALE * GELU_CUBIC) * square
        )
        branch = branch + dot(out_t[j], act, NN)
        pre_grad = (dot(w_out[j], dbranch, NN) * slope).astype(BF16)
        dnormed = dnormed + dot(w_in[j], pre_grad, NN)
        for side, grad in enumerate((dot(normed, pre_grad, NT), dot(act, dbranch, NT))):
            halves[side, j, 0:192] = grad[:, 0:128].astype(BF16)
            halves[side, j, 192:288] = pack_tail(grad[:, 128:192]).astype(BF16)
    core = lax.axis_index("core")
    keep_ref[...] = halves[core]
    give_ref[...] = halves[1 - core]
    xhat_grad = dnormed * gain_full
    first = jnp.sum(xhat_grad, axis=0, keepdims=True) / CHANNELS
    second = jnp.sum(xhat_grad * x_hat, axis=0, keepdims=True) / CHANNELS
    dmixed = (inv * (xhat_grad - first - x_hat * second)).astype(BF16)
    back_s[...] = dmixed.reshape(4, 48, 512)
    branch_s[...] = branch.astype(BF16).reshape(4, 48, 512)
    for j, g_ref in enumerate((g0, g1, g2, g3)):
        a = (mine + j) & 3
        for i in range(2):
            g_ref[48 * i : 48 * i + 48] = back_s[a, :, 256 * i : 256 * i + 256]
            g_ref[96 + 48 * i : 144 + 48 * i] = branch_s[a, :, 256 * i : 256 * i + 256]


def land_kernel(g0, g1, g2, g3, grad_ref):
    mine = lax.axis_index("chan")
    for j, ref in enumerate((g0, g1, g2, g3)):
        first = 2 * ((mine + 4 - j) & 3)
        for i in range(2):
            grad_ref[first + i] = ref[48 * i : 48 * i + 48]


def merge_kernel(keep_ref, got_ref, out_ref):
    mine = lax.axis_index("chan")
    for j in range(4):
        both = keep_ref[j].astype(F32) + got_ref[j].astype(F32)
        out_ref[(mine + 4 - j) & 3] = both.astype(BF16)


def taps_kernel(grad_ref, pad, fold, out_ref, grad_t, sums):
    grad_t[...] = grad_ref[...].reshape(384, 256).astype(F32).T
    sums[...] = jnp.zeros((64, 384), F32)

    def lane_block(block, carry):
        lanes = pl.ds(pl.multiple_of(block * 128, 128), 128)
        lines = [grad_t[pl.ds(16 * i, 16), lanes] for i in range(16)]
        for b in range(7):
            acc = [jnp.zeros((16, 128), F32) for _ in range(7)]
            for r in range(22):
                line = pad[block, pl.ds(WIDE * r + b, 16)]
                for a in range(7):
                    i = r - a
                    if 0 <= i < 16:
                        acc[a] = acc[a] + line * lines[i]
            for a in range(7):
                sums[pl.ds(7 * a + b, 1), lanes] = jnp.sum(acc[a], axis=0, keepdims=True)
        return carry

    lax.fori_loop(0, 3, lane_block, 0)
    out_ref[...] = lax.dot_general(
        sums[...], fold[...], NT, precision=lax.Precision.HIGHEST, preferred_element_type=F32
    )


def pieces_kernel(parts_ref, taps_ref, out_ref, total, rows):
    total[0:288] = jnp.sum(parts_ref[...].astype(F32), axis=0)
    total[288:352] = taps_ref[...]
    rows[...] = jnp.zeros((32, 16, 128), F32)
    for q in range(11):
        rows[:, q, :] = total[32 * q : 32 * q + 32]
    out_ref[...] = rows[...].astype(BF16)


def edges_kernel(own_ref, par_ref, edge_ref):
    odd = lax.axis_index("core")

    @pl.when(odd == 1)
    def _():
        for t in range(8):
            edge_ref[t] = pack_pair(par_ref[t, :, 128:256], own_ref[t, :, 128:256], False)

    @pl.when(odd == 0)
    def _():
        for t in range(8):
            edge_ref[t] = pack_pair(own_ref[t, :, 0:128], par_ref[t, :, 0:128], True)


def total_kernel(factor, in_ref, out_ref):
    total = jnp.sum(in_ref[...].astype(F32), axis=0, keepdims=True) * factor
    out_ref[...] = jnp.broadcast_to(total, in_ref.shape).astype(out_ref.dtype)


def finish_kernel(in_ref, other_ref, dw_ref, w1_ref, w2_ref, rows, flat):
    core = lax.axis_index("core")
    for ref, side in ((in_ref, core), (other_ref, 1 - core)):
        rows[...] = ref[...].astype(F32)
        for q in range(11):
            flat[side, 32 * q : 32 * q + 32] = rows[:, q, :]
    for out, side in ((w1_ref, 0), (w2_ref, 1)):
        out[:, 0:128] = flat[side, 0:192]
        out[:, 128:192] = unpack_tail(flat[side, 192:288])
    dw = flat[0, 288:352] + flat[1, 288:352]
    dw_ref[...] = dw.T[0:48, 0:49]


def surround_kernel(
    adj, grad_ref, par_ref, near_ref, far_ref, maps, pad, table, up_g, mid_g, down_g
):
    me = my_owner()
    odd = lax.axis_index("core")
    start = 16 * (me // 2) - 16
    table[pl.ds(16 + 8 * odd, 8)] = grad_ref[...]
    table[pl.ds(24 - 8 * odd, 8)] = par_ref[...]
    table[48] = jnp.zeros((48, 256), BF16)
    fill_edges(table, near_ref, far_ref, 32)
    for t in range(8):
        center = 16 + 8 * odd + t
        entries = [jnp.where(adj[t, k] < 512, adj[t, k] - start, 48) for k in range(8)]
        gather_tile(table, up_g, mid_g, down_g, t, center, entries)
    build_padded(pad, up_g, mid_g, down_g, maps)


def unmix_kernel(
    pad, cot_ref, taps, owned_ref, scale_ref, r0, r1, r2, r3, out_ref, gin_ref, result
):
    mine = lax.axis_index("chan")
    convolve(pad, taps, result, True)
    back = result[...].T.reshape(8, 48, 256)
    gin_ref[...] = (cot_ref[...].astype(F32) + back).astype(BF16)
    scale = column(scale_ref[...])
    for j, ref in enumerate((r0, r1, r2, r3)):
        first = 2 * ((mine + 4 - j) & 3)
        for i in range(2):
            out_ref[first + i] = (
                owned_ref[first + i].astype(F32)
                + scale * ref[96 + 48 * i : 144 + 48 * i].astype(F32)
            ).astype(BF16)


def call(kernel, shapes, scratch=(), smem=0, n_in=0, name=None, near=(), micros=None):
    vmem = pl.BlockSpec(memory_space=pltpu.VMEM)
    scalar = pl.BlockSpec(memory_space=pltpu.SMEM)
    many = isinstance(shapes, (list, tuple))

    inner = pl.pallas_call(
        kernel,
        out_shape=shapes,
        in_specs=[scalar] * smem + [vmem] * (n_in - smem),
        out_specs=[vmem] * len(shapes) if many else vmem,
        scratch_shapes=list(scratch),
        compiler_params=pltpu.CompilerParams(vmem_limit_bytes=24 << 20),
        cost_estimate=None if micros is None else pl.CostEstimate(
            flops=int(micros * 1e9), transcendentals=0, bytes_accessed=int(micros * 3.69e6)
        ),
        name=name,
    )

    def run(*args):
        return inner(
            *(
                pltpu.with_memory_space_constraint(a, pltpu.VMEM) if i in near else a
                for i, a in enumerate(args)
            )
        )

    return run


def shape(*dims, dtype=BF16):
    return jax.ShapeDtypeStruct(dims, dtype)


def held(*dims, dtype=BF16):
    return pltpu.VMEM(dims, dtype)


def along_chan(values):
    got = [values[0]]
    for j in range(1, 4):
        got.append(lax.ppermute(values[j], "chan", [(i, (i + j) % 4) for i in range(4)]))
    return got


def body(
    x_scan, slot_owner, adjacency, cotangent, dw_weight, ln_gain, w_in, b_in, w_out, layer_scale
):
    devices = lax.axis_size("chip") * 2
    maps = jnp.asarray(placement_tables())
    fold_map = (np.arange(384)[:, None] % 48 == np.arange(128)[None, :]).astype(np.float32)
    spread_map = jnp.asarray(np.ascontiguousarray(fold_map.T))
    scale_row = layer_scale.reshape(1, 48)
    owners = ("chip", "core")

    def after(value, *first):
        return lax.optimization_barrier((value, first))[0]

    def partner(value):
        return lax.ppermute(value, "core", [(0, 1), (1, 0)])

    def next_chip(value):
        pairs = [(i, i + 1 if i & 1 else i - 1) for i in range(devices)]
        return lax.ppermute(value, owners, [p for p in pairs if 0 <= p[1] < devices])

    tile_chunk = held(2, 48, 256)
    par_x = partner(x_scan)
    par_slots = partner(slot_owner)
    opening = (
        x_scan, cotangent, scale_row, w_in, w_out, b_in, ln_gain.reshape(1, 48), dw_weight, spread_map
    )
    strips, *sends, taps, fold, own_x = pl.pallas_call(
        open_kernel,
        out_shape=[held(8, 48, 128)] + [held(400, 256)] * 4
        + [held(56, 384, dtype=F32), held(128, 384, dtype=F32), held(16, 48, 256)],
        in_specs=[pl.BlockSpec(memory_space=pltpu.HBM)] * 9,
        out_specs=[pl.BlockSpec(memory_space=pltpu.VMEM)] * 8,
        scratch_shapes=[pltpu.VMEM(v.shape, v.dtype) for v in opening[1:-1]]
        + [
            pltpu.VMEM((16, 256), F32),
            pltpu.VMEM((128, 128), F32),
            pltpu.SemaphoreType.DMA((9,)),
        ],
        compiler_params=pltpu.CompilerParams(vmem_limit_bytes=24 << 20),
        name="open",
    )(*(pltpu.with_memory_space_constraint(v, pltpu.HBM) for v in opening))
    near = next_chip(strips)
    far = partner(near)
    sends[1] = after(sends[1], near, par_slots)
    all_sends = along_chan(sends)

    grid_scratch = lambda entries: [
        pltpu.VMEM((entries, 48, 256), BF16),
        pltpu.VMEM((384, 384), BF16),
        pltpu.VMEM((384, 768), BF16),
        pltpu.VMEM((384, 384), BF16),
    ]
    mix = call(
        mix_kernel,
        [held(8, 48, 256), held(3, 22 * WIDE, 128, dtype=F32)] + [tile_chunk] * 4,
        scratch=[pltpu.SMEM((8,), jnp.int32)]
        + grid_scratch(65)
        + [pltpu.VMEM((256, 384), F32), pltpu.VMEM((8, 48, 256), BF16)],
        smem=3,
        n_in=9,
        name="mix",
        near=(3, 4, 5, 6, 7),
    )
    owned, padded, *mixed = mix(
        slot_owner, par_slots, adjacency, own_x, par_x, near, far, taps, maps
    )
    all_mixed = along_chan(mixed)

    square = held(4, 192, 192)
    turn = call(
        turn_kernel,
        [square] * 4
        + [held(4, 192, 128, dtype=F32), held(4, 48, 128, dtype=F32), held(4, 48, 512)],
        n_in=4,
        name="turn",
        near=(0, 1, 2, 3),
    )
    turned = turn(*after(all_sends, mixed[0]))

    *packets, keep, give = call(
        mlp_kernel,
        [held(192, 256)] * 4 + [held(4, 288, 128)] * 2,
        scratch=[pltpu.VMEM((4, 48, 512), BF16)] * 3 + [pltpu.VMEM((2, 4, 288, 128), BF16)],
        n_in=11,
        name="mlp",
        near=range(11),
    )(*all_mixed, *turned)
    all_back = along_chan(packets)
    merged = call(merge_kernel, held(4, 288, 128), n_in=2, name="merge", near=range(2))(
        keep, partner(give)
    )
    partials = lax.all_to_all(merged, "chan", 0, 0, tiled=True)
    grads = call(land_kernel, held(8, 48, 256), n_in=4, name="land", near=range(4))(*all_back)
    par_grads = partner(grads)
    tap_sums = call(
        taps_kernel,
        held(64, 128, dtype=F32),
        scratch=[pltpu.VMEM((256, 384), F32), pltpu.VMEM((64, 384), F32)],
        n_in=3,
        name="tap_sums",
        near=(0, 1, 2),
    )(grads, padded, fold)
    edges = call(edges_kernel, held(8, 48, 128), n_in=2, name="edges", near=(0, 1))(
        after(grads, tap_sums), par_grads
    )
    near_grads = next_chip(edges)
    pieces = call(
        pieces_kernel,
        held(32, 16, 128),
        scratch=[pltpu.VMEM((352, 128), F32), pltpu.VMEM((32, 16, 128), F32)],
        n_in=2,
        name="pieces",
        near=range(2),
    )(partials, tap_sums)
    arrived = lax.all_to_all(after(pieces, edges), "chip", 0, 0, tiled=True)

    factor = 1.0 / math.sqrt(adjacency.shape[0] * devices * PIX)
    far_grads = partner(near_grads)
    surrounded = call(
        surround_kernel,
        held(3, 22 * WIDE, 128, dtype=F32),
        scratch=grid_scratch(49),
        smem=1,
        n_in=6,
        name="surround",
        near=(1, 2, 3, 4),
        micros=0.7,
    )(adjacency, grads, par_grads, near_grads, far_grads, maps)
    arrived, surrounded = lax.optimization_barrier((arrived, surrounded))
    totals = call(
        functools.partial(total_kernel, factor), held(32, 16, 128), n_in=1, name="totals", near=(0,)
    )(arrived)
    spread = lax.all_to_all(totals, "chip", 0, 0, tiled=True)

    output, grad_in = call(
        unmix_kernel,
        [shape(8, 48, 256), shape(8, 48, 256)],
        scratch=[pltpu.VMEM((256, 384), F32)],
        n_in=9,
        name="unmix",
        near=(0, 5, 6, 7, 8),
    )(surrounded, cotangent, taps, owned, after(scale_row, totals), *all_back)
    spread = after(spread, output)
    grad_dw, grad_w1, grad_w2 = call(
        finish_kernel,
        [shape(48, 49, dtype=F32), shape(192, 192, dtype=F32), shape(192, 192, dtype=F32)],
        scratch=[pltpu.VMEM((32, 16, 128), F32), pltpu.VMEM((2, 352, 128), F32)],
        n_in=2,
        name="finish",
        near=(0, 1),
    )(spread, partner(spread))
    return (output, grad_in, grad_dw, grad_w1, grad_w2)


def solution(mesh):
    chips, chan = mesh.devices.shape[0] // 2, mesh.devices.shape[1]
    parts = Mesh(mesh.devices.reshape(chips, 2, chan), ("chip", "core", "chan"))
    tiles = ("chip", "core")
    in_specs = (
        P(tiles, "chan", None),
        P(tiles),
        P(tiles, None),
        P(tiles, "chan", None),
        P("chan", None),
        P("chan"),
        P(None, "chan"),
        P("chan"),
        P("chan", None),
        P("chan"),
    )
    out_specs = (
        P(tiles, "chan", None),
        P(tiles, "chan", None),
        P("chan", None),
        P(None, "chan"),
        P("chan", None),
    )
    return jax.shard_map(body, mesh=parts, in_specs=in_specs, out_specs=out_specs, check_vma=False)
```
